32 devices in a mesh: grp: 2 (over y), section: 2 (over core), seq: 4 (over z), fsdp: 2 (over x).
Axes of the slice: x: 2, y: 2, z: 4, core: 2. Of those that a mesh axis runs over, the one named last changes fastest.
Arguments:
- head_inputs: bfloat16 [2, 4, 256, 7680], P('section', ('grp', 'fsdp'), 'seq'), parts along dimension 1, may hold values from -8 to 8
- hidden: bfloat16 [2, 4, 256, 2560], P('section', ('grp', 'fsdp'), 'seq'), parts along dimension 1, may hold values from -3 to 3
- out_weight: bfloat16 [2, 2560, 2560], P('section', 'fsdp'), may hold values from -0.125 to 0.125
- time_weight: bfloat16 [2, 256, 7680], P('section', None, ('seq', 'fsdp')), may hold values from -0.375 to 0.375
- head_weight: bfloat16 [2, 2560, 64], P('section', ('seq', 'fsdp')), may hold values from -0.125 to 0.125
- latent: float32 [2, 4, 128, 128], P('section', ('grp', 'fsdp'), 'seq'), parts along dimension 1, may hold values from -6 to 6
- timesteps: int32 [2, 4, 2], P('section', ('grp', 'fsdp')), parts along dimension 1, may hold values from 41 to 999, as said below
Outputs:
- velocity: float32 [2, 4, 128, 128], P('section', ('grp', 'fsdp'), 'seq'), parts along dimension 1
- carried: float32 [2, 4, 128, 128], P('section', ('grp', 'fsdp'), 'seq'), parts along dimension 1
The draws below stay inside these ranges and needn't reach their ends.
There are 2 independent parts, one for each index of `grp`. The reference program is written for one: setup_inputs(seed, part) draws one part's arguments, and reference() takes and returns one part's arrays. A program takes and returns all parts, laid end to end along the dimension named above; an argument that names none is the same for every part. Nothing has to cross between parts.
Inputs may be any that keep to these rules, and one draw needn't show every extreme that they name: timesteps[0] lie in 875 to 999 and timesteps[1] in 100 to 874 for the current entry; the next entry is the current one minus 10 to 59.
All inputs are finite; a program needn't handle non-finite values.
Results may differ from the reference program's by a relative error of at most 0.0049.
Values may be sent and summed in bfloat16 or wider, within the bound.
No kernel may reach another device: no remote copies, remote signals or barrier semaphores. Data moves between devices by JAX's collectives and lax.ppermute only.
A program may use at most 128 MiB of HBM per device.

```python
import math
import jax
import jax.numpy as jnp
from jax import lax

DIM = 2560
HEADS = 32
HEAD = 80
PATCH = 64
FREQ = 256
BATCH = 2
SEQLEN = 256


def draw_head_inputs(key, part):
    key_base = jax.random.fold_in(key, 11)
    shape = (2, BATCH, SEQLEN, HEADS, 3, HEAD)
    spreads = jnp.array([1.5, 1.5, 1.0], jnp.float32)[:, None]
    base = jnp.clip(jax.random.normal(key_base, shape, jnp.float32) * spreads, -8.0, 8.0)
    return base.reshape(2, BATCH, SEQLEN, HEADS * 3 * HEAD).astype(jnp.bfloat16)


def draw_timesteps(key, part):
    key_high = jax.random.fold_in(key, 21)
    key_low = jax.random.fold_in(key, 22)
    key_gap = jax.random.fold_in(key, 23)
    high_steps = jax.random.randint(key_high, (BATCH,), 875, 1000)
    low_steps = jax.random.randint(key_low, (BATCH,), 100, 875)
    current = jnp.stack([high_steps, low_steps]).astype(jnp.int32)
    gaps = jax.random.randint(key_gap, (2, BATCH), 10, 60).astype(jnp.int32)
    return jnp.stack([current, current - gaps], axis=-1).astype(jnp.int32)


def block_scale(rng, extent, split, smallest, top_value):
    level = 1.0
    for dim, shards_of in split:
        draws = jax.random.uniform(jax.random.fold_in(jax.random.fold_in(rng, 6), dim), (shards_of,), jnp.float32, smallest / len(split), top_value / len(split))
        level = level * jnp.repeat(jnp.exp(draws), extent[dim] // shards_of).reshape((-1,) + (1,) * (len(extent) - 1 - dim))
    return level


def bell_draw(rng, extent, deviation, most, cuts=(), held_as=jnp.bfloat16):
    loudness = block_scale(rng, extent, cuts, -0.22, 0.18) if cuts else 1.0
    result = jax.random.normal(rng, extent, jnp.float32) * deviation * loudness
    return jnp.minimum(jnp.maximum(result, -most), most).astype(held_as)


def setup_inputs(seed: int = 0, part: int = 0) -> dict:
    splits = jax.random.split(jax.random.key(seed), 8)
    part_keys = jax.random.split(jax.random.fold_in(splits[7], part), 8)
    return {
        "head_inputs": draw_head_inputs(jax.random.fold_in(jax.random.fold_in(splits[7], part), 71), part),
        "hidden": bell_draw(part_keys[1], (2, BATCH, SEQLEN, DIM), 0.5, 3.0, ((0, 2), (1, 2), (2, 4))),
        "out_weight": bell_draw(splits[2], (2, HEADS * HEAD, DIM), (HEADS * HEAD) ** -0.5, 0.125, ((0, 2), (1, 2))),
        "time_weight": bell_draw(splits[3], (2, FREQ, 3 * DIM), FREQ ** -0.5, 0.375, ((0, 2), (2, 8))),
        "head_weight": bell_draw(splits[4], (2, DIM, PATCH), DIM ** -0.5, 0.125, ((0, 2), (1, 8))),
        "latent": bell_draw(part_keys[5], (2, BATCH, SEQLEN // 2, 2 * PATCH), 1.0, 6.0, ((0, 2), (1, 2), (2, 4)), jnp.float32),
        "timesteps": draw_timesteps(jax.random.fold_in(jax.random.fold_in(splits[7], part), 71), part),
    }


def time_embed(steps_now):
    half = FREQ // 2
    freqs = jnp.exp(-math.log(10000.0) * jnp.arange(half, dtype=jnp.float32) / half)
    angle = steps_now.astype(jnp.float32)[..., None] * freqs
    return jnp.concatenate([jnp.cos(angle), jnp.sin(angle)], axis=-1)

def sigma_of(steps_now):
    unit_time = steps_now.astype(jnp.float32) / 1000.0
    return 5.0 * unit_time / (1.0 + 4.0 * unit_time)

def head_attention(group):
    query_rows = group[0]
    key_rows = group[1]
    value_rows = group[2]
    scores = jnp.dot(query_rows, key_rows.T, preferred_element_type=jnp.float32) * HEAD ** (-0.5)
    row_max = lax.optimization_barrier(jnp.max(scores, axis=-1, keepdims=True))
    exp_scores = jnp.exp(scores - row_max)
    row_sum = lax.optimization_barrier(jnp.sum(exp_scores, axis=-1, keepdims=True))
    weights = (exp_scores / row_sum).astype(jnp.bfloat16)
    return jnp.dot(weights, value_rows, preferred_element_type=jnp.float32).astype(jnp.bfloat16)

def reference(head_inputs, hidden, out_weight, time_weight, head_weight, latent, timesteps):

    def per_section(section_in):
        section_heads, section_hidden, section_out, section_time, section_head, section_latent, section_steps = section_in

        def per_sample(sample_in):
            item_heads, item_hidden, item_latent, item_steps = sample_in
            grouped = item_heads.reshape(SEQLEN, HEADS, 3, HEAD).transpose(1, 2, 0, 3)
            per_head = lax.map(head_attention, grouped)
            attended = per_head.transpose(1, 0, 2).reshape(SEQLEN, HEADS * HEAD)
            embedding = time_embed(item_steps[0]).astype(jnp.bfloat16)
            modulation = jnp.dot(embedding[None, :], section_time, preferred_element_type=jnp.float32)[0]
            gate_term = modulation[:DIM]
            shift_term = modulation[DIM:2 * DIM]
            scale_term = modulation[2 * DIM:]
            projected = jnp.dot(attended, section_out, preferred_element_type=jnp.float32)
            updated = item_hidden.astype(jnp.float32) + gate_term * projected
            average = lax.optimization_barrier(jnp.mean(updated, axis=-1, keepdims=True))
            centred = updated - average
            variance = lax.optimization_barrier(jnp.mean(centred * centred, axis=-1, keepdims=True))
            normed = (centred * lax.rsqrt(variance + 1e-06) * (1.0 + scale_term) + shift_term).astype(jnp.bfloat16)
            velocity = jnp.dot(normed, section_head, preferred_element_type=jnp.float32)
            velocity = velocity.reshape(SEQLEN // 2, 2 * PATCH)
            step_size = sigma_of(item_steps[1]) - sigma_of(item_steps[0])
            stepped = item_latent + step_size * velocity
            return (velocity, stepped)
        return lax.map(per_sample, (section_heads, section_hidden, section_latent, section_steps))
    velocity, stepped = lax.map(per_section, (head_inputs, hidden, out_weight, time_weight, head_weight, latent, timesteps))
    carried = jnp.stack([stepped[1], stepped[0]])
    return (velocity, carried)
```

```python
import functools
import math

import jax
import jax.numpy as jnp
from jax import lax
from jax.experimental import pallas as pl
from jax.experimental.pallas import tpu as pltpu
from jax.sharding import PartitionSpec as P

DIM = 2560
HEADS = 32
HEAD = 80
PATCH = 64
FREQ = 256
LANES = 128


def partner(block, axis, apart):
    count = lax.axis_size(axis)
    route = []
    for low in range(count):
        high = low | 1 << apart
        if high != low and high < count:
            route += [(low, high), (high, low)]
    return lax.ppermute(block, axis, route)


def time_embed(steps_now):
    half = FREQ // 2
    freqs = jnp.exp(-math.log(10000.0) * jnp.arange(half, dtype=jnp.float32) / half)
    angle = steps_now.astype(jnp.float32)[..., None] * freqs
    return jnp.concatenate([jnp.cos(angle), jnp.sin(angle)], axis=-1)


def sigma_of(steps_now):
    unit_time = steps_now.astype(jnp.float32) / 1000.0
    return 5.0 * unit_time / (1.0 + 4.0 * unit_time)


def attend(exchanged):
    items = exchanged.shape[0]
    length = exchanged.shape[1]
    local_heads = exchanged.shape[2]
    query_all = exchanged[..., :HEAD]
    key_rows = exchanged[..., HEAD : 2 * HEAD]
    value_rows = exchanged[..., 2 * HEAD :]
    block_rows = min(512, length)
    block_count = length // block_rows

    def one_block(block_index):
        query_block = lax.dynamic_slice_in_dim(query_all, block_index * block_rows, block_rows, 1)
        scores = jnp.einsum(
            "nqhe,nkhe->nhqk", query_block, key_rows, preferred_element_type=jnp.float32
        ) * HEAD ** (-0.5)
        row_max = jnp.max(scores, axis=-1, keepdims=True)
        exp_scores = jnp.exp(scores - row_max)
        row_sum = jnp.sum(exp_scores, axis=-1, keepdims=True)
        weights = (exp_scores / row_sum).astype(jnp.bfloat16)
        return jnp.einsum(
            "nhqk,nkhe->nqhe", weights, value_rows, preferred_element_type=jnp.float32
        ).astype(jnp.bfloat16)

    blocks = lax.map(one_block, jnp.arange(block_count, dtype=jnp.int32))
    return blocks.transpose(1, 0, 2, 3, 4).reshape(items, length, local_heads * HEAD)


def general_body(head_inputs, hidden, out_weight, time_weight, head_weight, latent, timesteps):
    samples = head_inputs.shape[1]
    row_count = head_inputs.shape[2]
    flat_count = samples * row_count
    local = head_inputs.reshape(samples, row_count, HEADS, 3 * HEAD)
    attended = lax.all_to_all(
        attend(lax.all_to_all(local, "seq", split_axis=2, concat_axis=1, tiled=True)),
        "seq",
        split_axis=1,
        concat_axis=2,
        tiled=True,
    )
    flattened = attended.reshape(flat_count, HEADS * HEAD)
    time_full, head_full = (
        lax.all_gather(time_weight, ("seq", "fsdp"), axis=2, tiled=True),
        lax.all_gather(head_weight, ("seq", "fsdp"), axis=1, tiled=True),
    )
    embedding = time_embed(timesteps[0, :, 0]).astype(jnp.bfloat16)
    modulation = jnp.dot(embedding, time_full[0], preferred_element_type=jnp.float32)
    gate_term = modulation[:, None, :DIM]
    shift_term = modulation[:, None, DIM : 2 * DIM]
    scale_term = modulation[:, None, 2 * DIM :]
    own_columns = lax.all_to_all(flattened, "fsdp", split_axis=1, concat_axis=0, tiled=True)
    projected = lax.psum_scatter(
        jnp.dot(own_columns, out_weight[0], preferred_element_type=jnp.float32).astype(
            jnp.bfloat16
        ),
        "fsdp",
        scatter_dimension=0,
        tiled=True,
    ).astype(jnp.float32)
    updated = hidden.reshape(samples, row_count, DIM).astype(
        jnp.float32
    ) + gate_term * projected.reshape(samples, row_count, DIM)
    average = jnp.mean(updated, axis=-1, keepdims=True)
    centred = updated - average
    variance = jnp.mean(centred * centred, axis=-1, keepdims=True)
    normed = (centred * lax.rsqrt(variance + 1e-06) * (1.0 + scale_term) + shift_term).astype(
        jnp.bfloat16
    )
    velocity = jnp.dot(
        normed.reshape(flat_count, DIM), head_full[0], preferred_element_type=jnp.float32
    )
    velocity = velocity.reshape(1, samples, row_count // 2, 2 * PATCH)
    step_size = sigma_of(timesteps[0, :, 1]) - sigma_of(timesteps[0, :, 0])
    stepped = latent + step_size[None, :, None, None] * velocity
    carried = partner(stepped, "section", 0)
    return (velocity, carried)


def turn(half):
    return pltpu.roll(half.astype(jnp.float32), LANES // 2, 1)


def pack_half(tile):
    rows = tile.shape[0]
    wide = tile.astype(jnp.float32)
    lane = lax.broadcasted_iota(jnp.int32, (rows // 2, LANES), 1)
    return jnp.where(
        lane < LANES // 2, wide[: rows // 2], pltpu.roll(wide[rows // 2 :], LANES // 2, 1)
    ).astype(jnp.bfloat16)


def unpack_tiles(ref, rows, width):
    whole = width // LANES
    tiles = [ref[t * rows : (t + 1) * rows, :] for t in range(whole)]
    last = ref[whole * rows : whole * rows + rows // 2, :]
    tiles.append(jnp.concatenate([last, turn(last).astype(jnp.bfloat16)], axis=0))
    return tiles


def split_kernel(width, place_ref, x_ref, *outs):
    rows = x_ref.shape[0]
    whole = width // LANES
    count = len(outs)
    me = place_ref[0]
    for r in range(count):
        to = lax.rem(me + r, count)
        start = pl.multiple_of(lax.div(to * width, LANES) * LANES, LANES)
        odd = lax.rem(to, 2) == 1

        @pl.when(jnp.logical_not(odd))
        def _():
            for t in range(whole):
                outs[r][t * rows : (t + 1) * rows, :] = x_ref[:, pl.ds(start + t * LANES, LANES)]
            outs[r][whole * rows :, :] = pack_half(x_ref[:, pl.ds(start + whole * LANES, LANES)])

        @pl.when(odd)
        def _():
            lane = lax.broadcasted_iota(jnp.int32, (rows, LANES), 1)
            turned = [
                turn(x_ref[:, pl.ds(start + t * LANES, LANES)]) for t in range(whole + 1)
            ]
            for t in range(whole):
                outs[r][t * rows : (t + 1) * rows, :] = jnp.where(
                    lane < LANES // 2, turned[t], turned[t + 1]
                ).astype(jnp.bfloat16)
            outs[r][whole * rows :, :] = pack_half(turned[whole])


def split_heads(x, half, place, count, halves):
    rows, columns = x.shape
    width = columns // halves // count
    piece = jax.ShapeDtypeStruct((rows * width // LANES, LANES), jnp.bfloat16)
    return pl.pallas_call(
        functools.partial(split_kernel, width),
        grid_spec=pltpu.PrefetchScalarGridSpec(
            num_scalar_prefetch=1,
            grid=(1,),
            in_specs=[pl.BlockSpec((rows, columns // halves), lambda i, p: (0, p[1]))],
            out_specs=[pl.BlockSpec(piece.shape, lambda i, p: (0, 0))] * count,
        ),
        out_shape=[piece] * count,
        compiler_params=pltpu.CompilerParams(vmem_limit_bytes=8 << 20),
        cost_estimate=pl.CostEstimate(
            flops=0, transcendentals=0, bytes_accessed=4 * rows * columns // halves
        ),
        name="split_heads",
    )(jnp.stack([place, half]).astype(jnp.int32), x)


def attend_kernel(heads, rows, *refs):
    count = len(refs) // 2
    ins, outs = refs[:count], refs[count:]
    width = heads * 3 * HEAD
    blocks = [unpack_tiles(ref, rows, width) for ref in ins]

    def columns(start):
        first, offset = divmod(start, LANES)
        parts = []
        for tiles in blocks:
            if offset + HEAD <= LANES:
                parts.append(tiles[first][:, offset : offset + HEAD])
            else:
                wide = jnp.concatenate([tiles[first], tiles[first + 1]], axis=1)
                parts.append(wide[:, offset : offset + HEAD])
        return jnp.concatenate(parts, axis=0)

    results = []
    for h in range(heads):
        start = h * 3 * HEAD
        query, key, value = (columns(start + i * HEAD) for i in range(3))
        scores = lax.dot_general(
            query, key, (((1,), (1,)), ((), ())), preferred_element_type=jnp.float32
        ) * HEAD ** (-0.5)
        row_max = jnp.max(scores, axis=-1, keepdims=True)
        exp_scores = jnp.exp(scores - row_max)
        row_sum = jnp.sum(exp_scores, axis=-1, keepdims=True)
        weights = (exp_scores / row_sum).astype(jnp.bfloat16)
        results.append(jnp.dot(weights, value, preferred_element_type=jnp.float32))
    attended = jnp.concatenate(results, axis=1).astype(jnp.bfloat16)
    whole = heads * HEAD // LANES
    for b in range(count):
        mine = attended[b * rows : (b + 1) * rows]
        for t in range(whole):
            outs[b][t * rows : (t + 1) * rows, :] = mine[:, t * LANES : (t + 1) * LANES]
        rest = mine[:, whole * LANES :].astype(jnp.float32)
        outs[b][whole * rows :, :] = jnp.concatenate(
            [rest[: rows // 2], rest[rows // 2 :]], axis=1
        ).astype(jnp.bfloat16)


def attend_packed(pieces, heads, rows):
    count = len(pieces)
    total = count * rows
    out = jax.ShapeDtypeStruct((rows * heads * HEAD // LANES, LANES), jnp.bfloat16)
    return pl.pallas_call(
        functools.partial(attend_kernel, heads, rows),
        out_shape=[out] * count,
        compiler_params=pltpu.CompilerParams(vmem_limit_bytes=24 << 20),
        cost_estimate=pl.CostEstimate(
            flops=4 * heads * total * total * HEAD,
            transcendentals=heads * total * total,
            bytes_accessed=8 * total * heads * HEAD,
        ),
        name="attend_packed",
    )(*pieces)


def product(place_ref, w_ref, refs, rows):
    count = len(refs)
    depth = w_ref.shape[0] // count
    total = None
    for r in range(count):
        owner = lax.rem(place_ref[0] + r, count)
        left = jnp.concatenate(unpack_tiles(refs[r], rows, depth), axis=1)[:, :depth]
        right = w_ref[pl.ds(pl.multiple_of(owner * depth, depth), depth), :]
        term = jnp.dot(left, right, preferred_element_type=jnp.float32)
        total = term if total is None else total + term
    return total


def project_kernel(rows, place_ref, w_ref, *refs):
    refs[-1][...] = product(place_ref, w_ref, refs[:-1], rows).astype(jnp.bfloat16)


def project_packed(pieces, weight, place, rows):
    depth, dim = weight.shape
    tile = 512
    specs = [pl.BlockSpec(piece.shape, lambda i, p: (0, 0)) for piece in pieces]
    return pl.pallas_call(
        functools.partial(project_kernel, rows),
        grid_spec=pltpu.PrefetchScalarGridSpec(
            num_scalar_prefetch=1,
            grid=(dim // tile,),
            in_specs=[pl.BlockSpec((depth, tile), lambda i, p: (0, i))] + specs,
            out_specs=pl.BlockSpec((rows, tile), lambda i, p: (0, i)),
        ),
        out_shape=jax.ShapeDtypeStruct((rows, dim), jnp.bfloat16),
        compiler_params=pltpu.CompilerParams(vmem_limit_bytes=24 << 20),
        cost_estimate=pl.CostEstimate(
            flops=2 * rows * depth * dim, transcendentals=0, bytes_accessed=2 * depth * dim
        ),
        name="project_packed",
    )(place[None].astype(jnp.int32), weight, *pieces)


def finish_kernel(rows, place_ref, w_ref, *refs):
    pieces = refs[:-6]
    far_ref, hidden_ref, mod_ref, head_ref, out_ref, acc_ref = refs[-6:]
    step = pl.program_id(0)
    tile = w_ref.shape[1]
    acc_ref[step] = product(place_ref, w_ref, pieces, rows)

    @pl.when(step == pl.num_programs(0) - 1)
    def _():
        steps = acc_ref.shape[0]
        dim = steps * tile
        updated = []
        total = jnp.zeros((rows, 1), jnp.float32)
        for i in range(steps):
            cut = slice(i * tile, (i + 1) * tile)
            projected = acc_ref[i] + far_ref[:, cut].astype(jnp.float32)
            part = hidden_ref[:, cut].astype(jnp.float32) + mod_ref[0:1, cut] * projected
            acc_ref[i] = part
            total += jnp.sum(part, axis=-1, keepdims=True)
        average = total / dim
        square = jnp.zeros((rows, 1), jnp.float32)
        for i in range(steps):
            centred = acc_ref[i] - average
            square += jnp.sum(centred * centred, axis=-1, keepdims=True)
        rate = lax.rsqrt(square / dim + 1e-06)
        velocity = jnp.zeros((rows, out_ref.shape[1]), jnp.float32)
        for i in range(steps):
            cut = slice(i * tile, (i + 1) * tile)
            normed = (
                (acc_ref[i] - average) * rate * (1.0 + mod_ref[2:3, cut]) + mod_ref[1:2, cut]
            ).astype(jnp.bfloat16)
            velocity += lax.dot_general(
                normed,
                head_ref[:, cut],
                (((1,), (1,)), ((), ())),
                preferred_element_type=jnp.float32,
            )
        out_ref[...] = velocity


def finish(pieces, weight, far, hidden, modulation, head_rows, place, rows):
    depth, dim = weight.shape
    tile = 512
    steps = dim // tile
    patch = head_rows.shape[0]

    def whole(shape):
        return pl.BlockSpec(shape, lambda i, p: (0, 0))

    return pl.pallas_call(
        functools.partial(finish_kernel, rows),
        grid_spec=pltpu.PrefetchScalarGridSpec(
            num_scalar_prefetch=1,
            grid=(steps,),
            in_specs=[pl.BlockSpec((depth, tile), lambda i, p: (0, i))]
            + [whole(piece.shape) for piece in pieces]
            + [whole(far.shape), whole(hidden.shape), whole(modulation.shape)]
            + [whole(head_rows.shape)],
            out_specs=whole((rows, patch)),
            scratch_shapes=[pltpu.VMEM((steps, rows, tile), jnp.float32)],
        ),
        out_shape=jax.ShapeDtypeStruct((rows, patch), jnp.float32),
        compiler_params=pltpu.CompilerParams(vmem_limit_bytes=24 << 20),
        cost_estimate=pl.CostEstimate(
            flops=2 * rows * depth * dim, transcendentals=0, bytes_accessed=2 * depth * dim
        ),
        name="finish",
    )(place[None].astype(jnp.int32), weight, *pieces, far, hidden, modulation, head_rows)


def ordered(blocks, place):
    count = len(blocks)
    turned = jnp.stack([blocks[(-i) % count] for i in range(count)])
    return lax.dynamic_slice_in_dim(
        jnp.concatenate([turned, turned]), (count - place) % count, count, 0
    )


def packed_body(head_inputs, hidden, out_weight, time_weight, head_weight, latent, timesteps):
    count = lax.axis_size("seq")
    halves = lax.axis_size("fsdp")
    rows = head_inputs.shape[2]
    place = lax.axis_index("seq")
    half = lax.axis_index("fsdp")
    heads = HEADS // halves // count

    def along(block, r):
        return lax.ppermute(block, "seq", [(i, (i + r) % count) for i in range(count)])

    def across(block):
        return lax.ppermute(block, "fsdp", [(0, 1), (1, 0)])

    def slanted(block, r):
        route = []
        for i in range(count):
            for j in range(halves):
                route.append((i * halves + j, (i + r) % count * halves + 1 - j))
        return lax.ppermute(block, ("seq", "fsdp"), route)

    x = head_inputs.reshape(rows, head_inputs.shape[3])
    far_sent = split_heads(x, 1 - half, place, count, halves)
    near_sent = split_heads(x, half, place, count, halves)
    far_pieces = [far_sent[0]] + [along(far_sent[r], r) for r in range(1, count)]
    near_pieces = [near_sent[0]] + [along(near_sent[r], r) for r in range(1, count)]

    other_steps = across(timesteps)
    steps_both = jnp.concatenate([timesteps[0, :, 0], other_steps[0, :, 0]])
    embedding = time_embed(steps_both).astype(jnp.bfloat16)
    own_modulation = jnp.dot(embedding, time_weight[0], preferred_element_type=jnp.float32)
    other_modulation = across(own_modulation[1:])
    pair = jnp.where(
        half == 0,
        jnp.concatenate([own_modulation[:1], other_modulation]),
        jnp.concatenate([other_modulation, own_modulation[:1]]),
    )
    modulation = ordered([pair] + [along(pair, r) for r in range(1, count)], place)
    modulation = modulation.reshape(3, DIM)

    head_own = jnp.swapaxes(head_weight[0], 0, 1)
    head_line = ordered([head_own] + [along(head_own, r) for r in range(1, count)], place)
    head_other = across(head_line)
    head_pair = jnp.where(
        half == 0, jnp.stack([head_line, head_other]), jnp.stack([head_other, head_line])
    )
    head_rows = head_pair.transpose(2, 1, 0, 3).reshape(PATCH, DIM)

    far_attended = attend_packed(far_pieces, heads, rows)
    far_home = [slanted(far_attended[r], -r) for r in range(count)]
    partial = project_packed(far_home, out_weight[0], place, rows)
    partial = across(partial)
    near_attended = attend_packed(near_pieces, heads, rows)
    near_home = [near_attended[0]] + [along(near_attended[r], -r) for r in range(1, count)]
    velocity = finish(
        near_home,
        out_weight[0],
        partial,
        hidden.reshape(rows, DIM),
        modulation,
        head_rows,
        place,
        rows,
    )
    velocity = velocity.reshape(1, 1, rows // 2, 2 * PATCH)
    step_size = sigma_of(timesteps[0, :, 1]) - sigma_of(timesteps[0, :, 0])
    stepped = latent + step_size[None, :, None, None] * velocity
    carried = partner(stepped, "section", 0)
    return (velocity, carried)


def body(head_inputs, *rest):
    count = lax.axis_size("seq")
    halves = lax.axis_size("fsdp")
    rows = head_inputs.shape[2]
    fits = (
        head_inputs.shape[1] == 1
        and halves == 2
        and HEADS % (halves * count) == 0
        and HEADS // (halves * count) * HEAD % LANES == LANES // 2
        and rows % 32 == 0
        and rows * count <= 512
    )
    return (packed_body if fits else general_body)(head_inputs, *rest)


def solution(mesh):
    return jax.shard_map(
        body,
        mesh=mesh,
        in_specs=(
            P("section", ("grp", "fsdp"), "seq", None),
            P("section", ("grp", "fsdp"), "seq", None),
            P("section", "fsdp", None),
            P("section", None, ("seq", "fsdp")),
            P("section", ("seq", "fsdp"), None),
            P("section", ("grp", "fsdp"), "seq", None),
            P("section", ("grp", "fsdp"), None),
        ),
        out_specs=(
            P("section", ("grp", "fsdp"), "seq", None),
            P("section", ("grp", "fsdp"), "seq", None),
        ),
        check_vma=False,
    )
```

```python
import functools
import math

import jax
import jax.numpy as jnp
from jax import lax
from jax.experimental import pallas as pl
from jax.experimental.pallas import tpu as pltpu
from jax.sharding import PartitionSpec as P


DIM = 2560
HEADS = 32
HEAD = 80
PATCH = 64
FREQ = 256
LANES = 128


def partner(block, axis, apart):
    count = lax.axis_size(axis)
    route = []
    for low in range(count):
        high = low | 1 << apart
        if high != low and high < count:
            route += [(low, high), (high, low)]
    return lax.ppermute(block, axis, route)


def time_embed(steps_now):
    half = FREQ // 2
    freqs = jnp.exp(-math.log(10000.0) * jnp.arange(half, dtype=jnp.float32) / half)
    angle = steps_now.astype(jnp.float32)[..., None] * freqs
    return jnp.concatenate([jnp.cos(angle), jnp.sin(angle)], axis=-1)


def sigma_of(steps_now):
    unit_time = steps_now.astype(jnp.float32) / 1000.0
    return 5.0 * unit_time / (1.0 + 4.0 * unit_time)


def attend(exchanged):
    items = exchanged.shape[0]
    length = exchanged.shape[1]
    local_heads = exchanged.shape[2]
    query_all = exchanged[..., :HEAD]
    key_rows = exchanged[..., HEAD : 2 * HEAD]
    value_rows = exchanged[..., 2 * HEAD :]
    block_rows = min(512, length)
    block_count = length // block_rows

    def one_block(block_index):
        query_block = lax.dynamic_slice_in_dim(query_all, block_index * block_rows, block_rows, 1)
        scores = jnp.einsum(
            "nqhe,nkhe->nhqk", query_block, key_rows, preferred_element_type=jnp.float32
        ) * HEAD ** (-0.5)
        row_max = jnp.max(scores, axis=-1, keepdims=True)
        exp_scores = jnp.exp(scores - row_max)
        row_sum = jnp.sum(exp_scores, axis=-1, keepdims=True)
        weights = (exp_scores / row_sum).astype(jnp.bfloat16)
        return jnp.einsum(
            "nhqk,nkhe->nqhe", weights, value_rows, preferred_element_type=jnp.float32
        ).astype(jnp.bfloat16)

    blocks = lax.map(one_block, jnp.arange(block_count, dtype=jnp.int32))
    return blocks.transpose(1, 0, 2, 3, 4).reshape(items, length, local_heads * HEAD)


def general_body(head_inputs, hidden, out_weight, time_weight, head_weight, latent, timesteps):
    samples = head_inputs.shape[1]
    row_count = head_inputs.shape[2]
    flat_count = samples * row_count
    local = head_inputs.reshape(samples, row_count, HEADS, 3 * HEAD)
    attended = lax.all_to_all(
        attend(lax.all_to_all(local, "seq", split_axis=2, concat_axis=1, tiled=True)),
        "seq",
        split_axis=1,
        concat_axis=2,
        tiled=True,
    )
    flattened = attended.reshape(flat_count, HEADS * HEAD)
    time_full, head_full = (
        lax.all_gather(time_weight, ("seq", "fsdp"), axis=2, tiled=True),
        lax.all_gather(head_weight, ("seq", "fsdp"), axis=1, tiled=True),
    )
    embedding = time_embed(timesteps[0, :, 0]).astype(jnp.bfloat16)
    modulation = jnp.dot(embedding, time_full[0], preferred_element_type=jnp.float32)
    gate_term = modulation[:, None, :DIM]
    shift_term = modulation[:, None, DIM : 2 * DIM]
    scale_term = modulation[:, None, 2 * DIM :]
    own_columns = lax.all_to_all(flattened, "fsdp", split_axis=1, concat_axis=0, tiled=True)
    projected = lax.psum_scatter(
        jnp.dot(own_columns, out_weight[0], preferred_element_type=jnp.float32).astype(
            jnp.bfloat16
        ),
        "fsdp",
        scatter_dimension=0,
        tiled=True,
    ).astype(jnp.float32)
    updated = hidden.reshape(samples, row_count, DIM).astype(
        jnp.float32
    ) + gate_term * projected.reshape(samples, row_count, DIM)
    average = jnp.mean(updated, axis=-1, keepdims=True)
    centred = updated - average
    variance = jnp.mean(centred * centred, axis=-1, keepdims=True)
    normed = (centred * lax.rsqrt(variance + 1e-06) * (1.0 + scale_term) + shift_term).astype(
        jnp.bfloat16
    )
    velocity = jnp.dot(
        normed.reshape(flat_count, DIM), head_full[0], preferred_element_type=jnp.float32
    )
    velocity = velocity.reshape(1, samples, row_count // 2, 2 * PATCH)
    step_size = sigma_of(timesteps[0, :, 1]) - sigma_of(timesteps[0, :, 0])
    stepped = latent + step_size[None, :, None, None] * velocity
    carried = partner(stepped, "section", 0)
    return (velocity, carried)


def turn(half):
    return pltpu.roll(half.astype(jnp.float32), LANES // 2, 1)


def pack_half(tile):
    rows = tile.shape[0]
    wide = tile.astype(jnp.float32)
    lane = lax.broadcasted_iota(jnp.int32, (rows // 2, LANES), 1)
    return jnp.where(
        lane < LANES // 2, wide[: rows // 2], pltpu.roll(wide[rows // 2 :], LANES // 2, 1)
    ).astype(jnp.bfloat16)


def unpack_tiles(ref, rows, width):
    whole = width // LANES
    tiles = [ref[t * rows : (t + 1) * rows, :] for t in range(whole)]
    last = ref[whole * rows : whole * rows + rows // 2, :]
    tiles.append(jnp.concatenate([last, turn(last).astype(jnp.bfloat16)], axis=0))
    return tiles


def head_tiles(width):
    return -(-width // LANES)


MOD_ROWS = 32


def put_head(out, at, head_ref, group_ref):
    patch, width = head_ref.shape
    cut = patch // 2
    mine = pl.ds(pl.multiple_of(group_ref[0] * cut, cut), cut)
    for t in range(head_tiles(width)):
        lanes = min(LANES, width - t * LANES)
        out[at + t * cut : at + (t + 1) * cut, :lanes] = head_ref[
            mine, t * LANES : t * LANES + lanes
        ]


def put_modulation(out, at, row):
    width = row.shape[1]
    tiles = -(-width // LANES)
    left = jnp.concatenate([row, jnp.zeros((1, tiles * LANES - width), jnp.float32)], axis=1)
    left = jnp.concatenate(
        [left[:, t * LANES : (t + 1) * LANES] for t in range(tiles)]
        + [jnp.zeros((8 - tiles, LANES), jnp.float32)][: 8 - tiles],
        axis=0,
    )
    terms = []
    for _ in range(3):
        term = left.astype(jnp.bfloat16).astype(jnp.float32)
        terms.append(term)
        left = left - term
    terms.append(jnp.zeros_like(left))
    out[at : at + MOD_ROWS, :] = jnp.concatenate(terms, axis=0).astype(jnp.bfloat16)


def get_modulation(ref, at, width):
    terms = ref[at : at + MOD_ROWS, :].astype(jnp.float32)
    total = terms[0:8] + terms[8:16] + terms[16:24]
    tiles = -(-width // LANES)
    return jnp.concatenate([total[t : t + 1] for t in range(tiles)], axis=1)[:, :width]


def near_extra(count):
    return [(r not in (0, count // 2), r != 0) for r in range(count)]


def far_extra(count):
    return [(r == count // 2, False) for r in range(count)]


def split_kernel(width, flip, extra, place_ref, half_ref, group_ref, x_ref, *refs):
    count = len(extra)
    head_ref, refs = refs[0], refs[1:]
    if not flip:
        mod_ref, refs = refs[0], refs[1:]
    outs, held, sems = refs[:count], refs[count], refs[count + 1]
    rows = x_ref.shape[0]
    whole = width // LANES
    me = place_ref[0]
    half = 1 - half_ref[0] if flip else half_ref[0]
    base = half * (count * width)

    def window(r):
        to = me ^ r
        start = pl.multiple_of(base + lax.div(to * width, LANES) * LANES, LANES)
        return pltpu.make_async_copy(
            x_ref.at[:, pl.ds(start, (whole + 1) * LANES)], held.at[r], sems.at[r]
        )

    order = [r for r in range(count) if r != 0] + [0]
    for r in order:
        window(r).start()
    packed = rows * width // LANES
    for r in order:
        at = packed
        if extra[r][0]:
            put_head(outs[r], at, head_ref, group_ref)
            at += head_ref.shape[0] // 2 * head_tiles(head_ref.shape[1])
        if extra[r][1]:
            put_modulation(outs[r], at, mod_ref[0:1, :])
    for r in order:
        window(r).wait()
        odd = lax.rem(me ^ r, 2) == 1
        last = slice(whole * rows, packed)

        @pl.when(jnp.logical_not(odd))
        def _():
            for t in range(whole):
                outs[r][t * rows : (t + 1) * rows, :] = held[r, :, t * LANES : (t + 1) * LANES]
            outs[r][last, :] = pack_half(held[r, :, whole * LANES :])

        @pl.when(odd)
        def _():
            lane = lax.broadcasted_iota(jnp.int32, (rows, LANES), 1)
            turned = [turn(held[r, :, t * LANES : (t + 1) * LANES]) for t in range(whole + 1)]
            for t in range(whole):
                outs[r][t * rows : (t + 1) * rows, :] = jnp.where(
                    lane < LANES // 2, turned[t], turned[t + 1]
                ).astype(jnp.bfloat16)
            outs[r][last, :] = pack_half(turned[whole])


def split_heads(x, flip, extra, scalars, riders, halves):
    rows, columns = x.shape
    count = len(extra)
    width = columns // halves // count
    head = riders[0]
    pieces = []
    for with_head, with_mod in extra:
        length = rows * width // LANES
        length += head.shape[0] // 2 * head_tiles(head.shape[1]) * with_head
        length += MOD_ROWS * with_mod
        pieces.append(jax.ShapeDtypeStruct((length, LANES), jnp.bfloat16))
    return pl.pallas_call(
        functools.partial(split_kernel, width, flip, extra),
        in_specs=[pl.BlockSpec(memory_space=pltpu.SMEM)] * 3
        + [pl.BlockSpec(memory_space=pltpu.HBM)]
        + [pl.BlockSpec(memory_space=pltpu.VMEM)] * len(riders),
        out_shape=pieces,
        scratch_shapes=[
            pltpu.VMEM((count, rows, (width // LANES + 1) * LANES), jnp.bfloat16),
            pltpu.SemaphoreType.DMA((count,)),
        ],
        compiler_params=pltpu.CompilerParams(vmem_limit_bytes=4 << 20),
        cost_estimate=pl.CostEstimate(
            flops=0, transcendentals=0, bytes_accessed=4 * rows * columns // halves
        ),
        name="split_heads",
    )(*scalars, pltpu.with_memory_space_constraint(x, pltpu.HBM), *riders)


def load_kernel(count, place_ref, w_ref, out_ref, sems):
    depth = w_ref.shape[0] // count

    def block(r):
        owner = place_ref[0] ^ r
        return pltpu.make_async_copy(
            w_ref.at[pl.ds(pl.multiple_of(owner * depth, depth), depth), :],
            out_ref.at[r * depth : (r + 1) * depth, :],
            sems.at[r],
        )

    for r in range(count):
        block(r).start()
    for r in range(count):
        block(r).wait()


def load_rows(weight, place, count):
    return pl.pallas_call(
        functools.partial(load_kernel, count),
        in_specs=[
            pl.BlockSpec(memory_space=pltpu.SMEM),
            pl.BlockSpec(memory_space=pltpu.HBM),
        ],
        out_specs=pl.BlockSpec(memory_space=pltpu.VMEM),
        out_shape=pltpu.VMEM(weight.shape, weight.dtype),
        scratch_shapes=[pltpu.SemaphoreType.DMA((count,))],
        compiler_params=pltpu.CompilerParams(vmem_limit_bytes=2 << 20),
        cost_estimate=pl.CostEstimate(
            flops=0, transcendentals=0, bytes_accessed=2 * weight.size * 2
        ),
        name="load_rows",
    )(place, pltpu.with_memory_space_constraint(weight, pltpu.HBM))


def attend_kernel(heads, rows, count, *refs):
    riders, ins, outs = refs[: -2 * count], refs[-2 * count : -count], refs[-count:]
    width = heads * 3 * HEAD
    blocks = [unpack_tiles(ref, rows, width) for ref in ins]

    def columns(start):
        first, offset = divmod(start, LANES)
        parts = []
        for tiles in blocks:
            if offset + HEAD <= LANES:
                parts.append(tiles[first][:, offset : offset + HEAD])
            else:
                wide = jnp.concatenate([tiles[first], tiles[first + 1]], axis=1)
                parts.append(wide[:, offset : offset + HEAD])
        return jnp.concatenate(parts, axis=0)

    results = []
    for h in range(heads):
        start = h * 3 * HEAD
        query, key, value = (columns(start + i * HEAD) for i in range(3))
        scores = lax.dot_general(
            query, key, (((1,), (1,)), ((), ())), preferred_element_type=jnp.float32
        ) * HEAD ** (-0.5)
        row_max = jnp.max(scores, axis=-1, keepdims=True)
        exp_scores = jnp.exp(scores - row_max)
        row_sum = jnp.sum(exp_scores, axis=-1, keepdims=True)
        weights = (exp_scores / row_sum).astype(jnp.bfloat16)
        results.append(jnp.dot(weights, value, preferred_element_type=jnp.float32))
    attended = jnp.concatenate(results, axis=1).astype(jnp.bfloat16)
    whole = heads * HEAD // LANES
    for b in range(count):
        mine = attended[b * rows : (b + 1) * rows]
        for t in range(whole):
            outs[b][t * rows : (t + 1) * rows, :] = mine[:, t * LANES : (t + 1) * LANES]
        rest = mine[:, whole * LANES :].astype(jnp.float32)
        packed = rows * heads * HEAD // LANES
        outs[b][whole * rows : packed, :] = jnp.concatenate(
            [rest[: rows // 2], rest[rows // 2 :]], axis=1
        ).astype(jnp.bfloat16)
        if riders:
            group_ref, head_ref, mod_ref = riders
            put_head(outs[b], packed, head_ref, group_ref)
            packed += head_ref.shape[0] // 2 * head_tiles(head_ref.shape[1])
            put_modulation(outs[b], packed, mod_ref[1:2, :])


def attend_packed(pieces, heads, rows, riders=()):
    count = len(pieces)
    total = count * rows
    length = rows * heads * HEAD // LANES
    specs = [pl.BlockSpec(memory_space=pltpu.VMEM)] * count
    if riders:
        head = riders[1]
        length += head.shape[0] // 2 * head_tiles(head.shape[1]) + MOD_ROWS
        specs = [pl.BlockSpec(memory_space=pltpu.SMEM)] + specs + specs[:2]
    out = jax.ShapeDtypeStruct((length, LANES), jnp.bfloat16)
    return pl.pallas_call(
        functools.partial(attend_kernel, heads, rows, count),
        in_specs=specs,
        out_shape=[out] * count,
        compiler_params=pltpu.CompilerParams(vmem_limit_bytes=12 << 20),
        cost_estimate=pl.CostEstimate(
            flops=4 * heads * total * total * HEAD,
            transcendentals=heads * total * total,
            bytes_accessed=8 * total * heads * HEAD,
        ),
        name="attend_packed",
    )(*riders, *pieces)


def gather_left(refs, left_ref, rows):
    depth = left_ref.shape[1] // len(refs)
    left_ref[...] = jnp.concatenate(
        [jnp.concatenate(unpack_tiles(ref, rows, depth), axis=1)[:, :depth] for ref in refs],
        axis=1,
    )


def project_kernel(rows, w_ref, *refs):
    pieces, out_ref, left_ref = refs[:-2], refs[-2], refs[-1]
    gather_left(pieces, left_ref, rows)
    for start in range(0, w_ref.shape[1], 512):
        cut = slice(start, start + 512)
        out_ref[:, cut] = jnp.dot(
            left_ref[...], w_ref[:, cut], preferred_element_type=jnp.float32
        ).astype(jnp.bfloat16)


def project_packed(pieces, weight, rows):
    depth, dim = weight.shape
    return pl.pallas_call(
        functools.partial(project_kernel, rows),
        out_shape=jax.ShapeDtypeStruct((rows, dim), jnp.bfloat16),
        scratch_shapes=[pltpu.VMEM((rows, depth), jnp.bfloat16)],
        compiler_params=pltpu.CompilerParams(vmem_limit_bytes=16 << 20),
        cost_estimate=pl.CostEstimate(
            flops=2 * rows * depth * dim, transcendentals=0, bytes_accessed=2 * depth * dim
        ),
        name="project_packed",
    )(pltpu.with_memory_space_constraint(weight, pltpu.VMEM), *pieces)


def finish_kernel(rows, count, size_ref, w_ref, *refs):
    pieces, refs = refs[:count], refs[count:]
    mod_ref, far_ref, hidden_ref, head_ref, latent_ref, out_ref, step_ref = refs[:7]
    acc_ref, left_ref, turn_ref = refs[7:]
    steps, _, tile = acc_ref.shape
    dim = steps * tile

    def modulation(which, i):
        start = which * dim + i * tile
        line, offset = divmod(start, mod_ref.shape[2])
        return mod_ref[line, :, offset : offset + tile]

    gather_left(pieces, left_ref, rows)
    total = jnp.zeros((rows, 1), jnp.float32)
    for i in range(steps):
        cut = slice(i * tile, (i + 1) * tile)
        projected = jnp.dot(left_ref[...], w_ref[:, cut], preferred_element_type=jnp.float32)
        projected = projected + far_ref[:, cut].astype(jnp.float32)
        part = hidden_ref[:, cut].astype(jnp.float32) + modulation(0, i) * projected
        acc_ref[i] = part
        total += jnp.sum(part, axis=-1, keepdims=True)
    average = total / dim
    square = jnp.zeros((rows, 1), jnp.float32)
    for i in range(steps):
        centred = acc_ref[i] - average
        square += jnp.sum(centred * centred, axis=-1, keepdims=True)
    rate = lax.rsqrt(square / dim + 1e-06)
    velocity = jnp.zeros(turn_ref.shape, jnp.float32)
    for i in range(steps):
        cut = slice(i * tile, (i + 1) * tile)
        normed = (
            (acc_ref[i] - average) * rate * (1.0 + modulation(2, i)) + modulation(1, i)
        ).astype(jnp.bfloat16)
        velocity += lax.dot_general(
            normed,
            head_ref[:, cut],
            (((1,), (1,)), ((), ())),
            preferred_element_type=jnp.float32,
        )
    turn_ref[...] = velocity
    paired = jnp.concatenate(
        [turn_ref[pl.ds(0, rows // 2, stride=2), :], turn_ref[pl.ds(1, rows // 2, stride=2), :]],
        axis=1,
    )
    out_ref[...] = paired
    step_ref[...] = latent_ref[...] + size_ref[0] * paired


def finish(pieces, weight, far, hidden, lines, head_rows, latent, size, rows):
    depth, dim = weight.shape
    count = len(pieces)
    tile = math.gcd(dim, lines.shape[2])
    patch = head_rows.shape[0]
    inputs = (pltpu.with_memory_space_constraint(weight, pltpu.VMEM), *pieces, lines)
    inputs += (far, hidden, head_rows, latent)
    result = jax.ShapeDtypeStruct((rows // 2, 2 * patch), jnp.float32)
    return pl.pallas_call(
        functools.partial(finish_kernel, rows, count),
        in_specs=[pl.BlockSpec(memory_space=pltpu.SMEM)]
        + [pl.BlockSpec(memory_space=pltpu.VMEM)] * len(inputs),
        out_shape=[result] * 2,
        scratch_shapes=[
            pltpu.VMEM((dim // tile, rows, tile), jnp.float32),
            pltpu.VMEM((rows, depth), jnp.bfloat16),
            pltpu.VMEM((rows, patch), jnp.float32),
        ],
        compiler_params=pltpu.CompilerParams(vmem_limit_bytes=16 << 20),
        cost_estimate=pl.CostEstimate(
            flops=2 * rows * depth * dim, transcendentals=0, bytes_accessed=2 * depth * dim
        ),
        name="finish",
    )(size, *inputs)


def collect_kernel(count, packed, done, group_ref, head_ref, *refs):
    queries, far, out_ref = refs[:count], refs[count:-1], refs[-1]
    span = out_ref.shape[0] // (2 * count)
    put_head(out_ref, 0, head_ref, group_ref)
    for r in range(1, count):
        out_ref[r * span : (r + 1) * span, :] = queries[r][packed : packed + span, :]
    for r in range(count):
        out_ref[(count + r) * span : (count + r + 1) * span, :] = far[r][done : done + span, :]


def collect_head(queries, far, head, group, packed, done):
    count = len(far)
    span = head.shape[0] // 2 * head_tiles(head.shape[1])
    return pl.pallas_call(
        functools.partial(collect_kernel, count, packed, done),
        in_specs=[pl.BlockSpec(memory_space=pltpu.SMEM)]
        + [pl.BlockSpec(memory_space=pltpu.VMEM)] * (1 + 2 * count),
        out_shape=jax.ShapeDtypeStruct((2 * count * span, LANES), jnp.bfloat16),
        compiler_params=pltpu.CompilerParams(vmem_limit_bytes=4 << 20),
        cost_estimate=pl.CostEstimate(
            flops=0, transcendentals=0, bytes_accessed=8 * count * span * LANES
        ),
        name="collect_head",
    )(group, head, *queries, *far)


def arrange_kernel(count, width, near_at, done, place_ref, half_ref, group_ref, *refs):
    mine_ref, up_ref, mod_ref = refs[:3]
    near, far = refs[3 : 3 + count], refs[3 + count : -2]
    head_out, mod_out = refs[-2:]
    span = mine_ref.shape[0] // (2 * count)
    cut = head_out.shape[0] // 2
    tiles = span // cut
    first = half_ref[0] == 0
    lower = group_ref[0] == 0
    columns = mod_ref.shape[1]

    def block(ref, k):
        parts = [ref[k * span + t * cut : k * span + (t + 1) * cut, :] for t in range(tiles)]
        return jnp.concatenate(parts, axis=1)[:, :width]

    def whole(k):
        mine, up = block(mine_ref, k), block(up_ref, k)
        return jnp.concatenate(
            [jnp.where(lower, mine, up), jnp.where(lower, up, mine)], axis=0
        )

    for r in range(count):
        owner = place_ref[0] ^ r
        own, other = whole(r), whole(count + r)
        start = pl.multiple_of(owner * 2 * width, LANES)
        head_out[:, pl.ds(start, 2 * width)] = jnp.concatenate(
            [jnp.where(first, own, other), jnp.where(first, other, own)], axis=1
        )
        own = mod_ref[0:1, :] if r == 0 else get_modulation(near[r], near_at[r], columns)
        other = get_modulation(far[r], done + span, columns)
        mod_out[owner] = jnp.concatenate(
            [jnp.where(first, own, other), jnp.where(first, other, own)], axis=1
        )


def arrange(mine, up, modulation, near, far, head, scalars, near_at, done):
    count = len(far)
    patch, width = head.shape
    columns = modulation.shape[1]
    return pl.pallas_call(
        functools.partial(arrange_kernel, count, width, near_at, done),
        in_specs=[pl.BlockSpec(memory_space=pltpu.SMEM)] * 3
        + [pl.BlockSpec(memory_space=pltpu.VMEM)] * (3 + 2 * count),
        out_shape=[
            jax.ShapeDtypeStruct((patch, 2 * count * width), jnp.bfloat16),
            jax.ShapeDtypeStruct((count, 1, 2 * columns), jnp.float32),
        ],
        compiler_params=pltpu.CompilerParams(vmem_limit_bytes=4 << 20),
        cost_estimate=pl.CostEstimate(
            flops=0, transcendentals=0, bytes_accessed=8 * count * patch * width
        ),
        name="arrange",
    )(*scalars, mine, up, modulation, *near, *far)


def packed_body(head_inputs, hidden, out_weight, time_weight, head_weight, latent, timesteps):
    count = lax.axis_size("seq")
    halves = lax.axis_size("fsdp")
    rows = head_inputs.shape[2]
    place = lax.axis_index("seq")
    half = lax.axis_index("fsdp")
    group = lax.axis_index("grp")
    heads = HEADS // halves // count

    def along(block, r):
        return lax.ppermute(block, "seq", [(i, i ^ r) for i in range(count)])

    def swap(block, axis):
        return lax.ppermute(block, axis, [(0, 1), (1, 0)])

    def slanted(block, r):
        route = []
        for i in range(count):
            for j in range(halves):
                route.append((i * halves + j, (i ^ r) * halves + 1 - j))
        return lax.ppermute(block, ("seq", "fsdp"), route)

    x = head_inputs.reshape(rows, head_inputs.shape[3])
    head = jnp.swapaxes(head_weight[0], 0, 1)
    span = head.shape[0] // 2 * head_tiles(head.shape[1])
    here = place[None].astype(jnp.int32)
    side = half[None].astype(jnp.int32)
    level = group[None].astype(jnp.int32)
    scalars = (here, side, level)
    far_rides, near_rides = far_extra(count), near_extra(count)

    far_sent = split_heads(x, True, far_rides, scalars, (head,), halves)
    far_pieces = [far_sent[0]] + [along(far_sent[r], r) for r in range(1, count)]

    other_steps = swap(timesteps, "fsdp")
    steps_both = jnp.concatenate([timesteps[0, :, 0], other_steps[0, :, 0]])
    embedding = time_embed(steps_both).astype(jnp.bfloat16)
    modulation = jnp.dot(embedding, time_weight[0], preferred_element_type=jnp.float32)
    step_size = sigma_of(timesteps[0, :, 1]) - sigma_of(timesteps[0, :, 0])

    near_sent = split_heads(x, False, near_rides, scalars, (head, modulation), halves)
    near_pieces = [near_sent[0]] + [along(near_sent[r], r) for r in range(1, count)]

    weight = load_rows(out_weight[0], here, count)
    far_attended = attend_packed(far_pieces, heads, rows, (level, head, modulation))
    far_home = [slanted(far_attended[r], r) for r in range(count)]
    partial = project_packed(far_home, weight, rows)
    partial = swap(partial, "fsdp")

    packed = far_sent[0].shape[0]
    done = far_home[0].shape[0] - span - MOD_ROWS
    queries = [far_pieces[r] if far_rides[r][0] else near_pieces[r] for r in range(count)]
    near_at = [packed + span * with_head for with_head, _ in near_rides]
    mine = collect_head(queries, far_home, head, level, packed, done)
    up = swap(mine, "grp")
    head_rows, lines = arrange(
        mine, up, modulation, near_pieces, far_home, head, scalars, near_at, done
    )

    near_attended = attend_packed(near_pieces, heads, rows)
    near_home = [near_attended[0]]
    near_home += [along(near_attended[r], r) for r in range(1, count)]
    velocity, stepped = finish(
        near_home,
        weight,
        partial,
        hidden.reshape(rows, DIM),
        lines,
        head_rows,
        latent.reshape(rows // 2, 2 * PATCH),
        step_size,
        rows,
    )
    carried = partner(stepped, "section", 0)
    return (velocity.reshape(latent.shape), carried.reshape(latent.shape))


def packed_fits(mesh, head_shape):
    count, halves = mesh.shape["seq"], mesh.shape["fsdp"]
    rows = head_shape[2]
    return (
        head_shape[1] == 1
        and halves == 2
        and mesh.shape["grp"] == 2
        and count & (count - 1) == 0
        and HEADS % (halves * count) == 0
        and 3 * DIM // (halves * count) <= 8 * LANES
        and DIM % (halves * count) == 0
        and HEADS // (halves * count) * HEAD % LANES == LANES // 2
        and rows % 32 == 0
        and rows * count <= 512
    )


def step(mesh, body):
    return jax.shard_map(
        body,
        mesh=mesh,
        in_specs=(
            P("section", ("grp", "fsdp"), "seq", None),
            P("section", ("grp", "fsdp"), "seq", None),
            P("section", "fsdp", None),
            P("section", None, ("seq", "fsdp")),
            P("section", ("seq", "fsdp"), None),
            P("section", ("grp", "fsdp"), "seq", None),
            P("section", ("grp", "fsdp"), None),
        ),
        out_specs=(
            P("section", ("grp", "fsdp"), "seq", None),
            P("section", ("grp", "fsdp"), "seq", None),
        ),
        check_vma=False,
    )


def solution(mesh):
    def choose(head_inputs, *rest):
        local = (
            head_inputs.shape[0] // mesh.shape["section"],
            head_inputs.shape[1] // mesh.shape["grp"] // mesh.shape["fsdp"],
            head_inputs.shape[2] // mesh.shape["seq"],
        )
        if not packed_fits(mesh, local):
            return step(mesh, general_body)(head_inputs, *rest)
        return step(mesh, packed_body)(head_inputs, *rest)

    return choose
```

```python
import functools
import math

import jax
import jax.numpy as jnp
from jax import lax
from jax.experimental import pallas as pl
from jax.experimental.pallas import tpu as pltpu
from jax.sharding import PartitionSpec as P


DIM = 2560
HEADS = 32
HEAD = 80
PATCH = 64
FREQ = 256
LANES = 128


def partner(block, axis, apart):
    count = lax.axis_size(axis)
    route = []
    for low in range(count):
        high = low | 1 << apart
        if high != low and high < count:
            route += [(low, high), (high, low)]
    return lax.ppermute(block, axis, route)


def time_embed(steps_now):
    half = FREQ // 2
    freqs = jnp.exp(-math.log(10000.0) * jnp.arange(half, dtype=jnp.float32) / half)
    angle = steps_now.astype(jnp.float32)[..., None] * freqs
    return jnp.concatenate([jnp.cos(angle), jnp.sin(angle)], axis=-1)


def sigma_of(steps_now):
    unit_time = steps_now.astype(jnp.float32) / 1000.0
    return 5.0 * unit_time / (1.0 + 4.0 * unit_time)


def attend(exchanged):
    items = exchanged.shape[0]
    length = exchanged.shape[1]
    local_heads = exchanged.shape[2]
    query_all = exchanged[..., :HEAD]
    key_rows = exchanged[..., HEAD : 2 * HEAD]
    value_rows = exchanged[..., 2 * HEAD :]
    block_rows = min(512, length)
    block_count = length // block_rows

    def one_block(block_index):
        query_block = lax.dynamic_slice_in_dim(query_all, block_index * block_rows, block_rows, 1)
        scores = jnp.einsum(
            "nqhe,nkhe->nhqk", query_block, key_rows, preferred_element_type=jnp.float32
        ) * HEAD ** (-0.5)
        row_max = jnp.max(scores, axis=-1, keepdims=True)
        exp_scores = jnp.exp(scores - row_max)
        row_sum = jnp.sum(exp_scores, axis=-1, keepdims=True)
        weights = (exp_scores / row_sum).astype(jnp.bfloat16)
        return jnp.einsum(
            "nhqk,nkhe->nqhe", weights, value_rows, preferred_element_type=jnp.float32
        ).astype(jnp.bfloat16)

    blocks = lax.map(one_block, jnp.arange(block_count, dtype=jnp.int32))
    return blocks.transpose(1, 0, 2, 3, 4).reshape(items, length, local_heads * HEAD)


def general_body(head_inputs, hidden, out_weight, time_weight, head_weight, latent, timesteps):
    samples = head_inputs.shape[1]
    row_count = head_inputs.shape[2]
    flat_count = samples * row_count
    local = head_inputs.reshape(samples, row_count, HEADS, 3 * HEAD)
    attended = lax.all_to_all(
        attend(lax.all_to_all(local, "seq", split_axis=2, concat_axis=1, tiled=True)),
        "seq",
        split_axis=1,
        concat_axis=2,
        tiled=True,
    )
    flattened = attended.reshape(flat_count, HEADS * HEAD)
    time_full, head_full = (
        lax.all_gather(time_weight, ("seq", "fsdp"), axis=2, tiled=True),
        lax.all_gather(head_weight, ("seq", "fsdp"), axis=1, tiled=True),
    )
    embedding = time_embed(timesteps[0, :, 0]).astype(jnp.bfloat16)
    modulation = jnp.dot(embedding, time_full[0], preferred_element_type=jnp.float32)
    gate_term = modulation[:, None, :DIM]
    shift_term = modulation[:, None, DIM : 2 * DIM]
    scale_term = modulation[:, None, 2 * DIM :]
    own_columns = lax.all_to_all(flattened, "fsdp", split_axis=1, concat_axis=0, tiled=True)
    projected = lax.psum_scatter(
        jnp.dot(own_columns, out_weight[0], preferred_element_type=jnp.float32).astype(
            jnp.bfloat16
        ),
        "fsdp",
        scatter_dimension=0,
        tiled=True,
    ).astype(jnp.float32)
    updated = hidden.reshape(samples, row_count, DIM).astype(
        jnp.float32
    ) + gate_term * projected.reshape(samples, row_count, DIM)
    average = jnp.mean(updated, axis=-1, keepdims=True)
    centred = updated - average
    variance = jnp.mean(centred * centred, axis=-1, keepdims=True)
    normed = (centred * lax.rsqrt(variance + 1e-06) * (1.0 + scale_term) + shift_term).astype(
        jnp.bfloat16
    )
    velocity = jnp.dot(
        normed.reshape(flat_count, DIM), head_full[0], preferred_element_type=jnp.float32
    )
    velocity = velocity.reshape(1, samples, row_count // 2, 2 * PATCH)
    step_size = sigma_of(timesteps[0, :, 1]) - sigma_of(timesteps[0, :, 0])
    stepped = latent + step_size[None, :, None, None] * velocity
    carried = partner(stepped, "section", 0)
    return (velocity, carried)


def turn(half):
    return pltpu.roll(half.astype(jnp.float32), LANES // 2, 1)


def pack_half(tile):
    rows = tile.shape[0]
    wide = tile.astype(jnp.float32)
    lane = lax.broadcasted_iota(jnp.int32, (rows // 2, LANES), 1)
    return jnp.where(
        lane < LANES // 2, wide[: rows // 2], pltpu.roll(wide[rows // 2 :], LANES // 2, 1)
    ).astype(jnp.bfloat16)


def unpack_tiles(ref, rows, width):
    whole = width // LANES
    tiles = [ref[t * rows : (t + 1) * rows, :] for t in range(whole)]
    last = ref[whole * rows : whole * rows + rows // 2, :]
    tiles.append(jnp.concatenate([last, turn(last).astype(jnp.bfloat16)], axis=0))
    return tiles


def head_tiles(width):
    return -(-width // LANES)


MOD_ROWS = 16


def put_modulation(out, at, row):
    width = row.shape[1]
    tiles = -(-width // LANES)
    left = jnp.concatenate([row, jnp.zeros((1, tiles * LANES - width), jnp.float32)], axis=1)
    left = jnp.concatenate(
        [left[:, t * LANES : (t + 1) * LANES] for t in range(tiles)]
        + [jnp.zeros((8 - tiles, LANES), jnp.float32)][: 8 - tiles],
        axis=0,
    )
    high = left.astype(jnp.bfloat16)
    low = (left - high.astype(jnp.float32)).astype(jnp.bfloat16)
    out[at : at + MOD_ROWS, :] = jnp.concatenate([high, low], axis=0)


def get_modulation(ref, at, width):
    terms = ref[at : at + MOD_ROWS, :].astype(jnp.float32)
    total = terms[0:8] + terms[8:16]
    tiles = -(-width // LANES)
    return jnp.concatenate([total[t : t + 1] for t in range(tiles)], axis=1)[:, :width]


def cut_window(width, held, out, r, odd):
    rows = held.shape[1]
    whole = width // LANES
    last = slice(whole * rows, rows * width // LANES)

    @pl.when(jnp.logical_not(odd))
    def _():
        for t in range(whole):
            out[t * rows : (t + 1) * rows, :] = held[r, :, t * LANES : (t + 1) * LANES]
        out[last, :] = pack_half(held[r, :, whole * LANES :])

    @pl.when(odd)
    def _():
        lane = lax.broadcasted_iota(jnp.int32, (rows, LANES), 1)
        turned = [turn(held[r, :, t * LANES : (t + 1) * LANES]) for t in range(whole + 1)]
        for t in range(whole):
            out[t * rows : (t + 1) * rows, :] = jnp.where(
                lane < LANES // 2, turned[t], turned[t + 1]
            ).astype(jnp.bfloat16)
        out[last, :] = pack_half(turned[whole])


def windows(x_ref, held, sems, me, half, count, width):
    span = held.shape[2]

    def window(r):
        start = half * (count * width) + lax.div((me ^ r) * width, LANES) * LANES
        return pltpu.make_async_copy(
            x_ref.at[:, pl.ds(pl.multiple_of(start, LANES), span)], held.at[r], sems.at[r]
        )

    return [window(r) for r in range(count)]


def sigma_row(step):
    unit_time = jnp.full((1, LANES), step, jnp.int32).astype(jnp.float32) / 1000.0
    return 5.0 * unit_time / (1.0 + 4.0 * unit_time)


def far_kernel(width, count, place_ref, half_ref, group_ref, when_ref, x_ref, head_ref, *refs):
    outs, refs = refs[:count], refs[count:]
    pack_ref, clock_ref, held, head_held, steps_ref, sems, head_sem, steps_sem = refs
    me = place_ref[0]
    cut, columns = head_held.shape
    order = [count // 2] + [r for r in range(count - 1, -1, -1) if r != count // 2]
    copies = windows(x_ref, held, sems, me, 1 - half_ref[0], count, width)
    head_copy = pltpu.make_async_copy(
        head_ref.at[pl.ds(pl.multiple_of(group_ref[0] * cut, cut), cut), :], head_held, head_sem
    )
    steps_copy = pltpu.make_async_copy(when_ref, steps_ref, steps_sem)
    copies[order[0]].start()
    steps_copy.start()
    head_copy.start()
    for r in order[1:]:
        copies[r].start()
    packed = outs[0].shape[0]
    for r in order:
        copies[r].wait()
        cut_window(width, held, outs[r], r, lax.rem(me ^ r, 2) == 1)
    head_copy.wait()
    for t in range(head_tiles(columns)):
        tile = head_held[:, t * LANES : min((t + 1) * LANES, columns)]
        if tile.shape[1] < LANES:
            fill = jnp.zeros((cut, LANES - tile.shape[1]), tile.dtype)
            tile = jnp.concatenate([tile, fill], axis=1)
        pack_ref[t * cut : (t + 1) * cut, :] = tile
        for r in range(1, count):
            outs[r][packed + t * cut : packed + (t + 1) * cut, :] = tile
    steps_copy.wait()
    now = jnp.full((1, LANES), steps_ref[0, 0], jnp.int32).astype(jnp.float32)
    change = sigma_row(steps_ref[0, 1]) - sigma_row(steps_ref[0, 0])
    clock_ref[...] = jnp.concatenate([now, change])


def split_far(x, head, steps, scalars, count, halves):
    rows, columns = x.shape
    width = columns // halves // count
    cut = head.shape[0] // 2
    span = cut * head_tiles(head.shape[1])
    length = rows * width // LANES
    pieces = [
        jax.ShapeDtypeStruct((length + span * (r != 0), LANES), jnp.bfloat16)
        for r in range(count)
    ]
    results = pl.pallas_call(
        functools.partial(far_kernel, width, count),
        in_specs=[pl.BlockSpec(memory_space=pltpu.SMEM)] * 3
        + [pl.BlockSpec(memory_space=pltpu.HBM)] * 3,
        out_shape=pieces
        + [
            jax.ShapeDtypeStruct((span, LANES), jnp.bfloat16),
            jax.ShapeDtypeStruct((2, LANES), jnp.float32),
        ],
        scratch_shapes=[
            pltpu.VMEM((count, rows, (width // LANES + 1) * LANES), jnp.bfloat16),
            pltpu.VMEM((cut, head.shape[1]), jnp.bfloat16),
            pltpu.SMEM((1, 2), jnp.int32),
            pltpu.SemaphoreType.DMA((count,)),
            pltpu.SemaphoreType.DMA,
            pltpu.SemaphoreType.DMA,
        ],
        compiler_params=pltpu.CompilerParams(vmem_limit_bytes=4 << 20),
        cost_estimate=pl.CostEstimate(
            flops=0, transcendentals=0, bytes_accessed=4 * rows * columns // halves
        ),
        name="split_far",
    )(
        *scalars,
        pltpu.with_memory_space_constraint(steps, pltpu.HBM),
        pltpu.with_memory_space_constraint(x, pltpu.HBM),
        pltpu.with_memory_space_constraint(head, pltpu.HBM),
    )
    return results[:count], results[count], results[count + 1]


def near_kernel(width, count, place_ref, half_ref, x_ref, mod_ref, *refs):
    outs, held, sems = refs[:count], refs[count], refs[count + 1]
    me = place_ref[0]
    copies = windows(x_ref, held, sems, me, half_ref[0], count, width)
    for r in range(count - 1, -1, -1):
        copies[r].start()
    for r in range(1, count):
        put_modulation(outs[r], outs[0].shape[0], mod_ref[0:1, :])
    for r in range(count - 1, -1, -1):
        copies[r].wait()
        cut_window(width, held, outs[r], r, lax.rem(me ^ r, 2) == 1)


def split_near(x, modulation, scalars, count, halves):
    rows, columns = x.shape
    width = columns // halves // count
    length = rows * width // LANES
    return pl.pallas_call(
        functools.partial(near_kernel, width, count),
        in_specs=[pl.BlockSpec(memory_space=pltpu.SMEM)] * 2
        + [pl.BlockSpec(memory_space=pltpu.HBM), pl.BlockSpec(memory_space=pltpu.VMEM)],
        out_shape=[
            jax.ShapeDtypeStruct((length + MOD_ROWS * (r != 0), LANES), jnp.bfloat16)
            for r in range(count)
        ],
        scratch_shapes=[
            pltpu.VMEM((count, rows, (width // LANES + 1) * LANES), jnp.bfloat16),
            pltpu.SemaphoreType.DMA((count,)),
        ],
        compiler_params=pltpu.CompilerParams(vmem_limit_bytes=4 << 20),
        cost_estimate=pl.CostEstimate(
            flops=0, transcendentals=0, bytes_accessed=4 * rows * columns // halves
        ),
        name="split_near",
    )(*scalars[:2], pltpu.with_memory_space_constraint(x, pltpu.HBM), modulation)


def load_kernel(count, place_ref, w_ref, out_ref, sems):
    depth = w_ref.shape[0] // count

    def block(r):
        owner = place_ref[0] ^ r
        return pltpu.make_async_copy(
            w_ref.at[pl.ds(pl.multiple_of(owner * depth, depth), depth), :],
            out_ref.at[r * depth : (r + 1) * depth, :],
            sems.at[r],
        )

    for r in range(count):
        block(r).start()
    for r in range(count):
        block(r).wait()


def load_rows(weight, place, count):
    return pl.pallas_call(
        functools.partial(load_kernel, count),
        in_specs=[
            pl.BlockSpec(memory_space=pltpu.SMEM),
            pl.BlockSpec(memory_space=pltpu.HBM),
        ],
        out_specs=pl.BlockSpec(memory_space=pltpu.VMEM),
        out_shape=pltpu.VMEM(weight.shape, weight.dtype),
        scratch_shapes=[pltpu.SemaphoreType.DMA((count,))],
        compiler_params=pltpu.CompilerParams(vmem_limit_bytes=2 << 20),
        cost_estimate=pl.CostEstimate(
            flops=0, transcendentals=0, bytes_accessed=2 * weight.size * 2
        ),
        name="load_rows",
    )(place, pltpu.with_memory_space_constraint(weight, pltpu.HBM))


def attend_kernel(heads, rows, count, *refs):
    riders, ins, outs = refs[: -2 * count], refs[-2 * count : -count], refs[-count:]
    width = heads * 3 * HEAD
    blocks = [unpack_tiles(ref, rows, width) for ref in ins]

    def columns(start):
        first, offset = divmod(start, LANES)
        parts = []
        for tiles in blocks:
            if offset + HEAD <= LANES:
                parts.append(tiles[first][:, offset : offset + HEAD])
            else:
                wide = jnp.concatenate([tiles[first], tiles[first + 1]], axis=1)
                parts.append(wide[:, offset : offset + HEAD])
        return jnp.concatenate(parts, axis=0)

    results = []
    for h in range(heads):
        start = h * 3 * HEAD
        query, key, value = (columns(start + i * HEAD) for i in range(3))
        scores = lax.dot_general(
            query, key, (((1,), (1,)), ((), ())), preferred_element_type=jnp.float32
        )
        row_max = jnp.max(scores, axis=-1, keepdims=True)
        exp_scores = jnp.exp2((scores - row_max) * (HEAD ** (-0.5) / math.log(2.0)))
        row_sum = jnp.sum(exp_scores, axis=-1, keepdims=True)
        summed = jnp.dot(
            exp_scores.astype(jnp.bfloat16), value, preferred_element_type=jnp.float32
        )
        results.append(summed / row_sum)
    attended = jnp.concatenate(results, axis=1).astype(jnp.bfloat16)
    whole = heads * HEAD // LANES
    for b in range(count):
        mine = attended[b * rows : (b + 1) * rows]
        for t in range(whole):
            outs[b][t * rows : (t + 1) * rows, :] = mine[:, t * LANES : (t + 1) * LANES]
        rest = mine[:, whole * LANES :].astype(jnp.float32)
        packed = rows * heads * HEAD // LANES
        outs[b][whole * rows : packed, :] = jnp.concatenate(
            [rest[: rows // 2], rest[rows // 2 :]], axis=1
        ).astype(jnp.bfloat16)
        if riders:
            put_modulation(outs[b], packed, riders[0][1:2, :])


def attend_packed(pieces, heads, rows, riders=()):
    count = len(pieces)
    total = count * rows
    length = rows * heads * HEAD // LANES
    specs = [pl.BlockSpec(memory_space=pltpu.VMEM)] * (count + len(riders))
    if riders:
        length += MOD_ROWS
    out = jax.ShapeDtypeStruct((length, LANES), jnp.bfloat16)
    return pl.pallas_call(
        functools.partial(attend_kernel, heads, rows, count),
        in_specs=specs,
        out_shape=[out] * count,
        compiler_params=pltpu.CompilerParams(vmem_limit_bytes=12 << 20),
        cost_estimate=pl.CostEstimate(
            flops=4 * heads * total * total * HEAD,
            transcendentals=heads * total * total,
            bytes_accessed=8 * total * heads * HEAD,
        ),
        name="attend_packed",
    )(*riders, *pieces)


def gather_left(refs, left_ref, rows):
    depth = left_ref.shape[1] // len(refs)
    left_ref[...] = jnp.concatenate(
        [jnp.concatenate(unpack_tiles(ref, rows, depth), axis=1)[:, :depth] for ref in refs],
        axis=1,
    )


def project_kernel(rows, w_ref, *refs):
    pieces, out_ref, left_ref = refs[:-2], refs[-2], refs[-1]
    gather_left(pieces, left_ref, rows)
    for start in range(0, w_ref.shape[1], 512):
        cut = slice(start, start + 512)
        out_ref[:, cut] = jnp.dot(
            left_ref[...], w_ref[:, cut], preferred_element_type=jnp.float32
        ).astype(jnp.bfloat16)


def project_packed(pieces, weight, rows):
    depth, dim = weight.shape
    return pl.pallas_call(
        functools.partial(project_kernel, rows),
        out_shape=jax.ShapeDtypeStruct((rows, dim), jnp.bfloat16),
        scratch_shapes=[pltpu.VMEM((rows, depth), jnp.bfloat16)],
        compiler_params=pltpu.CompilerParams(vmem_limit_bytes=16 << 20),
        cost_estimate=pl.CostEstimate(
            flops=2 * rows * depth * dim, transcendentals=0, bytes_accessed=2 * depth * dim
        ),
        name="project_packed",
    )(pltpu.with_memory_space_constraint(weight, pltpu.VMEM), *pieces)


def finish_kernel(rows, count, w_ref, *refs):
    pieces, refs = refs[:count], refs[count:]
    mod_ref, far_ref, hidden_ref, head_ref, latent_ref, clock_ref = refs[:6]
    out_ref, step_ref, acc_ref, left_ref, turn_ref = refs[6:]
    steps, _, tile = acc_ref.shape
    dim = steps * tile

    def modulation(which, i):
        start = which * dim + i * tile
        line, offset = divmod(start, mod_ref.shape[2])
        return mod_ref[line, :, offset : offset + tile]

    gather_left(pieces, left_ref, rows)
    total = jnp.zeros((rows, 1), jnp.float32)
    for i in range(steps):
        cut = slice(i * tile, (i + 1) * tile)
        projected = jnp.dot(left_ref[...], w_ref[:, cut], preferred_element_type=jnp.float32)
        projected = projected + far_ref[:, cut].astype(jnp.float32)
        part = hidden_ref[:, cut].astype(jnp.float32) + modulation(0, i) * projected
        acc_ref[i] = part
        total += jnp.sum(part, axis=-1, keepdims=True)
    average = total / dim
    square = jnp.zeros((rows, 1), jnp.float32)
    for i in range(steps):
        centred = acc_ref[i] - average
        square += jnp.sum(centred * centred, axis=-1, keepdims=True)
    rate = lax.rsqrt(square / dim + 1e-06)
    velocity = jnp.zeros(turn_ref.shape, jnp.float32)
    for i in range(steps):
        cut = slice(i * tile, (i + 1) * tile)
        normed = (
            (acc_ref[i] - average) * rate * (1.0 + modulation(2, i)) + modulation(1, i)
        ).astype(jnp.bfloat16)
        velocity += lax.dot_general(
            normed,
            head_ref[:, cut],
            (((1,), (1,)), ((), ())),
            preferred_element_type=jnp.float32,
        )
    turn_ref[...] = velocity
    paired = jnp.concatenate(
        [turn_ref[pl.ds(0, rows // 2, stride=2), :], turn_ref[pl.ds(1, rows // 2, stride=2), :]],
        axis=1,
    )
    out_ref[...] = paired
    step_ref[...] = latent_ref[...] + clock_ref[1:2, :] * paired


def finish(pieces, weight, far, hidden, lines, head_rows, latent, clock, rows):
    depth, dim = weight.shape
    count = len(pieces)
    tile = math.gcd(dim, lines.shape[2])
    patch = head_rows.shape[0]
    inputs = (pltpu.with_memory_space_constraint(weight, pltpu.VMEM), *pieces, lines)
    inputs += (far, hidden, head_rows, latent, clock)
    result = jax.ShapeDtypeStruct((rows // 2, 2 * patch), jnp.float32)
    return pl.pallas_call(
        functools.partial(finish_kernel, rows, count),
        in_specs=[pl.BlockSpec(memory_space=pltpu.VMEM)] * len(inputs),
        out_shape=[result] * 2,
        scratch_shapes=[
            pltpu.VMEM((dim // tile, rows, tile), jnp.float32),
            pltpu.VMEM((rows, depth), jnp.bfloat16),
            pltpu.VMEM((rows, patch), jnp.float32),
        ],
        compiler_params=pltpu.CompilerParams(vmem_limit_bytes=16 << 20),
        cost_estimate=pl.CostEstimate(
            flops=2 * rows * depth * dim, transcendentals=0, bytes_accessed=2 * depth * dim
        ),
        name="finish",
    )(*inputs)


def collect_kernel(start, *refs):
    out_ref = refs[-1]
    span = out_ref.shape[0] // (len(refs) - 1)
    for r, ref in enumerate(refs[:-1]):
        at = ref.shape[0] - span if start is None or r == 0 else start
        out_ref[r * span : (r + 1) * span, :] = ref[at : at + span, :]


def collect(pieces, span, start=None):
    return pl.pallas_call(
        functools.partial(collect_kernel, start),
        in_specs=[pl.BlockSpec(memory_space=pltpu.VMEM)] * len(pieces),
        out_shape=jax.ShapeDtypeStruct((len(pieces) * span, LANES), jnp.bfloat16),
        compiler_params=pltpu.CompilerParams(vmem_limit_bytes=4 << 20),
        cost_estimate=pl.CostEstimate(
            flops=0, transcendentals=0, bytes_accessed=4 * len(pieces) * span * LANES
        ),
        name="collect",
    )(*pieces)


def arrange_kernel(count, width, packed, done, place_ref, half_ref, group_ref, *refs):
    mine_ref, up_ref, mod_ref = refs[:3]
    near, far = refs[3 : 3 + count], refs[3 + count : -2]
    head_out, mod_out = refs[-2:]
    span = mine_ref.shape[0] // (2 * count)
    cut = head_out.shape[0] // 2
    tiles = span // cut
    first = half_ref[0] == 0
    lower = group_ref[0] == 0
    columns = mod_ref.shape[1]

    def block(ref, k):
        parts = [ref[k * span + t * cut : k * span + (t + 1) * cut, :] for t in range(tiles)]
        return jnp.concatenate(parts, axis=1)[:, :width]

    def whole(k):
        mine, up = block(mine_ref, k), block(up_ref, k)
        return jnp.concatenate(
            [jnp.where(lower, mine, up), jnp.where(lower, up, mine)], axis=0
        )

    for r in range(count):
        owner = place_ref[0] ^ r
        own, other = whole(r), whole(count + r)
        start = pl.multiple_of(owner * 2 * width, LANES)
        head_out[:, pl.ds(start, 2 * width)] = jnp.concatenate(
            [jnp.where(first, own, other), jnp.where(first, other, own)], axis=1
        )
        own = mod_ref[0:1, :] if r == 0 else get_modulation(near[r], packed, columns)
        other = get_modulation(far[r], done, columns)
        mod_out[owner] = jnp.concatenate(
            [jnp.where(first, own, other), jnp.where(first, other, own)], axis=1
        )


def arrange(mine, up, modulation, near, far, head, scalars, packed, done):
    count = len(far)
    patch, width = head.shape
    columns = modulation.shape[1]
    return pl.pallas_call(
        functools.partial(arrange_kernel, count, width, packed, done),
        in_specs=[pl.BlockSpec(memory_space=pltpu.SMEM)] * 3
        + [pl.BlockSpec(memory_space=pltpu.VMEM)] * (3 + 2 * count),
        out_shape=[
            jax.ShapeDtypeStruct((patch, 2 * count * width), jnp.bfloat16),
            jax.ShapeDtypeStruct((count, 1, 2 * columns), jnp.float32),
        ],
        compiler_params=pltpu.CompilerParams(vmem_limit_bytes=4 << 20),
        cost_estimate=pl.CostEstimate(
            flops=0, transcendentals=0, bytes_accessed=8 * count * patch * width
        ),
        name="arrange",
    )(*scalars, mine, up, modulation, *near, *far)


def packed_body(head_inputs, hidden, out_weight, time_weight, head_weight, latent, timesteps):
    count = lax.axis_size("seq")
    halves = lax.axis_size("fsdp")
    rows = head_inputs.shape[2]
    place = lax.axis_index("seq")
    half = lax.axis_index("fsdp")
    group = lax.axis_index("grp")
    heads = HEADS // halves // count

    def along(block, r):
        return lax.ppermute(block, "seq", [(i, i ^ r) for i in range(count)])

    def swap(block, axis):
        return lax.ppermute(block, axis, [(0, 1), (1, 0)])

    def slanted(block, r):
        route = []
        for i in range(count):
            for j in range(halves):
                route.append((i * halves + j, (i ^ r) * halves + 1 - j))
        return lax.ppermute(block, ("seq", "fsdp"), route)

    x = head_inputs.reshape(rows, head_inputs.shape[3])
    head = jnp.swapaxes(head_weight[0], 0, 1)
    span = head.shape[0] // 2 * head_tiles(head.shape[1])
    here = place[None].astype(jnp.int32)
    side = half[None].astype(jnp.int32)
    level = group[None].astype(jnp.int32)
    scalars = (here, side, level)
    far_sent, pack, clock = split_far(x, head, timesteps.reshape(1, 2), scalars, count, halves)
    far_pieces = [far_sent[0]] + [along(far_sent[r], r) for r in range(1, count)]

    other_steps = swap(timesteps, "fsdp")
    freqs = jnp.exp(
        -math.log(10000.0) * jnp.arange(FREQ // 2, dtype=jnp.float32) / (FREQ // 2)
    )
    angle = jnp.concatenate([clock[:1], jnp.full((1, LANES), other_steps[0, 0, 0], jnp.float32)])
    angle = angle * freqs
    embedding = jnp.concatenate([jnp.cos(angle), jnp.sin(angle)], axis=-1).astype(jnp.bfloat16)
    modulation = jnp.dot(embedding, time_weight[0], preferred_element_type=jnp.float32)

    near_sent = split_near(x, modulation, scalars, count, halves)
    near_pieces = [near_sent[0]] + [along(near_sent[r], r) for r in range(1, count)]

    weight = load_rows(out_weight[0], here, count)
    far_attended = attend_packed(far_pieces, heads, rows, (modulation,))
    far_home = [slanted(far_attended[r], r) for r in range(count)]
    partial = project_packed(far_home, weight, rows)
    partial = swap(partial, "fsdp")

    packed = far_sent[0].shape[0]
    done = far_home[0].shape[0] - MOD_ROWS
    line = collect([pack] + far_pieces[1:], span, packed)
    other = swap(line, "fsdp")
    mine = collect([line, other], line.shape[0])
    up = swap(mine, "grp")
    head_rows, lines = arrange(
        mine, up, modulation, near_pieces, far_home, head, scalars, packed, done
    )

    near_attended = attend_packed(near_pieces, heads, rows)
    near_home = [near_attended[0]]
    near_home += [along(near_attended[r], r) for r in range(1, count)]
    velocity, stepped = finish(
        near_home,
        weight,
        partial,
        hidden.reshape(rows, DIM),
        lines,
        head_rows,
        latent.reshape(rows // 2, 2 * PATCH),
        clock,
        rows,
    )
    carried = partner(stepped, "section", 0)
    return (velocity.reshape(latent.shape), carried.reshape(latent.shape))


def packed_fits(mesh, head_shape):
    count, halves = mesh.shape["seq"], mesh.shape["fsdp"]
    rows = head_shape[2]
    return (
        head_shape[1] == 1
        and halves == 2
        and FREQ == 2 * LANES
        and 2 * PATCH == LANES
        and mesh.shape["grp"] == 2
        and count & (count - 1) == 0
        and HEADS % (halves * count) == 0
        and 3 * DIM // (halves * count) <= 8 * LANES
        and DIM % (halves * count) == 0
        and HEADS // (halves * count) * HEAD % LANES == LANES // 2
        and rows % 32 == 0
        and rows * count <= 512
    )


def step(mesh, body):
    return jax.shard_map(
        body,
        mesh=mesh,
        in_specs=(
            P("section", ("grp", "fsdp"), "seq", None),
            P("section", ("grp", "fsdp"), "seq", None),
            P("section", "fsdp", None),
            P("section", None, ("seq", "fsdp")),
            P("section", ("seq", "fsdp"), None),
            P("section", ("grp", "fsdp"), "seq", None),
            P("section", ("grp", "fsdp"), None),
        ),
        out_specs=(
            P("section", ("grp", "fsdp"), "seq", None),
            P("section", ("grp", "fsdp"), "seq", None),
        ),
        check_vma=False,
    )


def solution(mesh):
    def choose(head_inputs, *rest):
        local = (
            head_inputs.shape[0] // mesh.shape["section"],
            head_inputs.shape[1] // mesh.shape["grp"] // mesh.shape["fsdp"],
            head_inputs.shape[2] // mesh.shape["seq"],
        )
        if not packed_fits(mesh, local):
            return step(mesh, general_body)(head_inputs, *rest)
        return step(mesh, packed_body)(head_inputs, *rest)

    return choose
```

```python
import functools
import math

import jax
import jax.numpy as jnp
from jax import lax
from jax.experimental import pallas as pl
from jax.experimental.pallas import tpu as pltpu
from jax.sharding import PartitionSpec as P


DIM = 2560
HEADS = 32
HEAD = 80
PATCH = 64
FREQ = 256
LANES = 128


def partner(block, axis, apart):
    count = lax.axis_size(axis)
    route = []
    for low in range(count):
        high = low | 1 << apart
        if high != low and high < count:
            route += [(low, high), (high, low)]
    return lax.ppermute(block, axis, route)


def time_embed(steps_now):
    half = FREQ // 2
    freqs = jnp.exp(-math.log(10000.0) * jnp.arange(half, dtype=jnp.float32) / half)
    angle = steps_now.astype(jnp.float32)[..., None] * freqs
    return jnp.concatenate([jnp.cos(angle), jnp.sin(angle)], axis=-1)


def sigma_of(steps_now):
    unit_time = steps_now.astype(jnp.float32) / 1000.0
    return 5.0 * unit_time / (1.0 + 4.0 * unit_time)


def attend(exchanged):
    items = exchanged.shape[0]
    length = exchanged.shape[1]
    local_heads = exchanged.shape[2]
    query_all = exchanged[..., :HEAD]
    key_rows = exchanged[..., HEAD : 2 * HEAD]
    value_rows = exchanged[..., 2 * HEAD :]
    block_rows = min(512, length)
    block_count = length // block_rows

    def one_block(block_index):
        query_block = lax.dynamic_slice_in_dim(query_all, block_index * block_rows, block_rows, 1)
        scores = jnp.einsum(
            "nqhe,nkhe->nhqk", query_block, key_rows, preferred_element_type=jnp.float32
        ) * HEAD ** (-0.5)
        row_max = jnp.max(scores, axis=-1, keepdims=True)
        exp_scores = jnp.exp(scores - row_max)
        row_sum = jnp.sum(exp_scores, axis=-1, keepdims=True)
        weights = (exp_scores / row_sum).astype(jnp.bfloat16)
        return jnp.einsum(
            "nhqk,nkhe->nqhe", weights, value_rows, preferred_element_type=jnp.float32
        ).astype(jnp.bfloat16)

    blocks = lax.map(one_block, jnp.arange(block_count, dtype=jnp.int32))
    return blocks.transpose(1, 0, 2, 3, 4).reshape(items, length, local_heads * HEAD)


def general_body(head_inputs, hidden, out_weight, time_weight, head_weight, latent, timesteps):
    samples = head_inputs.shape[1]
    row_count = head_inputs.shape[2]
    flat_count = samples * row_count
    local = head_inputs.reshape(samples, row_count, HEADS, 3 * HEAD)
    attended = lax.all_to_all(
        attend(lax.all_to_all(local, "seq", split_axis=2, concat_axis=1, tiled=True)),
        "seq",
        split_axis=1,
        concat_axis=2,
        tiled=True,
    )
    flattened = attended.reshape(flat_count, HEADS * HEAD)
    time_full, head_full = (
        lax.all_gather(time_weight, ("seq", "fsdp"), axis=2, tiled=True),
        lax.all_gather(head_weight, ("seq", "fsdp"), axis=1, tiled=True),
    )
    embedding = time_embed(timesteps[0, :, 0]).astype(jnp.bfloat16)
    modulation = jnp.dot(embedding, time_full[0], preferred_element_type=jnp.float32)
    gate_term = modulation[:, None, :DIM]
    shift_term = modulation[:, None, DIM : 2 * DIM]
    scale_term = modulation[:, None, 2 * DIM :]
    own_columns = lax.all_to_all(flattened, "fsdp", split_axis=1, concat_axis=0, tiled=True)
    projected = lax.psum_scatter(
        jnp.dot(own_columns, out_weight[0], preferred_element_type=jnp.float32).astype(
            jnp.bfloat16
        ),
        "fsdp",
        scatter_dimension=0,
        tiled=True,
    ).astype(jnp.float32)
    updated = hidden.reshape(samples, row_count, DIM).astype(
        jnp.float32
    ) + gate_term * projected.reshape(samples, row_count, DIM)
    average = jnp.mean(updated, axis=-1, keepdims=True)
    centred = updated - average
    variance = jnp.mean(centred * centred, axis=-1, keepdims=True)
    normed = (centred * lax.rsqrt(variance + 1e-06) * (1.0 + scale_term) + shift_term).astype(
        jnp.bfloat16
    )
    velocity = jnp.dot(
        normed.reshape(flat_count, DIM), head_full[0], preferred_element_type=jnp.float32
    )
    velocity = velocity.reshape(1, samples, row_count // 2, 2 * PATCH)
    step_size = sigma_of(timesteps[0, :, 1]) - sigma_of(timesteps[0, :, 0])
    stepped = latent + step_size[None, :, None, None] * velocity
    carried = partner(stepped, "section", 0)
    return (velocity, carried)


def turn(half):
    return pltpu.roll(half.astype(jnp.float32), LANES // 2, 1)


def pack_half(tile):
    rows = tile.shape[0]
    wide = tile.astype(jnp.float32)
    lane = lax.broadcasted_iota(jnp.int32, (rows // 2, LANES), 1)
    return jnp.where(
        lane < LANES // 2, wide[: rows // 2], pltpu.roll(wide[rows // 2 :], LANES // 2, 1)
    ).astype(jnp.bfloat16)


def unpack_tiles(ref, rows, width):
    whole = width // LANES
    tiles = [ref[t * rows : (t + 1) * rows, :] for t in range(whole)]
    last = ref[whole * rows : whole * rows + rows // 2, :]
    tiles.append(jnp.concatenate([last, turn(last).astype(jnp.bfloat16)], axis=0))
    return tiles


def head_tiles(width):
    return -(-width // LANES)


MOD_ROWS = 16


def put_modulation(out, at, row):
    width = row.shape[1]
    tiles = -(-width // LANES)
    left = jnp.concatenate([row, jnp.zeros((1, tiles * LANES - width), jnp.float32)], axis=1)
    left = jnp.concatenate(
        [left[:, t * LANES : (t + 1) * LANES] for t in range(tiles)]
        + [jnp.zeros((8 - tiles, LANES), jnp.float32)][: 8 - tiles],
        axis=0,
    )
    high = left.astype(jnp.bfloat16)
    low = (left - high.astype(jnp.float32)).astype(jnp.bfloat16)
    out[at : at + MOD_ROWS, :] = jnp.concatenate([high, low], axis=0)


def get_modulation(ref, at, width):
    terms = ref[at : at + MOD_ROWS, :].astype(jnp.float32)
    total = terms[0:8] + terms[8:16]
    tiles = -(-width // LANES)
    return jnp.concatenate([total[t : t + 1] for t in range(tiles)], axis=1)[:, :width]


def cut_window(width, held, out, r, odd):
    rows = held.shape[1]
    whole = width // LANES
    last = slice(whole * rows, rows * width // LANES)

    @pl.when(jnp.logical_not(odd))
    def _():
        for t in range(whole):
            out[t * rows : (t + 1) * rows, :] = held[r, :, t * LANES : (t + 1) * LANES]
        out[last, :] = pack_half(held[r, :, whole * LANES :])

    @pl.when(odd)
    def _():
        lane = lax.broadcasted_iota(jnp.int32, (rows, LANES), 1)
        turned = [turn(held[r, :, t * LANES : (t + 1) * LANES]) for t in range(whole + 1)]
        for t in range(whole):
            out[t * rows : (t + 1) * rows, :] = jnp.where(
                lane < LANES // 2, turned[t], turned[t + 1]
            ).astype(jnp.bfloat16)
        out[last, :] = pack_half(turned[whole])


def windows(x_ref, held, sems, me, half, count, width, slots):
    span = held.shape[2]

    def window(k, r):
        start = half * (count * width) + lax.div((me ^ r) * width, LANES) * LANES
        return pltpu.make_async_copy(
            x_ref.at[:, pl.ds(pl.multiple_of(start, LANES), span)], held.at[k], sems.at[k]
        )

    return [window(k, r) for k, r in enumerate(slots)]


def sigma_row(step):
    unit_time = jnp.full((1, LANES), step, jnp.int32).astype(jnp.float32) / 1000.0
    return 5.0 * unit_time / (1.0 + 4.0 * unit_time)


def first_kernel(width, count, slot, place_ref, half_ref, group_ref, x_ref, head_ref, *refs):
    out_ref, pack_ref, held, head_held, sems, head_sem = refs
    me = place_ref[0]
    cut, columns = head_held.shape
    copy = windows(x_ref, held, sems, me, 1 - half_ref[0], count, width, [slot])[0]
    head_copy = pltpu.make_async_copy(
        head_ref.at[pl.ds(pl.multiple_of(group_ref[0] * cut, cut), cut), :], head_held, head_sem
    )
    head_copy.start()
    copy.start()
    head_copy.wait()
    packed = out_ref.shape[0] - pack_ref.shape[0]
    for t in range(head_tiles(columns)):
        tile = head_held[:, t * LANES : min((t + 1) * LANES, columns)]
        if tile.shape[1] < LANES:
            fill = jnp.zeros((cut, LANES - tile.shape[1]), tile.dtype)
            tile = jnp.concatenate([tile, fill], axis=1)
        pack_ref[t * cut : (t + 1) * cut, :] = tile
        out_ref[packed + t * cut : packed + (t + 1) * cut, :] = tile
    copy.wait()
    cut_window(width, held, out_ref, 0, lax.rem(me ^ slot, 2) == 1)


def split_first(x, head, scalars, slot, count, halves):
    rows, columns = x.shape
    width = columns // halves // count
    cut = head.shape[0] // 2
    span = cut * head_tiles(head.shape[1])
    length = rows * width // LANES
    return pl.pallas_call(
        functools.partial(first_kernel, width, count, slot),
        in_specs=[pl.BlockSpec(memory_space=pltpu.SMEM)] * 3
        + [pl.BlockSpec(memory_space=pltpu.HBM)] * 2,
        out_shape=[
            jax.ShapeDtypeStruct((length + span, LANES), jnp.bfloat16),
            jax.ShapeDtypeStruct((span, LANES), jnp.bfloat16),
        ],
        scratch_shapes=[
            pltpu.VMEM((1, rows, (width // LANES + 1) * LANES), jnp.bfloat16),
            pltpu.VMEM((cut, head.shape[1]), jnp.bfloat16),
            pltpu.SemaphoreType.DMA((1,)),
            pltpu.SemaphoreType.DMA,
        ],
        compiler_params=pltpu.CompilerParams(vmem_limit_bytes=4 << 20),
        cost_estimate=pl.CostEstimate(
            flops=0, transcendentals=0, bytes_accessed=4 * rows * width
        ),
        name="split_first",
    )(
        *scalars,
        pltpu.with_memory_space_constraint(x, pltpu.HBM),
        pltpu.with_memory_space_constraint(head, pltpu.HBM),
    )


def far_kernel(width, count, slots, place_ref, half_ref, when_ref, x_ref, pack_ref, *refs):
    outs, (clock_ref, held, steps_ref, sems, steps_sem) = refs[: len(slots)], refs[len(slots) :]
    me = place_ref[0]
    copies = windows(x_ref, held, sems, me, 1 - half_ref[0], count, width, slots)
    steps_copy = pltpu.make_async_copy(when_ref, steps_ref, steps_sem)
    for copy in copies:
        copy.start()
    steps_copy.start()
    packed = held.shape[1] * width // LANES
    for out in outs:
        out[packed:, :] = pack_ref[...]
    for k, r in enumerate(slots):
        copies[k].wait()
        cut_window(width, held, outs[k], k, lax.rem(me ^ r, 2) == 1)
    steps_copy.wait()
    now = jnp.full((1, LANES), steps_ref[0, 0], jnp.int32).astype(jnp.float32)
    change = sigma_row(steps_ref[0, 1]) - sigma_row(steps_ref[0, 0])
    clock_ref[...] = jnp.concatenate([now, change])


def split_far(x, pack, steps, scalars, slots, count, halves):
    rows, columns = x.shape
    width = columns // halves // count
    length = rows * width // LANES
    results = pl.pallas_call(
        functools.partial(far_kernel, width, count, slots),
        in_specs=[pl.BlockSpec(memory_space=pltpu.SMEM)] * 2
        + [pl.BlockSpec(memory_space=pltpu.HBM)] * 2
        + [pl.BlockSpec(memory_space=pltpu.VMEM)],
        out_shape=[
            jax.ShapeDtypeStruct((length + pack.shape[0], LANES), jnp.bfloat16)
            for _ in slots
        ]
        + [jax.ShapeDtypeStruct((2, LANES), jnp.float32)],
        scratch_shapes=[
            pltpu.VMEM((len(slots), rows, (width // LANES + 1) * LANES), jnp.bfloat16),
            pltpu.SMEM((1, 2), jnp.int32),
            pltpu.SemaphoreType.DMA((len(slots),)),
            pltpu.SemaphoreType.DMA,
        ],
        compiler_params=pltpu.CompilerParams(vmem_limit_bytes=4 << 20),
        cost_estimate=pl.CostEstimate(
            flops=0, transcendentals=0, bytes_accessed=4 * rows * columns // halves
        ),
        name="split_far",
    )(
        *scalars[:2],
        pltpu.with_memory_space_constraint(steps, pltpu.HBM),
        pltpu.with_memory_space_constraint(x, pltpu.HBM),
        pack,
    )
    return results[:-1], results[-1]


def near_kernel(width, count, place_ref, half_ref, x_ref, *refs):
    outs, held, sems = refs[:count], refs[count], refs[count + 1]
    me = place_ref[0]
    copies = windows(x_ref, held, sems, me, half_ref[0], count, width, range(count))
    for r in range(count - 1, -1, -1):
        copies[r].start()
    for r in range(count - 1, -1, -1):
        copies[r].wait()
        cut_window(width, held, outs[r], r, lax.rem(me ^ r, 2) == 1)


def split_near(x, scalars, count, halves):
    rows, columns = x.shape
    width = columns // halves // count
    length = rows * width // LANES
    return pl.pallas_call(
        functools.partial(near_kernel, width, count),
        in_specs=[pl.BlockSpec(memory_space=pltpu.SMEM)] * 2
        + [pl.BlockSpec(memory_space=pltpu.HBM)],
        out_shape=[jax.ShapeDtypeStruct((length, LANES), jnp.bfloat16)] * count,
        scratch_shapes=[
            pltpu.VMEM((count, rows, (width // LANES + 1) * LANES), jnp.bfloat16),
            pltpu.SemaphoreType.DMA((count,)),
        ],
        compiler_params=pltpu.CompilerParams(vmem_limit_bytes=4 << 20),
        cost_estimate=pl.CostEstimate(
            flops=0, transcendentals=0, bytes_accessed=4 * rows * columns // halves
        ),
        name="split_near",
    )(*scalars[:2], pltpu.with_memory_space_constraint(x, pltpu.HBM))


def load_kernel(count, place_ref, w_ref, out_ref, sems):
    depth = w_ref.shape[0] // count

    def block(r):
        owner = place_ref[0] ^ r
        return pltpu.make_async_copy(
            w_ref.at[pl.ds(pl.multiple_of(owner * depth, depth), depth), :],
            out_ref.at[r * depth : (r + 1) * depth, :],
            sems.at[r],
        )

    for r in range(count):
        block(r).start()
    for r in range(count):
        block(r).wait()


def load_rows(weight, place, count):
    return pl.pallas_call(
        functools.partial(load_kernel, count),
        in_specs=[
            pl.BlockSpec(memory_space=pltpu.SMEM),
            pl.BlockSpec(memory_space=pltpu.HBM),
        ],
        out_specs=pl.BlockSpec(memory_space=pltpu.VMEM),
        out_shape=pltpu.VMEM(weight.shape, weight.dtype),
        scratch_shapes=[pltpu.SemaphoreType.DMA((count,))],
        compiler_params=pltpu.CompilerParams(vmem_limit_bytes=2 << 20),
        cost_estimate=pl.CostEstimate(
            flops=0, transcendentals=0, bytes_accessed=2 * weight.size * 2
        ),
        name="load_rows",
    )(place, pltpu.with_memory_space_constraint(weight, pltpu.HBM))


def attend_kernel(heads, rows, count, *refs):
    riders, ins, outs = refs[: -2 * count], refs[-2 * count : -count], refs[-count:]
    width = heads * 3 * HEAD
    blocks = [unpack_tiles(ref, rows, width) for ref in ins]

    def columns(start):
        first, offset = divmod(start, LANES)
        parts = []
        for tiles in blocks:
            if offset + HEAD <= LANES:
                parts.append(tiles[first][:, offset : offset + HEAD])
            else:
                wide = jnp.concatenate([tiles[first], tiles[first + 1]], axis=1)
                parts.append(wide[:, offset : offset + HEAD])
        return jnp.concatenate(parts, axis=0)

    results = []
    for h in range(heads):
        start = h * 3 * HEAD
        query, key, value = (columns(start + i * HEAD) for i in range(3))
        scores = lax.dot_general(
            query, key, (((1,), (1,)), ((), ())), preferred_element_type=jnp.float32
        )
        row_max = jnp.max(scores, axis=-1, keepdims=True)
        exp_scores = jnp.exp2((scores - row_max) * (HEAD ** (-0.5) / math.log(2.0)))
        row_sum = jnp.sum(exp_scores, axis=-1, keepdims=True)
        summed = jnp.dot(
            exp_scores.astype(jnp.bfloat16), value, preferred_element_type=jnp.float32
        )
        results.append(summed / row_sum)
    attended = jnp.concatenate(results, axis=1).astype(jnp.bfloat16)
    whole = heads * HEAD // LANES
    for b in range(count):
        mine = attended[b * rows : (b + 1) * rows]
        for t in range(whole):
            outs[b][t * rows : (t + 1) * rows, :] = mine[:, t * LANES : (t + 1) * LANES]
        rest = mine[:, whole * LANES :].astype(jnp.float32)
        packed = rows * heads * HEAD // LANES
        outs[b][whole * rows : packed, :] = jnp.concatenate(
            [rest[: rows // 2], rest[rows // 2 :]], axis=1
        ).astype(jnp.bfloat16)
        if riders:
            for k, rider in enumerate(riders):
                put_modulation(outs[b], packed + k * MOD_ROWS, rider[0:1, :])


def attend_packed(pieces, heads, rows, riders=()):
    count = len(pieces)
    total = count * rows
    length = rows * heads * HEAD // LANES
    specs = [pl.BlockSpec(memory_space=pltpu.VMEM)] * (count + len(riders))
    if riders:
        length += MOD_ROWS * len(riders)
    out = jax.ShapeDtypeStruct((length, LANES), jnp.bfloat16)
    return pl.pallas_call(
        functools.partial(attend_kernel, heads, rows, count),
        in_specs=specs,
        out_shape=[out] * count,
        compiler_params=pltpu.CompilerParams(vmem_limit_bytes=12 << 20),
        cost_estimate=pl.CostEstimate(
            flops=4 * heads * total * total * HEAD,
            transcendentals=heads * total * total,
            bytes_accessed=8 * total * heads * HEAD,
        ),
        name="attend_packed",
    )(*riders, *pieces)


def gather_left(refs, left_ref, rows):
    depth = left_ref.shape[1] // len(refs)
    left_ref[...] = jnp.concatenate(
        [jnp.concatenate(unpack_tiles(ref, rows, depth), axis=1)[:, :depth] for ref in refs],
        axis=1,
    )


def project_kernel(rows, first, w_ref, *refs):
    pieces, out_ref, left_ref = refs[:-2], refs[-2], refs[-1]
    gather_left(pieces, left_ref, rows)
    tile = math.gcd(out_ref.shape[1], 5 * LANES)
    for start in range(0, out_ref.shape[1], tile):
        out_ref[:, start : start + tile] = jnp.dot(
            left_ref[...],
            w_ref[:, first + start : first + start + tile],
            preferred_element_type=jnp.float32,
        ).astype(out_ref.dtype)


def project_packed(pieces, weight, rows, first, dim, dtype):
    depth = weight.shape[0]
    return pl.pallas_call(
        functools.partial(project_kernel, rows, first),
        out_shape=jax.ShapeDtypeStruct((rows, dim), dtype),
        scratch_shapes=[pltpu.VMEM((rows, depth), jnp.bfloat16)],
        compiler_params=pltpu.CompilerParams(vmem_limit_bytes=16 << 20),
        cost_estimate=pl.CostEstimate(
            flops=2 * rows * depth * dim, transcendentals=0, bytes_accessed=2 * depth * dim
        ),
        name="project_packed",
    )(pltpu.with_memory_space_constraint(weight, pltpu.VMEM), *pieces)


def finish_kernel(rows, near_ref, *refs):
    far, refs = refs[:2], refs[2:]
    mod_ref, hidden_ref, head_ref, latent_ref, clock_ref, out_ref, step_ref = refs[:7]
    acc_ref, turn_ref = refs[7:]
    steps, _, tile = acc_ref.shape
    dim = steps * tile

    def modulation(which, i):
        start = which * dim + i * tile
        line, offset = divmod(start, mod_ref.shape[2])
        return mod_ref[line, :, offset : offset + tile]

    total = jnp.zeros((rows, 1), jnp.float32)
    for i in range(steps):
        cut = slice(i * tile, (i + 1) * tile)
        side, offset = divmod(i * tile, dim // 2)
        projected = near_ref[:, cut] + far[side][:, offset : offset + tile].astype(jnp.float32)
        part = hidden_ref[:, cut].astype(jnp.float32) + modulation(0, i) * projected
        acc_ref[i] = part
        total += jnp.sum(part, axis=-1, keepdims=True)
    average = total / dim
    square = jnp.zeros((rows, 1), jnp.float32)
    for i in range(steps):
        centred = acc_ref[i] - average
        square += jnp.sum(centred * centred, axis=-1, keepdims=True)
    rate = lax.rsqrt(square / dim + 1e-06)
    velocity = jnp.zeros(turn_ref.shape, jnp.float32)
    for i in range(steps):
        cut = slice(i * tile, (i + 1) * tile)
        normed = (
            (acc_ref[i] - average) * rate * (1.0 + modulation(2, i)) + modulation(1, i)
        ).astype(jnp.bfloat16)
        velocity += lax.dot_general(
            normed,
            head_ref[:, cut],
            (((1,), (1,)), ((), ())),
            preferred_element_type=jnp.float32,
        )
    turn_ref[...] = velocity
    paired = jnp.concatenate(
        [turn_ref[pl.ds(0, rows // 2, stride=2), :], turn_ref[pl.ds(1, rows // 2, stride=2), :]],
        axis=1,
    )
    out_ref[...] = paired
    step_ref[...] = latent_ref[...] + clock_ref[1:2, :] * paired


def finish(near, far, hidden, lines, head_rows, latent, clock):
    rows, dim = near.shape
    tile = math.gcd(dim // 2, lines.shape[2])
    patch = head_rows.shape[0]
    inputs = (near, *far, lines, hidden, head_rows, latent, clock)
    result = jax.ShapeDtypeStruct((rows // 2, 2 * patch), jnp.float32)
    return pl.pallas_call(
        functools.partial(finish_kernel, rows),
        in_specs=[pl.BlockSpec(memory_space=pltpu.VMEM)] * len(inputs),
        out_shape=[result] * 2,
        scratch_shapes=[
            pltpu.VMEM((dim // tile, rows, tile), jnp.float32),
            pltpu.VMEM((rows, patch), jnp.float32),
        ],
        compiler_params=pltpu.CompilerParams(vmem_limit_bytes=8 << 20),
        cost_estimate=pl.CostEstimate(
            flops=2 * rows * patch * dim, transcendentals=0, bytes_accessed=8 * rows * dim
        ),
        name="finish",
    )(*inputs)


def collect_kernel(start, *refs):
    out_ref = refs[-1]
    span = out_ref.shape[0] // (len(refs) - 1)
    for r, ref in enumerate(refs[:-1]):
        out_ref[r * span : (r + 1) * span, :] = ref[start : start + span, :]


def collect(pieces, span, start):
    return pl.pallas_call(
        functools.partial(collect_kernel, start),
        in_specs=[pl.BlockSpec(memory_space=pltpu.VMEM)] * len(pieces),
        out_shape=jax.ShapeDtypeStruct((len(pieces) * span, LANES), jnp.bfloat16),
        compiler_params=pltpu.CompilerParams(vmem_limit_bytes=4 << 20),
        cost_estimate=pl.CostEstimate(
            flops=0, transcendentals=0, bytes_accessed=4 * len(pieces) * span * LANES
        ),
        name="collect",
    )(*pieces)


def arrange_kernel(count, width, done, place_ref, half_ref, group_ref, *refs):
    mine_ref, up_ref, mod_ref, mate_ref = refs[:4]
    far = refs[4:-2]
    head_out, mod_out = refs[-2:]
    span = mine_ref.shape[0] // (2 * count)
    cut = head_out.shape[0] // 2
    tiles = span // cut
    first = half_ref[0] == 0
    lower = group_ref[0] == 0
    columns = mod_ref.shape[1]

    def block(ref, k):
        parts = [ref[k * span + t * cut : k * span + (t + 1) * cut, :] for t in range(tiles)]
        return jnp.concatenate(parts, axis=1)[:, :width]

    def whole(k):
        mine, up = block(mine_ref, k), block(up_ref, k)
        return jnp.concatenate(
            [jnp.where(lower, mine, up), jnp.where(lower, up, mine)], axis=0
        )

    for r in range(count):
        owner = place_ref[0] ^ r
        own, other = whole(r), whole(count + r)
        start = pl.multiple_of(owner * 2 * width, LANES)
        head_out[:, pl.ds(start, 2 * width)] = jnp.concatenate(
            [jnp.where(first, own, other), jnp.where(first, other, own)], axis=1
        )
        if r == 0:
            own, other = mod_ref[0:1, :], mate_ref[...]
        else:
            own = get_modulation(far[r], done, columns)
            other = get_modulation(far[r], done + MOD_ROWS, columns)
        mod_out[owner] = jnp.concatenate(
            [jnp.where(first, own, other), jnp.where(first, other, own)], axis=1
        )


def arrange(mine, up, modulation, mate, far, head, scalars, done):
    count = len(far)
    patch, width = head.shape
    columns = modulation.shape[1]
    return pl.pallas_call(
        functools.partial(arrange_kernel, count, width, done),
        in_specs=[pl.BlockSpec(memory_space=pltpu.SMEM)] * 3
        + [pl.BlockSpec(memory_space=pltpu.VMEM)] * (4 + count),
        out_shape=[
            jax.ShapeDtypeStruct((patch, 2 * count * width), jnp.bfloat16),
            jax.ShapeDtypeStruct((count, 1, 2 * columns), jnp.float32),
        ],
        compiler_params=pltpu.CompilerParams(vmem_limit_bytes=4 << 20),
        cost_estimate=pl.CostEstimate(
            flops=0, transcendentals=0, bytes_accessed=8 * count * patch * width
        ),
        name="arrange",
    )(*scalars, mine, up, modulation, mate, *far)


def packed_body(head_inputs, hidden, out_weight, time_weight, head_weight, latent, timesteps):
    count = lax.axis_size("seq")
    halves = lax.axis_size("fsdp")
    rows = head_inputs.shape[2]
    place = lax.axis_index("seq")
    half = lax.axis_index("fsdp")
    group = lax.axis_index("grp")
    heads = HEADS // halves // count

    def along(block, r):
        return lax.ppermute(block, "seq", [(i, i ^ r) for i in range(count)])

    def swap(block, axis):
        return lax.ppermute(block, axis, [(0, 1), (1, 0)])

    def slanted(block, r):
        route = []
        for i in range(count):
            for j in range(halves):
                route.append((i * halves + j, (i ^ r) * halves + 1 - j))
        return lax.ppermute(block, ("seq", "fsdp"), route)

    x = head_inputs.reshape(rows, head_inputs.shape[3])
    head = jnp.swapaxes(head_weight[0], 0, 1)
    span = head.shape[0] // 2 * head_tiles(head.shape[1])
    here = place[None].astype(jnp.int32)
    side = half[None].astype(jnp.int32)
    level = group[None].astype(jnp.int32)
    scalars = (here, side, level)
    last = count // 2
    slots = [r for r in range(count - 1, 0, -1) if r != last] + [0]
    first, pack = split_first(x, head, scalars, last, count, halves)
    sent, clock = split_far(x, pack, timesteps.reshape(1, 2), scalars, slots, count, halves)
    far_sent = [first if r == last else sent[slots.index(r)] for r in range(count)]
    far_pieces = [slanted(far_sent[r], r) for r in range(count)]

    other_steps = swap(timesteps, "fsdp")
    freqs = jnp.exp(
        -math.log(10000.0) * jnp.arange(FREQ // 2, dtype=jnp.float32) / (FREQ // 2)
    )
    angle = jnp.concatenate([clock[:1], jnp.full((1, LANES), other_steps[0, 0, 0], jnp.float32)])
    angle = angle * freqs
    embedding = jnp.concatenate([jnp.cos(angle), jnp.sin(angle)], axis=-1).astype(jnp.bfloat16)
    modulation = jnp.dot(embedding, time_weight[0], preferred_element_type=jnp.float32)
    mate = swap(modulation[1:], "fsdp")

    near_sent = split_near(x, scalars, count, halves)
    near_pieces = [near_sent[0]] + [along(near_sent[r], r) for r in range(1, count)]

    weight = load_rows(out_weight[0], here, count)
    far_attended = attend_packed(far_pieces, heads, rows, (modulation, mate))
    far_home = [far_attended[0]]
    far_home += [along(far_attended[r], r) for r in range(1, count)]
    part = DIM // 2
    partial = []
    for k in range(2):
        term = project_packed(far_home, weight, rows, k * part, part, jnp.bfloat16)
        partial.append(swap(term, "fsdp"))

    packed = near_sent[0].shape[0]
    done = far_home[0].shape[0] - 2 * MOD_ROWS
    line = collect(far_pieces, span, packed)
    other = swap(line, "fsdp")
    mine = collect([other, line], line.shape[0], 0)
    up = swap(mine, "grp")
    head_rows, lines = arrange(
        mine, up, modulation, mate, far_home, head, scalars, done
    )

    near_attended = attend_packed(near_pieces, heads, rows)
    near_home = [near_attended[0]]
    near_home += [along(near_attended[r], r) for r in range(1, count)]
    projected = project_packed(near_home, weight, rows, 0, DIM, jnp.float32)
    velocity, stepped = finish(
        projected,
        partial,
        hidden.reshape(rows, DIM),
        lines,
        head_rows,
        latent.reshape(rows // 2, 2 * PATCH),
        clock,
    )
    carried = partner(stepped, "section", 0)
    return (velocity.reshape(latent.shape), carried.reshape(latent.shape))


def packed_fits(mesh, head_shape):
    count, halves = mesh.shape["seq"], mesh.shape["fsdp"]
    rows = head_shape[2]
    return (
        head_shape[1] == 1
        and halves == 2
        and FREQ == 2 * LANES
        and 2 * PATCH == LANES
        and mesh.shape["grp"] == 2
        and count & (count - 1) == 0
        and HEADS % (halves * count) == 0
        and 3 * DIM // (halves * count) <= 8 * LANES
        and DIM % (halves * count) == 0
        and HEADS // (halves * count) * HEAD % LANES == LANES // 2
        and rows % 32 == 0
        and rows * count <= 512
    )


def step(mesh, body):
    return jax.shard_map(
        body,
        mesh=mesh,
        in_specs=(
            P("section", ("grp", "fsdp"), "seq", None),
            P("section", ("grp", "fsdp"), "seq", None),
            P("section", "fsdp", None),
            P("section", None, ("seq", "fsdp")),
            P("section", ("seq", "fsdp"), None),
            P("section", ("grp", "fsdp"), "seq", None),
            P("section", ("grp", "fsdp"), None),
        ),
        out_specs=(
            P("section", ("grp", "fsdp"), "seq", None),
            P("section", ("grp", "fsdp"), "seq", None),
        ),
        check_vma=False,
    )


def solution(mesh):
    def choose(head_inputs, *rest):
        local = (
            head_inputs.shape[0] // mesh.shape["section"],
            head_inputs.shape[1] // mesh.shape["grp"] // mesh.shape["fsdp"],
            head_inputs.shape[2] // mesh.shape["seq"],
        )
        if not packed_fits(mesh, local):
            return step(mesh, general_body)(head_inputs, *rest)
        return step(mesh, packed_body)(head_inputs, *rest)

    return choose
```

```python
import functools
import math

import jax
import jax.numpy as jnp
from jax import lax
from jax.experimental import pallas as pl
from jax.experimental.pallas import tpu as pltpu
from jax.sharding import PartitionSpec as P


DIM = 2560
HEADS = 32
HEAD = 80
PATCH = 64
FREQ = 256
LANES = 128


def partner(block, axis, apart):
    count = lax.axis_size(axis)
    route = []
    for low in range(count):
        high = low | 1 << apart
        if high != low and high < count:
            route += [(low, high), (high, low)]
    return lax.ppermute(block, axis, route)


def time_embed(steps_now):
    half = FREQ // 2
    freqs = jnp.exp(-math.log(10000.0) * jnp.arange(half, dtype=jnp.float32) / half)
    angle = steps_now.astype(jnp.float32)[..., None] * freqs
    return jnp.concatenate([jnp.cos(angle), jnp.sin(angle)], axis=-1)


def sigma_of(steps_now):
    unit_time = steps_now.astype(jnp.float32) / 1000.0
    return 5.0 * unit_time / (1.0 + 4.0 * unit_time)


def attend(exchanged):
    items = exchanged.shape[0]
    length = exchanged.shape[1]
    local_heads = exchanged.shape[2]
    query_all = exchanged[..., :HEAD]
    key_rows = exchanged[..., HEAD : 2 * HEAD]
    value_rows = exchanged[..., 2 * HEAD :]
    block_rows = min(512, length)
    block_count = length // block_rows

    def one_block(block_index):
        query_block = lax.dynamic_slice_in_dim(query_all, block_index * block_rows, block_rows, 1)
        scores = jnp.einsum(
            "nqhe,nkhe->nhqk", query_block, key_rows, preferred_element_type=jnp.float32
        ) * HEAD ** (-0.5)
        row_max = jnp.max(scores, axis=-1, keepdims=True)
        exp_scores = jnp.exp(scores - row_max)
        row_sum = jnp.sum(exp_scores, axis=-1, keepdims=True)
        weights = (exp_scores / row_sum).astype(jnp.bfloat16)
        return jnp.einsum(
            "nhqk,nkhe->nqhe", weights, value_rows, preferred_element_type=jnp.float32
        ).astype(jnp.bfloat16)

    blocks = lax.map(one_block, jnp.arange(block_count, dtype=jnp.int32))
    return blocks.transpose(1, 0, 2, 3, 4).reshape(items, length, local_heads * HEAD)


def general_body(head_inputs, hidden, out_weight, time_weight, head_weight, latent, timesteps):
    samples = head_inputs.shape[1]
    row_count = head_inputs.shape[2]
    flat_count = samples * row_count
    local = head_inputs.reshape(samples, row_count, HEADS, 3 * HEAD)
    attended = lax.all_to_all(
        attend(lax.all_to_all(local, "seq", split_axis=2, concat_axis=1, tiled=True)),
        "seq",
        split_axis=1,
        concat_axis=2,
        tiled=True,
    )
    flattened = attended.reshape(flat_count, HEADS * HEAD)
    time_full, head_full = (
        lax.all_gather(time_weight, ("seq", "fsdp"), axis=2, tiled=True),
        lax.all_gather(head_weight, ("seq", "fsdp"), axis=1, tiled=True),
    )
    embedding = time_embed(timesteps[0, :, 0]).astype(jnp.bfloat16)
    modulation = jnp.dot(embedding, time_full[0], preferred_element_type=jnp.float32)
    gate_term = modulation[:, None, :DIM]
    shift_term = modulation[:, None, DIM : 2 * DIM]
    scale_term = modulation[:, None, 2 * DIM :]
    own_columns = lax.all_to_all(flattened, "fsdp", split_axis=1, concat_axis=0, tiled=True)
    projected = lax.psum_scatter(
        jnp.dot(own_columns, out_weight[0], preferred_element_type=jnp.float32).astype(
            jnp.bfloat16
        ),
        "fsdp",
        scatter_dimension=0,
        tiled=True,
    ).astype(jnp.float32)
    updated = hidden.reshape(samples, row_count, DIM).astype(
        jnp.float32
    ) + gate_term * projected.reshape(samples, row_count, DIM)
    average = jnp.mean(updated, axis=-1, keepdims=True)
    centred = updated - average
    variance = jnp.mean(centred * centred, axis=-1, keepdims=True)
    normed = (centred * lax.rsqrt(variance + 1e-06) * (1.0 + scale_term) + shift_term).astype(
        jnp.bfloat16
    )
    velocity = jnp.dot(
        normed.reshape(flat_count, DIM), head_full[0], preferred_element_type=jnp.float32
    )
    velocity = velocity.reshape(1, samples, row_count // 2, 2 * PATCH)
    step_size = sigma_of(timesteps[0, :, 1]) - sigma_of(timesteps[0, :, 0])
    stepped = latent + step_size[None, :, None, None] * velocity
    carried = partner(stepped, "section", 0)
    return (velocity, carried)


def turn(half):
    return pltpu.roll(half.astype(jnp.float32), LANES // 2, 1)


def pack_half(tile):
    rows = tile.shape[0]
    wide = tile.astype(jnp.float32)
    lane = lax.broadcasted_iota(jnp.int32, (rows // 2, LANES), 1)
    return jnp.where(
        lane < LANES // 2, wide[: rows // 2], pltpu.roll(wide[rows // 2 :], LANES // 2, 1)
    ).astype(jnp.bfloat16)


def unpack_tiles(ref, rows, width):
    whole = width // LANES
    tiles = [ref[t * rows : (t + 1) * rows, :] for t in range(whole)]
    last = ref[whole * rows : whole * rows + rows // 2, :]
    tiles.append(jnp.concatenate([last, turn(last).astype(jnp.bfloat16)], axis=0))
    return tiles


def head_tiles(width):
    return -(-width // LANES)


MOD_ROWS = 16


def put_modulation(out, at, row):
    width = row.shape[1]
    tiles = -(-width // LANES)
    left = jnp.concatenate([row, jnp.zeros((1, tiles * LANES - width), jnp.float32)], axis=1)
    left = jnp.concatenate(
        [left[:, t * LANES : (t + 1) * LANES] for t in range(tiles)]
        + [jnp.zeros((8 - tiles, LANES), jnp.float32)][: 8 - tiles],
        axis=0,
    )
    high = left.astype(jnp.bfloat16)
    low = (left - high.astype(jnp.float32)).astype(jnp.bfloat16)
    out[at : at + MOD_ROWS, :] = jnp.concatenate([high, low], axis=0)


def get_modulation(ref, at, width):
    terms = ref[at : at + MOD_ROWS, :].astype(jnp.float32)
    total = terms[0:8] + terms[8:16]
    tiles = -(-width // LANES)
    return jnp.concatenate([total[t : t + 1] for t in range(tiles)], axis=1)[:, :width]


def cut_window(width, held, out, r, odd):
    rows = held.shape[1]
    whole = width // LANES
    last = slice(whole * rows, rows * width // LANES)

    @pl.when(jnp.logical_not(odd))
    def _():
        for t in range(whole):
            out[t * rows : (t + 1) * rows, :] = held[r, :, t * LANES : (t + 1) * LANES]
        out[last, :] = pack_half(held[r, :, whole * LANES :])

    @pl.when(odd)
    def _():
        lane = lax.broadcasted_iota(jnp.int32, (rows, LANES), 1)
        turned = [turn(held[r, :, t * LANES : (t + 1) * LANES]) for t in range(whole + 1)]
        for t in range(whole):
            out[t * rows : (t + 1) * rows, :] = jnp.where(
                lane < LANES // 2, turned[t], turned[t + 1]
            ).astype(jnp.bfloat16)
        out[last, :] = pack_half(turned[whole])


def windows(x_ref, held, sems, me, half, count, width, slots):
    span = held.shape[2]

    def window(k, r):
        start = half * (count * width) + lax.div((me ^ r) * width, LANES) * LANES
        return pltpu.make_async_copy(
            x_ref.at[:, pl.ds(pl.multiple_of(start, LANES), span)], held.at[k], sems.at[k]
        )

    return [window(k, r) for k, r in enumerate(slots)]


def sigma_row(step):
    unit_time = jnp.full((1, LANES), step, jnp.int32).astype(jnp.float32) / 1000.0
    return 5.0 * unit_time / (1.0 + 4.0 * unit_time)


def first_kernel(width, count, slot, place_ref, half_ref, group_ref, x_ref, head_ref, *refs):
    out_ref, pack_ref, held, head_held, sems, head_sem = refs
    me = place_ref[0]
    cut, columns = head_held.shape
    copy = windows(x_ref, held, sems, me, 1 - half_ref[0], count, width, [slot])[0]
    head_copy = pltpu.make_async_copy(
        head_ref.at[pl.ds(pl.multiple_of(group_ref[0] * cut, cut), cut), :], head_held, head_sem
    )
    head_copy.start()
    copy.start()
    head_copy.wait()
    packed = out_ref.shape[0] - pack_ref.shape[0]
    for t in range(head_tiles(columns)):
        tile = head_held[:, t * LANES : min((t + 1) * LANES, columns)]
        if tile.shape[1] < LANES:
            fill = jnp.zeros((cut, LANES - tile.shape[1]), tile.dtype)
            tile = jnp.concatenate([tile, fill], axis=1)
        pack_ref[t * cut : (t + 1) * cut, :] = tile
        out_ref[packed + t * cut : packed + (t + 1) * cut, :] = tile
    copy.wait()
    cut_window(width, held, out_ref, 0, lax.rem(me ^ slot, 2) == 1)


def split_first(x, head, scalars, slot, count, halves):
    rows, columns = x.shape
    width = columns // halves // count
    cut = head.shape[0] // 2
    span = cut * head_tiles(head.shape[1])
    length = rows * width // LANES
    return pl.pallas_call(
        functools.partial(first_kernel, width, count, slot),
        in_specs=[pl.BlockSpec(memory_space=pltpu.SMEM)] * 3
        + [pl.BlockSpec(memory_space=pltpu.HBM)] * 2,
        out_shape=[
            jax.ShapeDtypeStruct((length + span, LANES), jnp.bfloat16),
            jax.ShapeDtypeStruct((span, LANES), jnp.bfloat16),
        ],
        scratch_shapes=[
            pltpu.VMEM((1, rows, (width // LANES + 1) * LANES), jnp.bfloat16),
            pltpu.VMEM((cut, head.shape[1]), jnp.bfloat16),
            pltpu.SemaphoreType.DMA((1,)),
            pltpu.SemaphoreType.DMA,
        ],
        compiler_params=pltpu.CompilerParams(vmem_limit_bytes=4 << 20),
        cost_estimate=pl.CostEstimate(
            flops=0, transcendentals=0, bytes_accessed=4 * rows * width
        ),
        name="split_first",
    )(
        *scalars,
        pltpu.with_memory_space_constraint(x, pltpu.HBM),
        pltpu.with_memory_space_constraint(head, pltpu.HBM),
    )


def far_kernel(width, count, slots, rider, place_ref, half_ref, when_ref, x_ref, pack_ref, *refs):
    outs, (clock_ref, held, steps_ref, sems, steps_sem) = refs[: len(slots)], refs[len(slots) :]
    me = place_ref[0]
    copies = windows(x_ref, held, sems, me, 1 - half_ref[0], count, width, slots)
    steps_copy = pltpu.make_async_copy(when_ref, steps_ref, steps_sem)
    for copy in copies:
        copy.start()
    steps_copy.start()
    packed = held.shape[1] * width // LANES
    outs[slots.index(rider)][packed:, :] = pack_ref[...]
    for k, r in enumerate(slots):
        copies[k].wait()
        cut_window(width, held, outs[k], k, lax.rem(me ^ r, 2) == 1)
    steps_copy.wait()
    now = jnp.full((1, LANES), steps_ref[0, 0], jnp.int32).astype(jnp.float32)
    change = sigma_row(steps_ref[0, 1]) - sigma_row(steps_ref[0, 0])
    clock_ref[...] = jnp.concatenate([now, change])


def split_far(x, pack, steps, scalars, slots, rider, count, halves):
    rows, columns = x.shape
    width = columns // halves // count
    length = rows * width // LANES
    results = pl.pallas_call(
        functools.partial(far_kernel, width, count, slots, rider),
        in_specs=[pl.BlockSpec(memory_space=pltpu.SMEM)] * 2
        + [pl.BlockSpec(memory_space=pltpu.HBM)] * 2
        + [pl.BlockSpec(memory_space=pltpu.VMEM)],
        out_shape=[
            jax.ShapeDtypeStruct((length + pack.shape[0] * (r == rider), LANES), jnp.bfloat16)
            for r in slots
        ]
        + [jax.ShapeDtypeStruct((2, LANES), jnp.float32)],
        scratch_shapes=[
            pltpu.VMEM((len(slots), rows, (width // LANES + 1) * LANES), jnp.bfloat16),
            pltpu.SMEM((1, 2), jnp.int32),
            pltpu.SemaphoreType.DMA((len(slots),)),
            pltpu.SemaphoreType.DMA,
        ],
        compiler_params=pltpu.CompilerParams(vmem_limit_bytes=4 << 20),
        cost_estimate=pl.CostEstimate(
            flops=0, transcendentals=0, bytes_accessed=4 * rows * columns // halves
        ),
        name="split_far",
    )(
        *scalars[:2],
        pltpu.with_memory_space_constraint(steps, pltpu.HBM),
        pltpu.with_memory_space_constraint(x, pltpu.HBM),
        pack,
    )
    return results[:-1], results[-1]


def near_kernel(width, count, place_ref, half_ref, x_ref, *refs):
    outs, held, sems = refs[:count], refs[count], refs[count + 1]
    me = place_ref[0]
    copies = windows(x_ref, held, sems, me, half_ref[0], count, width, range(count))
    for r in range(count - 1, -1, -1):
        copies[r].start()
    for r in range(count - 1, -1, -1):
        copies[r].wait()
        cut_window(width, held, outs[r], r, lax.rem(me ^ r, 2) == 1)


def split_near(x, scalars, count, halves):
    rows, columns = x.shape
    width = columns // halves // count
    length = rows * width // LANES
    return pl.pallas_call(
        functools.partial(near_kernel, width, count),
        in_specs=[pl.BlockSpec(memory_space=pltpu.SMEM)] * 2
        + [pl.BlockSpec(memory_space=pltpu.HBM)],
        out_shape=[jax.ShapeDtypeStruct((length, LANES), jnp.bfloat16)] * count,
        scratch_shapes=[
            pltpu.VMEM((count, rows, (width // LANES + 1) * LANES), jnp.bfloat16),
            pltpu.SemaphoreType.DMA((count,)),
        ],
        compiler_params=pltpu.CompilerParams(vmem_limit_bytes=4 << 20),
        cost_estimate=pl.CostEstimate(
            flops=0, transcendentals=0, bytes_accessed=4 * rows * columns // halves
        ),
        name="split_near",
    )(*scalars[:2], pltpu.with_memory_space_constraint(x, pltpu.HBM))


def load_kernel(count, place_ref, w_ref, out_ref, sems):
    depth = w_ref.shape[0] // count

    def block(r):
        owner = place_ref[0] ^ r
        return pltpu.make_async_copy(
            w_ref.at[pl.ds(pl.multiple_of(owner * depth, depth), depth), :],
            out_ref.at[r * depth : (r + 1) * depth, :],
            sems.at[r],
        )

    for r in range(count):
        block(r).start()
    for r in range(count):
        block(r).wait()


def load_rows(weight, place, count):
    return pl.pallas_call(
        functools.partial(load_kernel, count),
        in_specs=[
            pl.BlockSpec(memory_space=pltpu.SMEM),
            pl.BlockSpec(memory_space=pltpu.HBM),
        ],
        out_specs=pl.BlockSpec(memory_space=pltpu.VMEM),
        out_shape=pltpu.VMEM(weight.shape, weight.dtype),
        scratch_shapes=[pltpu.SemaphoreType.DMA((count,))],
        compiler_params=pltpu.CompilerParams(vmem_limit_bytes=2 << 20),
        cost_estimate=pl.CostEstimate(
            flops=0, transcendentals=0, bytes_accessed=2 * weight.size * 2
        ),
        name="load_rows",
    )(place, pltpu.with_memory_space_constraint(weight, pltpu.HBM))


def attend_kernel(heads, rows, count, *refs):
    riders, ins, outs = refs[: -2 * count], refs[-2 * count : -count], refs[-count:]
    width = heads * 3 * HEAD
    blocks = [unpack_tiles(ref, rows, width) for ref in ins]

    def columns(start):
        first, offset = divmod(start, LANES)
        parts = []
        for tiles in blocks:
            if offset + HEAD <= LANES:
                parts.append(tiles[first][:, offset : offset + HEAD])
            else:
                wide = jnp.concatenate([tiles[first], tiles[first + 1]], axis=1)
                parts.append(wide[:, offset : offset + HEAD])
        return jnp.concatenate(parts, axis=0)

    results = []
    for h in range(heads):
        start = h * 3 * HEAD
        query, key, value = (columns(start + i * HEAD) for i in range(3))
        scores = lax.dot_general(
            query, key, (((1,), (1,)), ((), ())), preferred_element_type=jnp.float32
        )
        row_max = jnp.max(scores, axis=-1, keepdims=True)
        exp_scores = jnp.exp2((scores - row_max) * (HEAD ** (-0.5) / math.log(2.0)))
        row_sum = jnp.sum(exp_scores, axis=-1, keepdims=True)
        summed = jnp.dot(
            exp_scores.astype(jnp.bfloat16), value, preferred_element_type=jnp.float32
        )
        results.append(summed / row_sum)
    attended = jnp.concatenate(results, axis=1).astype(jnp.bfloat16)
    whole = heads * HEAD // LANES
    for b in range(count):
        mine = attended[b * rows : (b + 1) * rows]
        for t in range(whole):
            outs[b][t * rows : (t + 1) * rows, :] = mine[:, t * LANES : (t + 1) * LANES]
        rest = mine[:, whole * LANES :].astype(jnp.float32)
        packed = rows * heads * HEAD // LANES
        outs[b][whole * rows : packed, :] = jnp.concatenate(
            [rest[: rows // 2], rest[rows // 2 :]], axis=1
        ).astype(jnp.bfloat16)
        if riders:
            mod_ref, other_ref = riders
            put_modulation(outs[b], packed, mod_ref[0:1, :])
            packed += MOD_ROWS
            outs[b][packed : packed + MOD_ROWS, :] = other_ref[other_ref.shape[0] - MOD_ROWS :, :]


def attend_packed(pieces, heads, rows, riders=()):
    count = len(pieces)
    total = count * rows
    length = rows * heads * HEAD // LANES
    specs = [pl.BlockSpec(memory_space=pltpu.VMEM)] * (count + len(riders))
    if riders:
        length += MOD_ROWS * len(riders)
    out = jax.ShapeDtypeStruct((length, LANES), jnp.bfloat16)
    return pl.pallas_call(
        functools.partial(attend_kernel, heads, rows, count),
        in_specs=specs,
        out_shape=[out] * count,
        compiler_params=pltpu.CompilerParams(vmem_limit_bytes=12 << 20),
        cost_estimate=pl.CostEstimate(
            flops=4 * heads * total * total * HEAD,
            transcendentals=heads * total * total,
            bytes_accessed=8 * total * heads * HEAD,
        ),
        name="attend_packed",
    )(*riders, *pieces)


def gather_left(refs, left_ref, rows):
    depth = left_ref.shape[1] // len(refs)
    left_ref[...] = jnp.concatenate(
        [jnp.concatenate(unpack_tiles(ref, rows, depth), axis=1)[:, :depth] for ref in refs],
        axis=1,
    )


def project_kernel(rows, first, slots, w_ref, *refs):
    pieces, rest = refs[: len(slots)], refs[len(slots) :]
    out_ref, left_ref = rest[-2:]
    gather_left(pieces, left_ref, rows)
    depth = left_ref.shape[1] // len(slots)
    tile = math.gcd(out_ref.shape[1], 5 * LANES)
    for start in range(0, out_ref.shape[1], tile):
        cut = slice(first + start, first + start + tile)
        here = slice(start, start + tile)
        right = [w_ref[r * depth : (r + 1) * depth, cut] for r in slots]
        term = jnp.dot(
            left_ref[...], jnp.concatenate(right, axis=0), preferred_element_type=jnp.float32
        )
        if len(rest) == 3:
            term = rest[0][:, here] + term
        out_ref[:, here] = term.astype(out_ref.dtype)


def project_packed(pieces, slots, count, weight, rows, first, dim, dtype, base=()):
    depth = weight.shape[0] // count
    held = pltpu.with_memory_space_constraint(weight, pltpu.VMEM)
    inputs = (*pieces, *base)
    return pl.pallas_call(
        functools.partial(project_kernel, rows, first, slots),
        in_specs=[pl.BlockSpec(memory_space=pltpu.VMEM)] * (1 + len(inputs)),
        out_shape=jax.ShapeDtypeStruct((rows, dim), dtype),
        scratch_shapes=[pltpu.VMEM((rows, depth * len(slots)), jnp.bfloat16)],
        compiler_params=pltpu.CompilerParams(vmem_limit_bytes=16 << 20),
        cost_estimate=pl.CostEstimate(
            flops=2 * rows * depth * len(slots) * dim,
            transcendentals=0,
            bytes_accessed=2 * depth * len(slots) * dim,
        ),
        name="project_packed",
    )(held, *inputs)


def finish_kernel(rows, near_ref, *refs):
    far, refs = refs[:2], refs[2:]
    mod_ref, hidden_ref, head_ref, latent_ref, clock_ref, out_ref, step_ref = refs[:7]
    acc_ref, turn_ref = refs[7:]
    steps, _, tile = acc_ref.shape
    dim = steps * tile

    def modulation(which, i):
        start = which * dim + i * tile
        line, offset = divmod(start, mod_ref.shape[2])
        return mod_ref[line, :, offset : offset + tile]

    total = jnp.zeros((rows, 1), jnp.float32)
    for i in range(steps):
        cut = slice(i * tile, (i + 1) * tile)
        side, offset = divmod(i * tile, dim // 2)
        projected = near_ref[:, cut] + far[side][:, offset : offset + tile].astype(jnp.float32)
        part = hidden_ref[:, cut].astype(jnp.float32) + modulation(0, i) * projected
        acc_ref[i] = part
        total += jnp.sum(part, axis=-1, keepdims=True)
    average = total / dim
    square = jnp.zeros((rows, 1), jnp.float32)
    for i in range(steps):
        centred = acc_ref[i] - average
        square += jnp.sum(centred * centred, axis=-1, keepdims=True)
    rate = lax.rsqrt(square / dim + 1e-06)
    velocity = jnp.zeros(turn_ref.shape, jnp.float32)
    for i in range(steps):
        cut = slice(i * tile, (i + 1) * tile)
        normed = (
            (acc_ref[i] - average) * rate * (1.0 + modulation(2, i)) + modulation(1, i)
        ).astype(jnp.bfloat16)
        velocity += lax.dot_general(
            normed,
            head_ref[:, cut],
            (((1,), (1,)), ((), ())),
            preferred_element_type=jnp.float32,
        )
    turn_ref[...] = velocity
    paired = jnp.concatenate(
        [turn_ref[pl.ds(0, rows // 2, stride=2), :], turn_ref[pl.ds(1, rows // 2, stride=2), :]],
        axis=1,
    )
    out_ref[...] = paired
    step_ref[...] = latent_ref[...] + clock_ref[1:2, :] * paired


def finish(near, far, hidden, lines, head_rows, latent, clock):
    rows, dim = near.shape
    tile = math.gcd(dim // 2, lines.shape[2])
    patch = head_rows.shape[0]
    inputs = (near, *far, lines, hidden, head_rows, latent, clock)
    result = jax.ShapeDtypeStruct((rows // 2, 2 * patch), jnp.float32)
    return pl.pallas_call(
        functools.partial(finish_kernel, rows),
        in_specs=[pl.BlockSpec(memory_space=pltpu.VMEM)] * len(inputs),
        out_shape=[result] * 2,
        scratch_shapes=[
            pltpu.VMEM((dim // tile, rows, tile), jnp.float32),
            pltpu.VMEM((rows, patch), jnp.float32),
        ],
        compiler_params=pltpu.CompilerParams(vmem_limit_bytes=8 << 20),
        cost_estimate=pl.CostEstimate(
            flops=2 * rows * patch * dim, transcendentals=0, bytes_accessed=8 * rows * dim
        ),
        name="finish",
    )(*inputs)


def collect_kernel(starts, *refs):
    out_ref = refs[-1]
    span = out_ref.shape[0] // len(starts)
    for k, (which, start) in enumerate(starts):
        out_ref[k * span : (k + 1) * span, :] = refs[which][start : start + span, :]


def collect(pieces, starts, span):
    return pl.pallas_call(
        functools.partial(collect_kernel, starts),
        in_specs=[pl.BlockSpec(memory_space=pltpu.VMEM)] * len(pieces),
        out_shape=jax.ShapeDtypeStruct((len(starts) * span, LANES), jnp.bfloat16),
        compiler_params=pltpu.CompilerParams(vmem_limit_bytes=4 << 20),
        cost_estimate=pl.CostEstimate(
            flops=0, transcendentals=0, bytes_accessed=4 * len(starts) * span * LANES
        ),
        name="collect",
    )(*pieces)


def line_kernel(starts, *refs):
    pieces, (mod_ref, out_ref) = refs[:-2], refs[-2:]
    span = (out_ref.shape[0] - MOD_ROWS) // len(starts)
    for k, start in enumerate(starts):
        out_ref[k * span : (k + 1) * span, :] = pieces[k][start : start + span, :]
    put_modulation(out_ref, out_ref.shape[0] - MOD_ROWS, mod_ref[1:2, :])


def collect_line(pieces, starts, span, modulation):
    return pl.pallas_call(
        functools.partial(line_kernel, starts),
        in_specs=[pl.BlockSpec(memory_space=pltpu.VMEM)] * (len(pieces) + 1),
        out_shape=jax.ShapeDtypeStruct((len(starts) * span + MOD_ROWS, LANES), jnp.bfloat16),
        compiler_params=pltpu.CompilerParams(vmem_limit_bytes=4 << 20),
        cost_estimate=pl.CostEstimate(
            flops=0, transcendentals=0, bytes_accessed=4 * len(starts) * span * LANES
        ),
        name="collect_line",
    )(*pieces, modulation)


def arrange_kernel(count, width, done, place_ref, half_ref, group_ref, *refs):
    mine_ref, up_ref, mod_ref, other_ref = refs[:4]
    near = refs[4:-2]
    head_out, mod_out = refs[-2:]
    span = mine_ref.shape[0] // (2 * count)
    cut = head_out.shape[0] // 2
    tiles = span // cut
    first = half_ref[0] == 0
    lower = group_ref[0] == 0
    columns = mod_ref.shape[1]

    def block(ref, k):
        parts = [ref[k * span + t * cut : k * span + (t + 1) * cut, :] for t in range(tiles)]
        return jnp.concatenate(parts, axis=1)[:, :width]

    def whole(k):
        mine, up = block(mine_ref, k), block(up_ref, k)
        return jnp.concatenate(
            [jnp.where(lower, mine, up), jnp.where(lower, up, mine)], axis=0
        )

    for r in range(count):
        owner = place_ref[0] ^ r
        own, other = whole(r), whole(count + r)
        start = pl.multiple_of(owner * 2 * width, LANES)
        head_out[:, pl.ds(start, 2 * width)] = jnp.concatenate(
            [jnp.where(first, own, other), jnp.where(first, other, own)], axis=1
        )
        if r == 0:
            own = mod_ref[0:1, :]
            other = get_modulation(other_ref, other_ref.shape[0] - MOD_ROWS, columns)
        else:
            own = get_modulation(near[r], done, columns)
            other = get_modulation(near[r], done + MOD_ROWS, columns)
        mod_out[owner] = jnp.concatenate(
            [jnp.where(first, own, other), jnp.where(first, other, own)], axis=1
        )


def arrange(mine, up, modulation, other, near, head, scalars, done):
    count = len(near)
    patch, width = head.shape
    columns = modulation.shape[1]
    return pl.pallas_call(
        functools.partial(arrange_kernel, count, width, done),
        in_specs=[pl.BlockSpec(memory_space=pltpu.SMEM)] * 3
        + [pl.BlockSpec(memory_space=pltpu.VMEM)] * (4 + count),
        out_shape=[
            jax.ShapeDtypeStruct((patch, 2 * count * width), jnp.bfloat16),
            jax.ShapeDtypeStruct((count, 1, 2 * columns), jnp.float32),
        ],
        compiler_params=pltpu.CompilerParams(vmem_limit_bytes=4 << 20),
        cost_estimate=pl.CostEstimate(
            flops=0, transcendentals=0, bytes_accessed=8 * count * patch * width
        ),
        name="arrange",
    )(*scalars, mine, up, modulation, other, *near)


def packed_body(head_inputs, hidden, out_weight, time_weight, head_weight, latent, timesteps):
    count = lax.axis_size("seq")
    halves = lax.axis_size("fsdp")
    rows = head_inputs.shape[2]
    place = lax.axis_index("seq")
    half = lax.axis_index("fsdp")
    group = lax.axis_index("grp")
    heads = HEADS // halves // count

    def along(block, r):
        return lax.ppermute(block, "seq", [(i, i ^ r) for i in range(count)])

    def swap(block, axis):
        return lax.ppermute(block, axis, [(0, 1), (1, 0)])

    def slanted(block, r):
        route = []
        for i in range(count):
            for j in range(halves):
                route.append((i * halves + j, (i ^ r) * halves + 1 - j))
        return lax.ppermute(block, ("seq", "fsdp"), route)

    x = head_inputs.reshape(rows, head_inputs.shape[3])
    head = jnp.swapaxes(head_weight[0], 0, 1)
    span = head.shape[0] // 2 * head_tiles(head.shape[1])
    here = place[None].astype(jnp.int32)
    side = half[None].astype(jnp.int32)
    level = group[None].astype(jnp.int32)
    scalars = (here, side, level)
    last = count // 2
    slots = [r for r in range(count - 1, 0, -1) if r != last] + [0]
    first, pack = split_first(x, head, scalars, last, count, halves)
    sent, clock = split_far(x, pack, timesteps.reshape(1, 2), scalars, slots, 1, count, halves)
    far_sent = [first if r == last else sent[slots.index(r)] for r in range(count)]
    far_pieces = [slanted(far_sent[r], r) for r in range(count)]

    other_steps = swap(timesteps, "fsdp")
    freqs = jnp.exp(
        -math.log(10000.0) * jnp.arange(FREQ // 2, dtype=jnp.float32) / (FREQ // 2)
    )
    angle = jnp.concatenate([clock[:1], jnp.full((1, LANES), other_steps[0, 0, 0], jnp.float32)])
    angle = angle * freqs
    embedding = jnp.concatenate([jnp.cos(angle), jnp.sin(angle)], axis=-1).astype(jnp.bfloat16)
    modulation = jnp.dot(embedding, time_weight[0], preferred_element_type=jnp.float32)

    near_sent = split_near(x, scalars, count, halves)
    near_pieces = [near_sent[0]] + [along(near_sent[r], r) for r in range(1, count)]

    weight = load_rows(out_weight[0], here, count)
    far_attended = attend_packed(far_pieces, heads, rows)
    far_home = [far_attended[0]]
    far_home += [along(far_attended[r], r) for r in range(1, count)]
    part = DIM // 2
    partial = []
    for k in range(2):
        term = project_packed(
            far_home, range(count), count, weight, rows, k * part, part, jnp.bfloat16
        )
        partial.append(swap(term, "fsdp"))

    packed = near_sent[0].shape[0]
    relay = collect([far_pieces[2]], [(0, packed)], span)
    relayed = along(relay, 1)
    line = collect_line(
        [pack, far_pieces[1], far_pieces[2], relayed], [0, packed, packed, 0], span, modulation
    )
    other = swap(line, "fsdp")
    own_slots = [(0 if r == 0 else 1, r * span) for r in range(count)]
    far_slots = [(1 if r == 0 else 0, r * span) for r in range(count)]
    mine = collect([line, other], own_slots + far_slots, span)
    up = swap(mine, "grp")
    near_attended = attend_packed(near_pieces, heads, rows, (modulation, other))
    near_home = [near_attended[0]]
    near_home += [along(near_attended[r], r) for r in range(1, count)]
    done = near_home[0].shape[0] - 2 * MOD_ROWS
    head_rows, lines = arrange(mine, up, modulation, other, near_home, head, scalars, done)
    others = [r for r in range(count) if r != 1]
    most = project_packed(
        [near_home[r] for r in others], others, count, weight, rows, 0, DIM, jnp.float32
    )
    projected = project_packed(
        [near_home[1]], [1], count, weight, rows, 0, DIM, jnp.float32, (most,)
    )
    velocity, stepped = finish(
        projected,
        partial,
        hidden.reshape(rows, DIM),
        lines,
        head_rows,
        latent.reshape(rows // 2, 2 * PATCH),
        clock,
    )
    carried = partner(stepped, "section", 0)
    return (velocity.reshape(latent.shape), carried.reshape(latent.shape))


def packed_fits(mesh, head_shape):
    count, halves = mesh.shape["seq"], mesh.shape["fsdp"]
    rows = head_shape[2]
    return (
        head_shape[1] == 1
        and halves == 2
        and FREQ == 2 * LANES
        and 2 * PATCH == LANES
        and mesh.shape["grp"] == 2
        and count == 4
        and HEADS % (halves * count) == 0
        and 3 * DIM // (halves * count) <= 8 * LANES
        and DIM % (halves * count) == 0
        and HEADS // (halves * count) * HEAD % LANES == LANES // 2
        and rows % 32 == 0
        and rows * count <= 512
    )


def step(mesh, body):
    return jax.shard_map(
        body,
        mesh=mesh,
        in_specs=(
            P("section", ("grp", "fsdp"), "seq", None),
            P("section", ("grp", "fsdp"), "seq", None),
            P("section", "fsdp", None),
            P("section", None, ("seq", "fsdp")),
            P("section", ("seq", "fsdp"), None),
            P("section", ("grp", "fsdp"), "seq", None),
            P("section", ("grp", "fsdp"), None),
        ),
        out_specs=(
            P("section", ("grp", "fsdp"), "seq", None),
            P("section", ("grp", "fsdp"), "seq", None),
        ),
        check_vma=False,
    )


def solution(mesh):
    def choose(head_inputs, *rest):
        local = (
            head_inputs.shape[0] // mesh.shape["section"],
            head_inputs.shape[1] // mesh.shape["grp"] // mesh.shape["fsdp"],
            head_inputs.shape[2] // mesh.shape["seq"],
        )
        if not packed_fits(mesh, local):
            return step(mesh, general_body)(head_inputs, *rest)
        return step(mesh, packed_body)(head_inputs, *rest)

    return choose
```

```python
import functools
import math

import jax
import jax.numpy as jnp
from jax import lax
from jax.experimental import pallas as pl
from jax.experimental.pallas import tpu as pltpu
from jax.sharding import PartitionSpec as P


DIM = 2560
HEADS = 32
HEAD = 80
PATCH = 64
FREQ = 256
LANES = 128


def partner(block, axis, apart):
    count = lax.axis_size(axis)
    route = []
    for low in range(count):
        high = low | 1 << apart
        if high != low and high < count:
            route += [(low, high), (high, low)]
    return lax.ppermute(block, axis, route)


def time_embed(steps_now):
    half = FREQ // 2
    freqs = jnp.exp(-math.log(10000.0) * jnp.arange(half, dtype=jnp.float32) / half)
    angle = steps_now.astype(jnp.float32)[..., None] * freqs
    return jnp.concatenate([jnp.cos(angle), jnp.sin(angle)], axis=-1)


def sigma_of(steps_now):
    unit_time = steps_now.astype(jnp.float32) / 1000.0
    return 5.0 * unit_time / (1.0 + 4.0 * unit_time)


def attend(exchanged):
    items = exchanged.shape[0]
    length = exchanged.shape[1]
    local_heads = exchanged.shape[2]
    query_all = exchanged[..., :HEAD]
    key_rows = exchanged[..., HEAD : 2 * HEAD]
    value_rows = exchanged[..., 2 * HEAD :]
    block_rows = min(512, length)
    block_count = length // block_rows

    def one_block(block_index):
        query_block = lax.dynamic_slice_in_dim(query_all, block_index * block_rows, block_rows, 1)
        scores = jnp.einsum(
            "nqhe,nkhe->nhqk", query_block, key_rows, preferred_element_type=jnp.float32
        ) * HEAD ** (-0.5)
        row_max = jnp.max(scores, axis=-1, keepdims=True)
        exp_scores = jnp.exp(scores - row_max)
        row_sum = jnp.sum(exp_scores, axis=-1, keepdims=True)
        weights = (exp_scores / row_sum).astype(jnp.bfloat16)
        return jnp.einsum(
            "nhqk,nkhe->nqhe", weights, value_rows, preferred_element_type=jnp.float32
        ).astype(jnp.bfloat16)

    blocks = lax.map(one_block, jnp.arange(block_count, dtype=jnp.int32))
    return blocks.transpose(1, 0, 2, 3, 4).reshape(items, length, local_heads * HEAD)


def general_body(head_inputs, hidden, out_weight, time_weight, head_weight, latent, timesteps):
    samples = head_inputs.shape[1]
    row_count = head_inputs.shape[2]
    flat_count = samples * row_count
    local = head_inputs.reshape(samples, row_count, HEADS, 3 * HEAD)
    attended = lax.all_to_all(
        attend(lax.all_to_all(local, "seq", split_axis=2, concat_axis=1, tiled=True)),
        "seq",
        split_axis=1,
        concat_axis=2,
        tiled=True,
    )
    flattened = attended.reshape(flat_count, HEADS * HEAD)
    time_full, head_full = (
        lax.all_gather(time_weight, ("seq", "fsdp"), axis=2, tiled=True),
        lax.all_gather(head_weight, ("seq", "fsdp"), axis=1, tiled=True),
    )
    embedding = time_embed(timesteps[0, :, 0]).astype(jnp.bfloat16)
    modulation = jnp.dot(embedding, time_full[0], preferred_element_type=jnp.float32)
    gate_term = modulation[:, None, :DIM]
    shift_term = modulation[:, None, DIM : 2 * DIM]
    scale_term = modulation[:, None, 2 * DIM :]
    own_columns = lax.all_to_all(flattened, "fsdp", split_axis=1, concat_axis=0, tiled=True)
    projected = lax.psum_scatter(
        jnp.dot(own_columns, out_weight[0], preferred_element_type=jnp.float32).astype(
            jnp.bfloat16
        ),
        "fsdp",
        scatter_dimension=0,
        tiled=True,
    ).astype(jnp.float32)
    updated = hidden.reshape(samples, row_count, DIM).astype(
        jnp.float32
    ) + gate_term * projected.reshape(samples, row_count, DIM)
    average = jnp.mean(updated, axis=-1, keepdims=True)
    centred = updated - average
    variance = jnp.mean(centred * centred, axis=-1, keepdims=True)
    normed = (centred * lax.rsqrt(variance + 1e-06) * (1.0 + scale_term) + shift_term).astype(
        jnp.bfloat16
    )
    velocity = jnp.dot(
        normed.reshape(flat_count, DIM), head_full[0], preferred_element_type=jnp.float32
    )
    velocity = velocity.reshape(1, samples, row_count // 2, 2 * PATCH)
    step_size = sigma_of(timesteps[0, :, 1]) - sigma_of(timesteps[0, :, 0])
    stepped = latent + step_size[None, :, None, None] * velocity
    carried = partner(stepped, "section", 0)
    return (velocity, carried)


def turn(half):
    return pltpu.roll(half.astype(jnp.float32), LANES // 2, 1)


def pack_half(tile):
    rows = tile.shape[0]
    wide = tile.astype(jnp.float32)
    lane = lax.broadcasted_iota(jnp.int32, (rows // 2, LANES), 1)
    return jnp.where(
        lane < LANES // 2, wide[: rows // 2], pltpu.roll(wide[rows // 2 :], LANES // 2, 1)
    ).astype(jnp.bfloat16)


def unpack_tiles(ref, rows, width):
    whole = width // LANES
    tiles = [ref[t * rows : (t + 1) * rows, :] for t in range(whole)]
    last = ref[whole * rows : whole * rows + rows // 2, :]
    tiles.append(jnp.concatenate([last, turn(last).astype(jnp.bfloat16)], axis=0))
    return tiles


def head_tiles(width):
    return -(-width // LANES)


MOD_ROWS = 16


def put_modulation(out, at, row):
    width = row.shape[1]
    tiles = -(-width // LANES)
    left = jnp.concatenate([row, jnp.zeros((1, tiles * LANES - width), jnp.float32)], axis=1)
    left = jnp.concatenate(
        [left[:, t * LANES : (t + 1) * LANES] for t in range(tiles)]
        + [jnp.zeros((8 - tiles, LANES), jnp.float32)][: 8 - tiles],
        axis=0,
    )
    high = left.astype(jnp.bfloat16)
    low = (left - high.astype(jnp.float32)).astype(jnp.bfloat16)
    out[at : at + MOD_ROWS, :] = jnp.concatenate([high, low], axis=0)


def get_modulation(ref, at, width):
    terms = ref[at : at + MOD_ROWS, :].astype(jnp.float32)
    total = terms[0:8] + terms[8:16]
    tiles = -(-width // LANES)
    return jnp.concatenate([total[t : t + 1] for t in range(tiles)], axis=1)[:, :width]


def cut_window(width, held, out, r, odd):
    rows = held.shape[1]
    whole = width // LANES
    last = slice(whole * rows, rows * width // LANES)

    @pl.when(jnp.logical_not(odd))
    def _():
        for t in range(whole):
            out[t * rows : (t + 1) * rows, :] = held[r, :, t * LANES : (t + 1) * LANES]
        out[last, :] = pack_half(held[r, :, whole * LANES :])

    @pl.when(odd)
    def _():
        lane = lax.broadcasted_iota(jnp.int32, (rows, LANES), 1)
        turned = [turn(held[r, :, t * LANES : (t + 1) * LANES]) for t in range(whole + 1)]
        for t in range(whole):
            out[t * rows : (t + 1) * rows, :] = jnp.where(
                lane < LANES // 2, turned[t], turned[t + 1]
            ).astype(jnp.bfloat16)
        out[last, :] = pack_half(turned[whole])


def windows(x_ref, held, sems, me, half, count, width, slots):
    span = held.shape[2]

    def window(k, r):
        start = half * (count * width) + lax.div((me ^ r) * width, LANES) * LANES
        return pltpu.make_async_copy(
            x_ref.at[:, pl.ds(pl.multiple_of(start, LANES), span)], held.at[k], sems.at[k]
        )

    return [window(k, r) for k, r in enumerate(slots)]


def sigma_row(step):
    unit_time = jnp.full((1, LANES), step, jnp.int32).astype(jnp.float32) / 1000.0
    return 5.0 * unit_time / (1.0 + 4.0 * unit_time)


def first_kernel(width, count, slot, place_ref, half_ref, group_ref, x_ref, head_ref, *refs):
    out_ref, pack_ref, held, head_held, sems, head_sem = refs
    me = place_ref[0]
    cut, columns = head_held.shape
    copy = windows(x_ref, held, sems, me, 1 - half_ref[0], count, width, [slot])[0]
    head_copy = pltpu.make_async_copy(
        head_ref.at[pl.ds(pl.multiple_of(group_ref[0] * cut, cut), cut), :], head_held, head_sem
    )
    head_copy.start()
    copy.start()
    head_copy.wait()
    packed = out_ref.shape[0] - pack_ref.shape[0]
    for t in range(head_tiles(columns)):
        tile = head_held[:, t * LANES : min((t + 1) * LANES, columns)]
        if tile.shape[1] < LANES:
            fill = jnp.zeros((cut, LANES - tile.shape[1]), tile.dtype)
            tile = jnp.concatenate([tile, fill], axis=1)
        pack_ref[t * cut : (t + 1) * cut, :] = tile
        out_ref[packed + t * cut : packed + (t + 1) * cut, :] = tile
    copy.wait()
    cut_window(width, held, out_ref, 0, lax.rem(me ^ slot, 2) == 1)


def split_first(x, head, scalars, slot, count, halves):
    rows, columns = x.shape
    width = columns // halves // count
    cut = head.shape[0] // 2
    span = cut * head_tiles(head.shape[1])
    length = rows * width // LANES
    return pl.pallas_call(
        functools.partial(first_kernel, width, count, slot),
        in_specs=[pl.BlockSpec(memory_space=pltpu.SMEM)] * 3
        + [pl.BlockSpec(memory_space=pltpu.HBM)] * 2,
        out_shape=[
            jax.ShapeDtypeStruct((length + span, LANES), jnp.bfloat16),
            jax.ShapeDtypeStruct((span, LANES), jnp.bfloat16),
        ],
        scratch_shapes=[
            pltpu.VMEM((1, rows, (width // LANES + 1) * LANES), jnp.bfloat16),
            pltpu.VMEM((cut, head.shape[1]), jnp.bfloat16),
            pltpu.SemaphoreType.DMA((1,)),
            pltpu.SemaphoreType.DMA,
        ],
        compiler_params=pltpu.CompilerParams(vmem_limit_bytes=4 << 20),
        cost_estimate=pl.CostEstimate(
            flops=0, transcendentals=0, bytes_accessed=4 * rows * width
        ),
    )(
        *scalars,
        pltpu.with_memory_space_constraint(x, pltpu.HBM),
        pltpu.with_memory_space_constraint(head, pltpu.HBM),
    )


def far_kernel(width, count, slots, rider, place_ref, half_ref, when_ref, x_ref, pack_ref, *refs):
    outs, (clock_ref, held, steps_ref, sems, steps_sem) = refs[: len(slots)], refs[len(slots) :]
    me = place_ref[0]
    copies = windows(x_ref, held, sems, me, 1 - half_ref[0], count, width, slots)
    steps_copy = pltpu.make_async_copy(when_ref, steps_ref, steps_sem)
    for copy in copies:
        copy.start()
    steps_copy.start()
    packed = held.shape[1] * width // LANES
    outs[slots.index(rider)][packed:, :] = pack_ref[...]
    for k, r in enumerate(slots):
        copies[k].wait()
        cut_window(width, held, outs[k], k, lax.rem(me ^ r, 2) == 1)
    steps_copy.wait()
    now = jnp.full((1, LANES), steps_ref[0, 0], jnp.int32).astype(jnp.float32)
    change = sigma_row(steps_ref[0, 1]) - sigma_row(steps_ref[0, 0])
    clock_ref[...] = jnp.concatenate([now, change])


def split_far(x, pack, steps, scalars, slots, rider, count, halves):
    rows, columns = x.shape
    width = columns // halves // count
    length = rows * width // LANES
    results = pl.pallas_call(
        functools.partial(far_kernel, width, count, slots, rider),
        in_specs=[pl.BlockSpec(memory_space=pltpu.SMEM)] * 2
        + [pl.BlockSpec(memory_space=pltpu.HBM)] * 2
        + [pl.BlockSpec(memory_space=pltpu.VMEM)],
        out_shape=[
            jax.ShapeDtypeStruct((length + pack.shape[0] * (r == rider), LANES), jnp.bfloat16)
            for r in slots
        ]
        + [jax.ShapeDtypeStruct((2, LANES), jnp.float32)],
        scratch_shapes=[
            pltpu.VMEM((len(slots), rows, (width // LANES + 1) * LANES), jnp.bfloat16),
            pltpu.SMEM((1, 2), jnp.int32),
            pltpu.SemaphoreType.DMA((len(slots),)),
            pltpu.SemaphoreType.DMA,
        ],
        compiler_params=pltpu.CompilerParams(vmem_limit_bytes=4 << 20),
        cost_estimate=pl.CostEstimate(
            flops=0, transcendentals=0, bytes_accessed=4 * rows * columns // halves
        ),
    )(
        *scalars[:2],
        pltpu.with_memory_space_constraint(steps, pltpu.HBM),
        pltpu.with_memory_space_constraint(x, pltpu.HBM),
        pack,
    )
    return results[:-1], results[-1]


def near_kernel(width, count, place_ref, half_ref, x_ref, *refs):
    outs, held, sems = refs[:count], refs[count], refs[count + 1]
    me = place_ref[0]
    copies = windows(x_ref, held, sems, me, half_ref[0], count, width, range(count))
    for r in range(count - 1, -1, -1):
        copies[r].start()
    for r in range(count - 1, -1, -1):
        copies[r].wait()
        cut_window(width, held, outs[r], r, lax.rem(me ^ r, 2) == 1)


def split_near(x, scalars, count, halves):
    rows, columns = x.shape
    width = columns // halves // count
    length = rows * width // LANES
    return pl.pallas_call(
        functools.partial(near_kernel, width, count),
        in_specs=[pl.BlockSpec(memory_space=pltpu.SMEM)] * 2
        + [pl.BlockSpec(memory_space=pltpu.HBM)],
        out_shape=[jax.ShapeDtypeStruct((length, LANES), jnp.bfloat16)] * count,
        scratch_shapes=[
            pltpu.VMEM((count, rows, (width // LANES + 1) * LANES), jnp.bfloat16),
            pltpu.SemaphoreType.DMA((count,)),
        ],
        compiler_params=pltpu.CompilerParams(vmem_limit_bytes=4 << 20),
        cost_estimate=pl.CostEstimate(
            flops=0, transcendentals=0, bytes_accessed=4 * rows * columns // halves
        ),
    )(*scalars[:2], pltpu.with_memory_space_constraint(x, pltpu.HBM))


def load_kernel(count, place_ref, w_ref, out_ref, sems):
    depth = w_ref.shape[0] // count

    def block(r):
        owner = place_ref[0] ^ r
        return pltpu.make_async_copy(
            w_ref.at[pl.ds(pl.multiple_of(owner * depth, depth), depth), :],
            out_ref.at[r * depth : (r + 1) * depth, :],
            sems.at[r],
        )

    for r in range(count):
        block(r).start()
    for r in range(count):
        block(r).wait()


def load_rows(weight, place, count):
    return pl.pallas_call(
        functools.partial(load_kernel, count),
        in_specs=[
            pl.BlockSpec(memory_space=pltpu.SMEM),
            pl.BlockSpec(memory_space=pltpu.HBM),
        ],
        out_specs=pl.BlockSpec(memory_space=pltpu.VMEM),
        out_shape=pltpu.VMEM(weight.shape, weight.dtype),
        scratch_shapes=[pltpu.SemaphoreType.DMA((count,))],
        compiler_params=pltpu.CompilerParams(vmem_limit_bytes=2 << 20),
        cost_estimate=pl.CostEstimate(
            flops=0, transcendentals=0, bytes_accessed=2 * weight.size * 2
        ),
    )(place, pltpu.with_memory_space_constraint(weight, pltpu.HBM))


def attend_kernel(heads, rows, count, *refs):
    riders, ins, outs = refs[: -2 * count], refs[-2 * count : -count], refs[-count:]
    width = heads * 3 * HEAD
    blocks = [unpack_tiles(ref, rows, width) for ref in ins]

    def columns(start):
        first, offset = divmod(start, LANES)
        parts = []
        for tiles in blocks:
            if offset + HEAD <= LANES:
                parts.append(tiles[first][:, offset : offset + HEAD])
            else:
                wide = jnp.concatenate([tiles[first], tiles[first + 1]], axis=1)
                parts.append(wide[:, offset : offset + HEAD])
        return jnp.concatenate(parts, axis=0)

    results = []
    for h in range(heads):
        start = h * 3 * HEAD
        query, key, value = (columns(start + i * HEAD) for i in range(3))
        scores = lax.dot_general(
            query, key, (((1,), (1,)), ((), ())), preferred_element_type=jnp.float32
        )
        row_max = jnp.max(scores, axis=-1, keepdims=True)
        exp_scores = jnp.exp2((scores - row_max) * (HEAD ** (-0.5) / math.log(2.0)))
        row_sum = jnp.sum(exp_scores, axis=-1, keepdims=True)
        summed = jnp.dot(
            exp_scores.astype(jnp.bfloat16), value, preferred_element_type=jnp.float32
        )
        results.append(summed / row_sum)
    attended = jnp.concatenate(results, axis=1).astype(jnp.bfloat16)
    whole = heads * HEAD // LANES
    for b in range(count):
        mine = attended[b * rows : (b + 1) * rows]
        for t in range(whole):
            outs[b][t * rows : (t + 1) * rows, :] = mine[:, t * LANES : (t + 1) * LANES]
        rest = mine[:, whole * LANES :].astype(jnp.float32)
        packed = rows * heads * HEAD // LANES
        outs[b][whole * rows : packed, :] = jnp.concatenate(
            [rest[: rows // 2], rest[rows // 2 :]], axis=1
        ).astype(jnp.bfloat16)
        if riders:
            mod_ref, other_ref = riders
            put_modulation(outs[b], packed, mod_ref[0:1, :])
            packed += MOD_ROWS
            outs[b][packed : packed + MOD_ROWS, :] = other_ref[other_ref.shape[0] - MOD_ROWS :, :]


def attend_packed(pieces, heads, rows, riders=()):
    count = len(pieces)
    total = count * rows
    length = rows * heads * HEAD // LANES
    specs = [pl.BlockSpec(memory_space=pltpu.VMEM)] * (count + len(riders))
    if riders:
        length += MOD_ROWS * len(riders)
    out = jax.ShapeDtypeStruct((length, LANES), jnp.bfloat16)
    return pl.pallas_call(
        functools.partial(attend_kernel, heads, rows, count),
        in_specs=specs,
        out_shape=[out] * count,
        compiler_params=pltpu.CompilerParams(vmem_limit_bytes=12 << 20),
        cost_estimate=pl.CostEstimate(
            flops=4 * heads * total * total * HEAD,
            transcendentals=heads * total * total,
            bytes_accessed=8 * total * heads * HEAD,
        ),
    )(*riders, *pieces)


def gather_left(refs, left_ref, rows):
    depth = left_ref.shape[1] // len(refs)
    left_ref[...] = jnp.concatenate(
        [jnp.concatenate(unpack_tiles(ref, rows, depth), axis=1)[:, :depth] for ref in refs],
        axis=1,
    )


def project_kernel(rows, first, slots, w_ref, *refs):
    pieces, rest = refs[: len(slots)], refs[len(slots) :]
    out_ref, left_ref = rest[-2:]
    gather_left(pieces, left_ref, rows)
    depth = left_ref.shape[1] // len(slots)
    tile = math.gcd(out_ref.shape[1], 5 * LANES)
    for start in range(0, out_ref.shape[1], tile):
        cut = slice(first + start, first + start + tile)
        here = slice(start, start + tile)
        right = [w_ref[r * depth : (r + 1) * depth, cut] for r in slots]
        term = jnp.dot(
            left_ref[...], jnp.concatenate(right, axis=0), preferred_element_type=jnp.float32
        )
        if len(rest) == 3:
            term = rest[0][:, here] + term
        out_ref[:, here] = term.astype(out_ref.dtype)


def project_packed(pieces, slots, count, weight, rows, first, dim, dtype, base=()):
    depth = weight.shape[0] // count
    held = pltpu.with_memory_space_constraint(weight, pltpu.VMEM)
    inputs = (*pieces, *base)
    return pl.pallas_call(
        functools.partial(project_kernel, rows, first, slots),
        in_specs=[pl.BlockSpec(memory_space=pltpu.VMEM)] * (1 + len(inputs)),
        out_shape=jax.ShapeDtypeStruct((rows, dim), dtype),
        scratch_shapes=[pltpu.VMEM((rows, depth * len(slots)), jnp.bfloat16)],
        compiler_params=pltpu.CompilerParams(vmem_limit_bytes=16 << 20),
        cost_estimate=pl.CostEstimate(
            flops=2 * rows * depth * len(slots) * dim,
            transcendentals=0,
            bytes_accessed=2 * depth * len(slots) * dim,
        ),
    )(held, *inputs)


def finish_kernel(rows, near_ref, *refs):
    far, refs = refs[:2], refs[2:]
    mod_ref, hidden_ref, head_ref, latent_ref, clock_ref, out_ref, step_ref = refs[:7]
    acc_ref, turn_ref = refs[7:]
    steps, _, tile = acc_ref.shape
    dim = steps * tile

    def modulation(which, i):
        start = which * dim + i * tile
        line, offset = divmod(start, mod_ref.shape[2])
        return mod_ref[line, :, offset : offset + tile]

    total = jnp.zeros((rows, 1), jnp.float32)
    for i in range(steps):
        cut = slice(i * tile, (i + 1) * tile)
        side, offset = divmod(i * tile, dim // 2)
        projected = near_ref[:, cut] + far[side][:, offset : offset + tile].astype(jnp.float32)
        part = hidden_ref[:, cut].astype(jnp.float32) + modulation(0, i) * projected
        acc_ref[i] = part
        total += jnp.sum(part, axis=-1, keepdims=True)
    average = total / dim
    square = jnp.zeros((rows, 1), jnp.float32)
    for i in range(steps):
        centred = acc_ref[i] - average
        square += jnp.sum(centred * centred, axis=-1, keepdims=True)
    rate = lax.rsqrt(square / dim + 1e-06)
    velocity = jnp.zeros(turn_ref.shape, jnp.float32)
    for i in range(steps):
        cut = slice(i * tile, (i + 1) * tile)
        normed = (
            (acc_ref[i] - average) * rate * (1.0 + modulation(2, i)) + modulation(1, i)
        ).astype(jnp.bfloat16)
        velocity += lax.dot_general(
            normed,
            head_ref[:, cut],
            (((1,), (1,)), ((), ())),
            preferred_element_type=jnp.float32,
        )
    turn_ref[...] = velocity
    paired = jnp.concatenate(
        [turn_ref[pl.ds(0, rows // 2, stride=2), :], turn_ref[pl.ds(1, rows // 2, stride=2), :]],
        axis=1,
    )
    out_ref[...] = paired
    step_ref[...] = latent_ref[...] + clock_ref[1:2, :] * paired


def finish(near, far, hidden, lines, head_rows, latent, clock):
    rows, dim = near.shape
    tile = math.gcd(dim // 2, lines.shape[2])
    patch = head_rows.shape[0]
    inputs = (near, *far, lines, hidden, head_rows, latent, clock)
    result = jax.ShapeDtypeStruct((rows // 2, 2 * patch), jnp.float32)
    return pl.pallas_call(
        functools.partial(finish_kernel, rows),
        in_specs=[pl.BlockSpec(memory_space=pltpu.VMEM)] * len(inputs),
        out_shape=[result] * 2,
        scratch_shapes=[
            pltpu.VMEM((dim // tile, rows, tile), jnp.float32),
            pltpu.VMEM((rows, patch), jnp.float32),
        ],
        compiler_params=pltpu.CompilerParams(vmem_limit_bytes=8 << 20),
        cost_estimate=pl.CostEstimate(
            flops=2 * rows * patch * dim, transcendentals=0, bytes_accessed=8 * rows * dim
        ),
    )(*inputs)


def collect_kernel(starts, *refs):
    out_ref = refs[-1]
    span = out_ref.shape[0] // len(starts)
    for k, (which, start) in enumerate(starts):
        out_ref[k * span : (k + 1) * span, :] = refs[which][start : start + span, :]


def collect(pieces, starts, span):
    return pl.pallas_call(
        functools.partial(collect_kernel, starts),
        in_specs=[pl.BlockSpec(memory_space=pltpu.VMEM)] * len(pieces),
        out_shape=jax.ShapeDtypeStruct((len(starts) * span, LANES), jnp.bfloat16),
        compiler_params=pltpu.CompilerParams(vmem_limit_bytes=4 << 20),
        cost_estimate=pl.CostEstimate(
            flops=0, transcendentals=0, bytes_accessed=4 * len(starts) * span * LANES
        ),
    )(*pieces)


def line_kernel(starts, *refs):
    pieces, (mod_ref, out_ref) = refs[:-2], refs[-2:]
    span = (out_ref.shape[0] - MOD_ROWS) // len(starts)
    for k, start in enumerate(starts):
        out_ref[k * span : (k + 1) * span, :] = pieces[k][start : start + span, :]
    put_modulation(out_ref, out_ref.shape[0] - MOD_ROWS, mod_ref[1:2, :])


def collect_line(pieces, starts, span, modulation):
    return pl.pallas_call(
        functools.partial(line_kernel, starts),
        in_specs=[pl.BlockSpec(memory_space=pltpu.VMEM)] * (len(pieces) + 1),
        out_shape=jax.ShapeDtypeStruct((len(starts) * span + MOD_ROWS, LANES), jnp.bfloat16),
        compiler_params=pltpu.CompilerParams(vmem_limit_bytes=4 << 20),
        cost_estimate=pl.CostEstimate(
            flops=0, transcendentals=0, bytes_accessed=4 * len(starts) * span * LANES
        ),
    )(*pieces, modulation)


def arrange_kernel(count, width, done, place_ref, half_ref, group_ref, *refs):
    mine_ref, up_ref, mod_ref, other_ref = refs[:4]
    near = refs[4:-2]
    head_out, mod_out = refs[-2:]
    span = mine_ref.shape[0] // (2 * count)
    cut = head_out.shape[0] // 2
    tiles = span // cut
    first = half_ref[0] == 0
    lower = group_ref[0] == 0
    columns = mod_ref.shape[1]

    def block(ref, k):
        parts = [ref[k * span + t * cut : k * span + (t + 1) * cut, :] for t in range(tiles)]
        return jnp.concatenate(parts, axis=1)[:, :width]

    def whole(k):
        mine, up = block(mine_ref, k), block(up_ref, k)
        return jnp.concatenate(
            [jnp.where(lower, mine, up), jnp.where(lower, up, mine)], axis=0
        )

    for r in range(count):
        owner = place_ref[0] ^ r
        own, other = whole(r), whole(count + r)
        start = pl.multiple_of(owner * 2 * width, LANES)
        head_out[:, pl.ds(start, 2 * width)] = jnp.concatenate(
            [jnp.where(first, own, other), jnp.where(first, other, own)], axis=1
        )
        if r == 0:
            own = mod_ref[0:1, :]
            other = get_modulation(other_ref, other_ref.shape[0] - MOD_ROWS, columns)
        else:
            own = get_modulation(near[r], done, columns)
            other = get_modulation(near[r], done + MOD_ROWS, columns)
        mod_out[owner] = jnp.concatenate(
            [jnp.where(first, own, other), jnp.where(first, other, own)], axis=1
        )


def arrange(mine, up, modulation, other, near, head, scalars, done):
    count = len(near)
    patch, width = head.shape
    columns = modulation.shape[1]
    return pl.pallas_call(
        functools.partial(arrange_kernel, count, width, done),
        in_specs=[pl.BlockSpec(memory_space=pltpu.SMEM)] * 3
        + [pl.BlockSpec(memory_space=pltpu.VMEM)] * (4 + count),
        out_shape=[
            jax.ShapeDtypeStruct((patch, 2 * count * width), jnp.bfloat16),
            jax.ShapeDtypeStruct((count, 1, 2 * columns), jnp.float32),
        ],
        compiler_params=pltpu.CompilerParams(vmem_limit_bytes=4 << 20),
        cost_estimate=pl.CostEstimate(
            flops=0, transcendentals=0, bytes_accessed=8 * count * patch * width
        ),
    )(*scalars, mine, up, modulation, other, *near)


def packed_body(head_inputs, hidden, out_weight, time_weight, head_weight, latent, timesteps):
    count = lax.axis_size("seq")
    halves = lax.axis_size("fsdp")
    rows = head_inputs.shape[2]
    place = lax.axis_index("seq")
    half = lax.axis_index("fsdp")
    group = lax.axis_index("grp")
    heads = HEADS // halves // count

    def along(block, r):
        return lax.ppermute(block, "seq", [(i, i ^ r) for i in range(count)])

    def swap(block, axis):
        return lax.ppermute(block, axis, [(0, 1), (1, 0)])

    def slanted(block, r):
        route = []
        for i in range(count):
            for j in range(halves):
                route.append((i * halves + j, (i ^ r) * halves + 1 - j))
        return lax.ppermute(block, ("seq", "fsdp"), route)

    x = head_inputs.reshape(rows, head_inputs.shape[3])
    head = jnp.swapaxes(head_weight[0], 0, 1)
    span = head.shape[0] // 2 * head_tiles(head.shape[1])
    here = place[None].astype(jnp.int32)
    side = half[None].astype(jnp.int32)
    level = group[None].astype(jnp.int32)
    scalars = (here, side, level)
    last = count // 2
    slots = [r for r in range(count - 1, 0, -1) if r != last] + [0]
    first, pack = split_first(x, head, scalars, last, count, halves)
    sent, clock = split_far(x, pack, timesteps.reshape(1, 2), scalars, slots, 1, count, halves)
    far_sent = [first if r == last else sent[slots.index(r)] for r in range(count)]
    far_pieces = [slanted(far_sent[r], r) for r in range(count)]

    other_steps = swap(timesteps, "fsdp")
    freqs = jnp.exp(
        -math.log(10000.0) * jnp.arange(FREQ // 2, dtype=jnp.float32) / (FREQ // 2)
    )
    angle = jnp.concatenate([clock[:1], jnp.full((1, LANES), other_steps[0, 0, 0], jnp.float32)])
    angle = angle * freqs
    embedding = jnp.concatenate([jnp.cos(angle), jnp.sin(angle)], axis=-1).astype(jnp.bfloat16)
    modulation = jnp.dot(embedding, time_weight[0], preferred_element_type=jnp.float32)

    near_sent = split_near(x, scalars, count, halves)
    near_pieces = [near_sent[0]] + [along(near_sent[r], r) for r in range(1, count)]

    weight = load_rows(out_weight[0], here, count)
    far_attended = attend_packed(far_pieces, heads, rows)
    far_home = [far_attended[0]]
    far_home += [along(far_attended[r], r) for r in range(1, count)]
    part = DIM // 2
    partial = []
    for k in range(2):
        term = project_packed(
            far_home, range(count), count, weight, rows, k * part, part, jnp.bfloat16
        )
        partial.append(swap(term, "fsdp"))

    packed = near_sent[0].shape[0]
    relay = collect([far_pieces[2]], [(0, packed)], span)
    relayed = along(relay, 1)
    line = collect_line(
        [pack, far_pieces[1], far_pieces[2], relayed], [0, packed, packed, 0], span, modulation
    )
    other = swap(line, "fsdp")
    own_slots = [(0 if r == 0 else 1, r * span) for r in range(count)]
    far_slots = [(1 if r == 0 else 0, r * span) for r in range(count)]
    mine = collect([line, other], own_slots + far_slots, span)
    up = swap(mine, "grp")
    near_attended = attend_packed(near_pieces, heads, rows, (modulation, other))
    near_home = [near_attended[0]]
    near_home += [along(near_attended[r], r) for r in range(1, count)]
    done = near_home[0].shape[0] - 2 * MOD_ROWS
    head_rows, lines = arrange(mine, up, modulation, other, near_home, head, scalars, done)
    others = [r for r in range(count) if r != 1]
    most = project_packed(
        [near_home[r] for r in others], others, count, weight, rows, 0, DIM, jnp.float32
    )
    projected = project_packed(
        [near_home[1]], [1], count, weight, rows, 0, DIM, jnp.float32, (most,)
    )
    velocity, stepped = finish(
        projected,
        partial,
        hidden.reshape(rows, DIM),
        lines,
        head_rows,
        latent.reshape(rows // 2, 2 * PATCH),
        clock,
    )
    carried = partner(stepped, "section", 0)
    return (velocity.reshape(latent.shape), carried.reshape(latent.shape))


def packed_fits(mesh, head_shape):
    count, halves = mesh.shape["seq"], mesh.shape["fsdp"]
    rows = head_shape[2]
    return (
        head_shape[1] == 1
        and halves == 2
        and FREQ == 2 * LANES
        and 2 * PATCH == LANES
        and mesh.shape["grp"] == 2
        and count == 4
        and HEADS % (halves * count) == 0
        and 3 * DIM // (halves * count) <= 8 * LANES
        and DIM % (halves * count) == 0
        and HEADS // (halves * count) * HEAD % LANES == LANES // 2
        and rows % 32 == 0
        and rows * count <= 512
    )


def step(mesh, body):
    return jax.shard_map(
        body,
        mesh=mesh,
        in_specs=(
            P("section", ("grp", "fsdp"), "seq", None),
            P("section", ("grp", "fsdp"), "seq", None),
            P("section", "fsdp", None),
            P("section", None, ("seq", "fsdp")),
            P("section", ("seq", "fsdp"), None),
            P("section", ("grp", "fsdp"), "seq", None),
            P("section", ("grp", "fsdp"), None),
        ),
        out_specs=(
            P("section", ("grp", "fsdp"), "seq", None),
            P("section", ("grp", "fsdp"), "seq", None),
        ),
        check_vma=False,
    )


def solution(mesh):
    def choose(head_inputs, *rest):
        local = (
            head_inputs.shape[0] // mesh.shape["section"],
            head_inputs.shape[1] // mesh.shape["grp"] // mesh.shape["fsdp"],
            head_inputs.shape[2] // mesh.shape["seq"],
        )
        if not packed_fits(mesh, local):
            return step(mesh, general_body)(head_inputs, *rest)
        return step(mesh, packed_body)(head_inputs, *rest)

    return choose
```

```python
import functools
import math

import jax
import jax.numpy as jnp
from jax import lax
from jax.experimental import pallas as pl
from jax.experimental.pallas import tpu as pltpu
from jax.sharding import PartitionSpec as P


DIM = 2560
HEADS = 32
HEAD = 80
PATCH = 64
FREQ = 256
LANES = 128


def partner(block, axis, apart):
    count = lax.axis_size(axis)
    route = []
    for low in range(count):
        high = low | 1 << apart
        if high != low and high < count:
            route += [(low, high), (high, low)]
    return lax.ppermute(block, axis, route)


def time_embed(steps_now):
    half = FREQ // 2
    freqs = jnp.exp(-math.log(10000.0) * jnp.arange(half, dtype=jnp.float32) / half)
    angle = steps_now.astype(jnp.float32)[..., None] * freqs
    return jnp.concatenate([jnp.cos(angle), jnp.sin(angle)], axis=-1)


def sigma_of(steps_now):
    unit_time = steps_now.astype(jnp.float32) / 1000.0
    return 5.0 * unit_time / (1.0 + 4.0 * unit_time)


def attend(exchanged):
    items = exchanged.shape[0]
    length = exchanged.shape[1]
    local_heads = exchanged.shape[2]
    query_all = exchanged[..., :HEAD]
    key_rows = exchanged[..., HEAD : 2 * HEAD]
    value_rows = exchanged[..., 2 * HEAD :]
    block_rows = min(512, length)
    block_count = length // block_rows

    def one_block(block_index):
        query_block = lax.dynamic_slice_in_dim(query_all, block_index * block_rows, block_rows, 1)
        scores = jnp.einsum(
            "nqhe,nkhe->nhqk", query_block, key_rows, preferred_element_type=jnp.float32
        ) * HEAD ** (-0.5)
        row_max = jnp.max(scores, axis=-1, keepdims=True)
        exp_scores = jnp.exp(scores - row_max)
        row_sum = jnp.sum(exp_scores, axis=-1, keepdims=True)
        weights = (exp_scores / row_sum).astype(jnp.bfloat16)
        return jnp.einsum(
            "nhqk,nkhe->nqhe", weights, value_rows, preferred_element_type=jnp.float32
        ).astype(jnp.bfloat16)

    blocks = lax.map(one_block, jnp.arange(block_count, dtype=jnp.int32))
    return blocks.transpose(1, 0, 2, 3, 4).reshape(items, length, local_heads * HEAD)


def general_body(head_inputs, hidden, out_weight, time_weight, head_weight, latent, timesteps):
    samples = head_inputs.shape[1]
    row_count = head_inputs.shape[2]
    flat_count = samples * row_count
    local = head_inputs.reshape(samples, row_count, HEADS, 3 * HEAD)
    attended = lax.all_to_all(
        attend(lax.all_to_all(local, "seq", split_axis=2, concat_axis=1, tiled=True)),
        "seq",
        split_axis=1,
        concat_axis=2,
        tiled=True,
    )
    flattened = attended.reshape(flat_count, HEADS * HEAD)
    time_full, head_full = (
        lax.all_gather(time_weight, ("seq", "fsdp"), axis=2, tiled=True),
        lax.all_gather(head_weight, ("seq", "fsdp"), axis=1, tiled=True),
    )
    embedding = time_embed(timesteps[0, :, 0]).astype(jnp.bfloat16)
    modulation = jnp.dot(embedding, time_full[0], preferred_element_type=jnp.float32)
    gate_term = modulation[:, None, :DIM]
    shift_term = modulation[:, None, DIM : 2 * DIM]
    scale_term = modulation[:, None, 2 * DIM :]
    own_columns = lax.all_to_all(flattened, "fsdp", split_axis=1, concat_axis=0, tiled=True)
    projected = lax.psum_scatter(
        jnp.dot(own_columns, out_weight[0], preferred_element_type=jnp.float32).astype(
            jnp.bfloat16
        ),
        "fsdp",
        scatter_dimension=0,
        tiled=True,
    ).astype(jnp.float32)
    updated = hidden.reshape(samples, row_count, DIM).astype(
        jnp.float32
    ) + gate_term * projected.reshape(samples, row_count, DIM)
    average = jnp.mean(updated, axis=-1, keepdims=True)
    centred = updated - average
    variance = jnp.mean(centred * centred, axis=-1, keepdims=True)
    normed = (centred * lax.rsqrt(variance + 1e-06) * (1.0 + scale_term) + shift_term).astype(
        jnp.bfloat16
    )
    velocity = jnp.dot(
        normed.reshape(flat_count, DIM), head_full[0], preferred_element_type=jnp.float32
    )
    velocity = velocity.reshape(1, samples, row_count // 2, 2 * PATCH)
    step_size = sigma_of(timesteps[0, :, 1]) - sigma_of(timesteps[0, :, 0])
    stepped = latent + step_size[None, :, None, None] * velocity
    carried = partner(stepped, "section", 0)
    return (velocity, carried)


def turn(half):
    return pltpu.roll(half.astype(jnp.float32), LANES // 2, 1)


def pack_half(tile):
    rows = tile.shape[0]
    wide = tile.astype(jnp.float32)
    lane = lax.broadcasted_iota(jnp.int32, (rows // 2, LANES), 1)
    return jnp.where(
        lane < LANES // 2, wide[: rows // 2], pltpu.roll(wide[rows // 2 :], LANES // 2, 1)
    ).astype(jnp.bfloat16)


def unpack_tiles(ref, rows, width):
    whole = width // LANES
    tiles = [ref[t * rows : (t + 1) * rows, :] for t in range(whole)]
    last = ref[whole * rows : whole * rows + rows // 2, :]
    tiles.append(jnp.concatenate([last, turn(last).astype(jnp.bfloat16)], axis=0))
    return tiles


def head_tiles(width):
    return -(-width // LANES)


MOD_ROWS = 16


def put_modulation(out, at, row):
    width = row.shape[1]
    tiles = -(-width // LANES)
    left = jnp.concatenate([row, jnp.zeros((1, tiles * LANES - width), jnp.float32)], axis=1)
    left = jnp.concatenate(
        [left[:, t * LANES : (t + 1) * LANES] for t in range(tiles)]
        + [jnp.zeros((8 - tiles, LANES), jnp.float32)][: 8 - tiles],
        axis=0,
    )
    high = left.astype(jnp.bfloat16)
    low = (left - high.astype(jnp.float32)).astype(jnp.bfloat16)
    out[at : at + MOD_ROWS, :] = jnp.concatenate([high, low], axis=0)


def get_modulation(ref, at, width):
    terms = ref[at : at + MOD_ROWS, :].astype(jnp.float32)
    total = terms[0:8] + terms[8:16]
    tiles = -(-width // LANES)
    return jnp.concatenate([total[t : t + 1] for t in range(tiles)], axis=1)[:, :width]


def cut_window(width, held, out, r, odd):
    rows = held.shape[1]
    whole = width // LANES
    last = slice(whole * rows, rows * width // LANES)

    @pl.when(jnp.logical_not(odd))
    def _():
        for t in range(whole):
            out[t * rows : (t + 1) * rows, :] = held[r, :, t * LANES : (t + 1) * LANES]
        out[last, :] = pack_half(held[r, :, whole * LANES :])

    @pl.when(odd)
    def _():
        lane = lax.broadcasted_iota(jnp.int32, (rows, LANES), 1)
        turned = [turn(held[r, :, t * LANES : (t + 1) * LANES]) for t in range(whole + 1)]
        for t in range(whole):
            out[t * rows : (t + 1) * rows, :] = jnp.where(
                lane < LANES // 2, turned[t], turned[t + 1]
            ).astype(jnp.bfloat16)
        out[last, :] = pack_half(turned[whole])


def windows(x_ref, held, sems, me, half, count, width, slots):
    span = held.shape[2]

    def window(k, r):
        start = half * (count * width) + lax.div((me ^ r) * width, LANES) * LANES
        return pltpu.make_async_copy(
            x_ref.at[:, pl.ds(pl.multiple_of(start, LANES), span)], held.at[k], sems.at[k]
        )

    return [window(k, r) for k, r in enumerate(slots)]


def sigma_row(step):
    unit_time = jnp.full((1, LANES), step, jnp.int32).astype(jnp.float32) / 1000.0
    return 5.0 * unit_time / (1.0 + 4.0 * unit_time)


def first_kernel(width, count, slot, place_ref, half_ref, group_ref, x_ref, head_ref, *refs):
    out_ref, pack_ref, held, head_held, sems, head_sem = refs
    me = place_ref[0]
    cut, columns = head_held.shape
    copy = windows(x_ref, held, sems, me, 1 - half_ref[0], count, width, [slot])[0]
    head_copy = pltpu.make_async_copy(
        head_ref.at[pl.ds(pl.multiple_of(group_ref[0] * cut, cut), cut), :], head_held, head_sem
    )
    head_copy.start()
    copy.start()
    head_copy.wait()
    packed = out_ref.shape[0] - pack_ref.shape[0]
    for t in range(head_tiles(columns)):
        tile = head_held[:, t * LANES : min((t + 1) * LANES, columns)]
        if tile.shape[1] < LANES:
            fill = jnp.zeros((cut, LANES - tile.shape[1]), tile.dtype)
            tile = jnp.concatenate([tile, fill], axis=1)
        pack_ref[t * cut : (t + 1) * cut, :] = tile
        out_ref[packed + t * cut : packed + (t + 1) * cut, :] = tile
    copy.wait()
    cut_window(width, held, out_ref, 0, lax.rem(me ^ slot, 2) == 1)


def split_first(x, head, scalars, slot, count, halves):
    rows, columns = x.shape
    width = columns // halves // count
    cut = head.shape[0] // 2
    span = cut * head_tiles(head.shape[1])
    length = rows * width // LANES
    return pl.pallas_call(
        functools.partial(first_kernel, width, count, slot),
        in_specs=[pl.BlockSpec(memory_space=pltpu.SMEM)] * 3
        + [pl.BlockSpec(memory_space=pltpu.HBM)] * 2,
        out_shape=[
            jax.ShapeDtypeStruct((length + span, LANES), jnp.bfloat16),
            jax.ShapeDtypeStruct((span, LANES), jnp.bfloat16),
        ],
        scratch_shapes=[
            pltpu.VMEM((1, rows, (width // LANES + 1) * LANES), jnp.bfloat16),
            pltpu.VMEM((cut, head.shape[1]), jnp.bfloat16),
            pltpu.SemaphoreType.DMA((1,)),
            pltpu.SemaphoreType.DMA,
        ],
        compiler_params=pltpu.CompilerParams(vmem_limit_bytes=4 << 20),
        cost_estimate=pl.CostEstimate(
            flops=0, transcendentals=0, bytes_accessed=4 * rows * width
        ),
    )(
        *scalars,
        pltpu.with_memory_space_constraint(x, pltpu.HBM),
        pltpu.with_memory_space_constraint(head, pltpu.HBM),
    )


def far_kernel(width, count, slots, rider, place_ref, half_ref, when_ref, x_ref, pack_ref, *refs):
    outs, (clock_ref, held, steps_ref, sems, steps_sem) = refs[: len(slots)], refs[len(slots) :]
    me = place_ref[0]
    copies = windows(x_ref, held, sems, me, 1 - half_ref[0], count, width, slots)
    steps_copy = pltpu.make_async_copy(when_ref, steps_ref, steps_sem)
    for copy in copies:
        copy.start()
    steps_copy.start()
    packed = held.shape[1] * width // LANES
    outs[slots.index(rider)][packed:, :] = pack_ref[...]
    for k, r in enumerate(slots):
        copies[k].wait()
        cut_window(width, held, outs[k], k, lax.rem(me ^ r, 2) == 1)
    steps_copy.wait()
    now = jnp.full((1, LANES), steps_ref[0, 0], jnp.int32).astype(jnp.float32)
    change = sigma_row(steps_ref[0, 1]) - sigma_row(steps_ref[0, 0])
    clock_ref[...] = jnp.concatenate([now, change])


def split_far(x, pack, steps, scalars, slots, rider, count, halves):
    rows, columns = x.shape
    width = columns // halves // count
    length = rows * width // LANES
    results = pl.pallas_call(
        functools.partial(far_kernel, width, count, slots, rider),
        in_specs=[pl.BlockSpec(memory_space=pltpu.SMEM)] * 2
        + [pl.BlockSpec(memory_space=pltpu.HBM)] * 2
        + [pl.BlockSpec(memory_space=pltpu.VMEM)],
        out_shape=[
            jax.ShapeDtypeStruct((length + pack.shape[0] * (r == rider), LANES), jnp.bfloat16)
            for r in slots
        ]
        + [jax.ShapeDtypeStruct((2, LANES), jnp.float32)],
        scratch_shapes=[
            pltpu.VMEM((len(slots), rows, (width // LANES + 1) * LANES), jnp.bfloat16),
            pltpu.SMEM((1, 2), jnp.int32),
            pltpu.SemaphoreType.DMA((len(slots),)),
            pltpu.SemaphoreType.DMA,
        ],
        compiler_params=pltpu.CompilerParams(vmem_limit_bytes=4 << 20),
        cost_estimate=pl.CostEstimate(
            flops=0, transcendentals=0, bytes_accessed=4 * rows * columns // halves
        ),
    )(
        *scalars[:2],
        pltpu.with_memory_space_constraint(steps, pltpu.HBM),
        pltpu.with_memory_space_constraint(x, pltpu.HBM),
        pack,
    )
    return results[:-1], results[-1]


def near_kernel(width, count, place_ref, half_ref, x_ref, *refs):
    outs, held, sems = refs[:count], refs[count], refs[count + 1]
    me = place_ref[0]
    copies = windows(x_ref, held, sems, me, half_ref[0], count, width, range(count))
    for r in range(count - 1, -1, -1):
        copies[r].start()
    for r in range(count - 1, -1, -1):
        copies[r].wait()
        cut_window(width, held, outs[r], r, lax.rem(me ^ r, 2) == 1)


def split_near(x, scalars, count, halves):
    rows, columns = x.shape
    width = columns // halves // count
    length = rows * width // LANES
    return pl.pallas_call(
        functools.partial(near_kernel, width, count),
        in_specs=[pl.BlockSpec(memory_space=pltpu.SMEM)] * 2
        + [pl.BlockSpec(memory_space=pltpu.HBM)],
        out_shape=[jax.ShapeDtypeStruct((length, LANES), jnp.bfloat16)] * count,
        scratch_shapes=[
            pltpu.VMEM((count, rows, (width // LANES + 1) * LANES), jnp.bfloat16),
            pltpu.SemaphoreType.DMA((count,)),
        ],
        compiler_params=pltpu.CompilerParams(vmem_limit_bytes=4 << 20),
        cost_estimate=pl.CostEstimate(
            flops=0, transcendentals=0, bytes_accessed=4 * rows * columns // halves
        ),
    )(*scalars[:2], pltpu.with_memory_space_constraint(x, pltpu.HBM))


def load_kernel(count, place_ref, w_ref, out_ref, sems):
    depth = w_ref.shape[0] // count

    def block(r):
        owner = place_ref[0] ^ r
        return pltpu.make_async_copy(
            w_ref.at[pl.ds(pl.multiple_of(owner * depth, depth), depth), :],
            out_ref.at[r * depth : (r + 1) * depth, :],
            sems.at[r],
        )

    for r in range(count):
        block(r).start()
    for r in range(count):
        block(r).wait()


def load_rows(weight, place, count):
    return pl.pallas_call(
        functools.partial(load_kernel, count),
        in_specs=[
            pl.BlockSpec(memory_space=pltpu.SMEM),
            pl.BlockSpec(memory_space=pltpu.HBM),
        ],
        out_specs=pl.BlockSpec(memory_space=pltpu.VMEM),
        out_shape=pltpu.VMEM(weight.shape, weight.dtype),
        scratch_shapes=[pltpu.SemaphoreType.DMA((count,))],
        compiler_params=pltpu.CompilerParams(vmem_limit_bytes=2 << 20),
        cost_estimate=pl.CostEstimate(
            flops=0, transcendentals=0, bytes_accessed=2 * weight.size * 2
        ),
    )(place, pltpu.with_memory_space_constraint(weight, pltpu.HBM))


def attend_kernel(heads, rows, count, *refs):
    riders, ins, outs = refs[: -2 * count], refs[-2 * count : -count], refs[-count:]
    width = heads * 3 * HEAD
    blocks = [unpack_tiles(ref, rows, width) for ref in ins]

    def columns(start):
        first, offset = divmod(start, LANES)
        parts = []
        for tiles in blocks:
            if offset + HEAD <= LANES:
                parts.append(tiles[first][:, offset : offset + HEAD])
            else:
                wide = jnp.concatenate([tiles[first], tiles[first + 1]], axis=1)
                parts.append(wide[:, offset : offset + HEAD])
        return jnp.concatenate(parts, axis=0)

    results = []
    for h in range(heads):
        start = h * 3 * HEAD
        query, key, value = (columns(start + i * HEAD) for i in range(3))
        scores = lax.dot_general(
            query, key, (((1,), (1,)), ((), ())), preferred_element_type=jnp.float32
        )
        row_max = jnp.max(scores, axis=-1, keepdims=True)
        exp_scores = jnp.exp2((scores - row_max) * (HEAD ** (-0.5) / math.log(2.0)))
        row_sum = jnp.sum(exp_scores, axis=-1, keepdims=True)
        summed = jnp.dot(
            exp_scores.astype(jnp.bfloat16), value, preferred_element_type=jnp.float32
        )
        results.append(summed / row_sum)
    attended = jnp.concatenate(results, axis=1).astype(jnp.bfloat16)
    whole = heads * HEAD // LANES
    for b in range(count):
        mine = attended[b * rows : (b + 1) * rows]
        for t in range(whole):
            outs[b][t * rows : (t + 1) * rows, :] = mine[:, t * LANES : (t + 1) * LANES]
        rest = mine[:, whole * LANES :].astype(jnp.float32)
        packed = rows * heads * HEAD // LANES
        outs[b][whole * rows : packed, :] = jnp.concatenate(
            [rest[: rows // 2], rest[rows // 2 :]], axis=1
        ).astype(jnp.bfloat16)
        if riders:
            mod_ref, other_ref = riders
            put_modulation(outs[b], packed, mod_ref[0:1, :])
            packed += MOD_ROWS
            outs[b][packed : packed + MOD_ROWS, :] = other_ref[other_ref.shape[0] - MOD_ROWS :, :]


def attend_packed(pieces, heads, rows, riders=()):
    count = len(pieces)
    total = count * rows
    length = rows * heads * HEAD // LANES
    specs = [pl.BlockSpec(memory_space=pltpu.VMEM)] * (count + len(riders))
    if riders:
        length += MOD_ROWS * len(riders)
    out = jax.ShapeDtypeStruct((length, LANES), jnp.bfloat16)
    return pl.pallas_call(
        functools.partial(attend_kernel, heads, rows, count),
        in_specs=specs,
        out_shape=[out] * count,
        compiler_params=pltpu.CompilerParams(vmem_limit_bytes=12 << 20),
        cost_estimate=pl.CostEstimate(
            flops=4 * heads * total * total * HEAD,
            transcendentals=heads * total * total,
            bytes_accessed=8 * total * heads * HEAD,
        ),
    )(*riders, *pieces)


def gather_left(refs, left_ref, rows):
    depth = left_ref.shape[1] // len(refs)
    left_ref[...] = jnp.concatenate(
        [jnp.concatenate(unpack_tiles(ref, rows, depth), axis=1)[:, :depth] for ref in refs],
        axis=1,
    )


def project_kernel(rows, first, slots, w_ref, *refs):
    pieces, rest = refs[: len(slots)], refs[len(slots) :]
    out_ref, left_ref = rest[-2:]
    gather_left(pieces, left_ref, rows)
    depth = left_ref.shape[1] // len(slots)
    tile = math.gcd(out_ref.shape[1], 5 * LANES)
    for start in range(0, out_ref.shape[1], tile):
        cut = slice(first + start, first + start + tile)
        here = slice(start, start + tile)
        right = [w_ref[r * depth : (r + 1) * depth, cut] for r in slots]
        term = jnp.dot(
            left_ref[...], jnp.concatenate(right, axis=0), preferred_element_type=jnp.float32
        )
        if len(rest) == 3:
            term = rest[0][:, here] + term
        out_ref[:, here] = term.astype(out_ref.dtype)


def project_packed(pieces, slots, count, weight, rows, first, dim, dtype, base=()):
    depth = weight.shape[0] // count
    held = pltpu.with_memory_space_constraint(weight, pltpu.VMEM)
    inputs = (*pieces, *base)
    return pl.pallas_call(
        functools.partial(project_kernel, rows, first, slots),
        in_specs=[pl.BlockSpec(memory_space=pltpu.VMEM)] * (1 + len(inputs)),
        out_shape=jax.ShapeDtypeStruct((rows, dim), dtype),
        scratch_shapes=[pltpu.VMEM((rows, depth * len(slots)), jnp.bfloat16)],
        compiler_params=pltpu.CompilerParams(vmem_limit_bytes=16 << 20),
        cost_estimate=pl.CostEstimate(
            flops=2 * rows * depth * len(slots) * dim,
            transcendentals=0,
            bytes_accessed=2 * depth * len(slots) * dim,
        ),
    )(held, *inputs)


def finish_kernel(rows, near_ref, *refs):
    far, refs = refs[:2], refs[2:]
    mod_ref, hidden_ref, head_ref, latent_ref, clock_ref, out_ref, step_ref = refs[:7]
    acc_ref, turn_ref = refs[7:]
    steps, _, tile = acc_ref.shape
    dim = steps * tile

    def modulation(which, i):
        start = which * dim + i * tile
        line, offset = divmod(start, mod_ref.shape[2])
        return mod_ref[line, :, offset : offset + tile]

    total = jnp.zeros((rows, 1), jnp.float32)
    for i in range(steps):
        cut = slice(i * tile, (i + 1) * tile)
        bound = far[0].shape[1]
        side = int(i * tile >= bound)
        offset = i * tile - side * bound
        projected = near_ref[:, cut] + far[side][:, offset : offset + tile].astype(jnp.float32)
        part = hidden_ref[:, cut].astype(jnp.float32) + modulation(0, i) * projected
        acc_ref[i] = part
        total += jnp.sum(part, axis=-1, keepdims=True)
    average = total / dim
    square = jnp.zeros((rows, 1), jnp.float32)
    for i in range(steps):
        centred = acc_ref[i] - average
        square += jnp.sum(centred * centred, axis=-1, keepdims=True)
    rate = lax.rsqrt(square / dim + 1e-06)
    velocity = jnp.zeros(turn_ref.shape, jnp.float32)
    for i in range(steps):
        cut = slice(i * tile, (i + 1) * tile)
        normed = (
            (acc_ref[i] - average) * rate * (1.0 + modulation(2, i)) + modulation(1, i)
        ).astype(jnp.bfloat16)
        velocity += lax.dot_general(
            normed,
            head_ref[:, cut],
            (((1,), (1,)), ((), ())),
            preferred_element_type=jnp.float32,
        )
    turn_ref[...] = velocity
    paired = jnp.concatenate(
        [turn_ref[pl.ds(0, rows // 2, stride=2), :], turn_ref[pl.ds(1, rows // 2, stride=2), :]],
        axis=1,
    )
    out_ref[...] = paired
    step_ref[...] = latent_ref[...] + clock_ref[1:2, :] * paired


def finish(near, far, hidden, lines, head_rows, latent, clock):
    rows, dim = near.shape
    tile = math.gcd(far[0].shape[1], far[1].shape[1], lines.shape[2])
    patch = head_rows.shape[0]
    inputs = (near, *far, lines, hidden, head_rows, latent, clock)
    result = jax.ShapeDtypeStruct((rows // 2, 2 * patch), jnp.float32)
    return pl.pallas_call(
        functools.partial(finish_kernel, rows),
        in_specs=[pl.BlockSpec(memory_space=pltpu.VMEM)] * len(inputs),
        out_shape=[result] * 2,
        scratch_shapes=[
            pltpu.VMEM((dim // tile, rows, tile), jnp.float32),
            pltpu.VMEM((rows, patch), jnp.float32),
        ],
        compiler_params=pltpu.CompilerParams(vmem_limit_bytes=8 << 20),
        cost_estimate=pl.CostEstimate(
            flops=2 * rows * patch * dim, transcendentals=0, bytes_accessed=8 * rows * dim
        ),
    )(*inputs)


def collect_kernel(starts, *refs):
    out_ref = refs[-1]
    span = out_ref.shape[0] // len(starts)
    for k, (which, start) in enumerate(starts):
        out_ref[k * span : (k + 1) * span, :] = refs[which][start : start + span, :]


def collect(pieces, starts, span):
    return pl.pallas_call(
        functools.partial(collect_kernel, starts),
        in_specs=[pl.BlockSpec(memory_space=pltpu.VMEM)] * len(pieces),
        out_shape=jax.ShapeDtypeStruct((len(starts) * span, LANES), jnp.bfloat16),
        compiler_params=pltpu.CompilerParams(vmem_limit_bytes=4 << 20),
        cost_estimate=pl.CostEstimate(
            flops=0, transcendentals=0, bytes_accessed=4 * len(starts) * span * LANES
        ),
    )(*pieces)


def line_kernel(starts, *refs):
    pieces, (mod_ref, out_ref) = refs[:-2], refs[-2:]
    span = (out_ref.shape[0] - MOD_ROWS) // len(starts)
    for k, start in enumerate(starts):
        out_ref[k * span : (k + 1) * span, :] = pieces[k][start : start + span, :]
    put_modulation(out_ref, out_ref.shape[0] - MOD_ROWS, mod_ref[1:2, :])


def collect_line(pieces, starts, span, modulation):
    return pl.pallas_call(
        functools.partial(line_kernel, starts),
        in_specs=[pl.BlockSpec(memory_space=pltpu.VMEM)] * (len(pieces) + 1),
        out_shape=jax.ShapeDtypeStruct((len(starts) * span + MOD_ROWS, LANES), jnp.bfloat16),
        compiler_params=pltpu.CompilerParams(vmem_limit_bytes=4 << 20),
        cost_estimate=pl.CostEstimate(
            flops=0, transcendentals=0, bytes_accessed=4 * len(starts) * span * LANES
        ),
    )(*pieces, modulation)


def arrange_kernel(count, width, done, place_ref, half_ref, group_ref, *refs):
    mine_ref, up_ref, mod_ref, other_ref = refs[:4]
    near = refs[4:-2]
    head_out, mod_out = refs[-2:]
    span = mine_ref.shape[0] // (2 * count)
    cut = head_out.shape[0] // 2
    tiles = span // cut
    first = half_ref[0] == 0
    lower = group_ref[0] == 0
    columns = mod_ref.shape[1]

    def block(ref, k):
        parts = [ref[k * span + t * cut : k * span + (t + 1) * cut, :] for t in range(tiles)]
        return jnp.concatenate(parts, axis=1)[:, :width]

    def whole(k):
        mine, up = block(mine_ref, k), block(up_ref, k)
        return jnp.concatenate(
            [jnp.where(lower, mine, up), jnp.where(lower, up, mine)], axis=0
        )

    for r in range(count):
        owner = place_ref[0] ^ r
        own, other = whole(r), whole(count + r)
        start = pl.multiple_of(owner * 2 * width, LANES)
        head_out[:, pl.ds(start, 2 * width)] = jnp.concatenate(
            [jnp.where(first, own, other), jnp.where(first, other, own)], axis=1
        )
        if r == 0:
            own = mod_ref[0:1, :]
            other = get_modulation(other_ref, other_ref.shape[0] - MOD_ROWS, columns)
        else:
            own = get_modulation(near[r], done, columns)
            other = get_modulation(near[r], done + MOD_ROWS, columns)
        mod_out[owner] = jnp.concatenate(
            [jnp.where(first, own, other), jnp.where(first, other, own)], axis=1
        )


def arrange(mine, up, modulation, other, near, head, scalars, done):
    count = len(near)
    patch, width = head.shape
    columns = modulation.shape[1]
    return pl.pallas_call(
        functools.partial(arrange_kernel, count, width, done),
        in_specs=[pl.BlockSpec(memory_space=pltpu.SMEM)] * 3
        + [pl.BlockSpec(memory_space=pltpu.VMEM)] * (4 + count),
        out_shape=[
            jax.ShapeDtypeStruct((patch, 2 * count * width), jnp.bfloat16),
            jax.ShapeDtypeStruct((count, 1, 2 * columns), jnp.float32),
        ],
        compiler_params=pltpu.CompilerParams(vmem_limit_bytes=4 << 20),
        cost_estimate=pl.CostEstimate(
            flops=0, transcendentals=0, bytes_accessed=8 * count * patch * width
        ),
    )(*scalars, mine, up, modulation, other, *near)


def packed_body(head_inputs, hidden, out_weight, time_weight, head_weight, latent, timesteps):
    count = lax.axis_size("seq")
    halves = lax.axis_size("fsdp")
    rows = head_inputs.shape[2]
    place = lax.axis_index("seq")
    half = lax.axis_index("fsdp")
    group = lax.axis_index("grp")
    heads = HEADS // halves // count

    def along(block, r):
        return lax.ppermute(block, "seq", [(i, i ^ r) for i in range(count)])

    def swap(block, axis):
        return lax.ppermute(block, axis, [(0, 1), (1, 0)])

    def slanted(block, r):
        route = []
        for i in range(count):
            for j in range(halves):
                route.append((i * halves + j, (i ^ r) * halves + 1 - j))
        return lax.ppermute(block, ("seq", "fsdp"), route)

    x = head_inputs.reshape(rows, head_inputs.shape[3])
    head = jnp.swapaxes(head_weight[0], 0, 1)
    span = head.shape[0] // 2 * head_tiles(head.shape[1])
    here = place[None].astype(jnp.int32)
    side = half[None].astype(jnp.int32)
    level = group[None].astype(jnp.int32)
    scalars = (here, side, level)
    last = count // 2
    slots = [r for r in range(count - 1, 0, -1) if r != last] + [0]
    first, pack = split_first(x, head, scalars, last, count, halves)
    sent, clock = split_far(x, pack, timesteps.reshape(1, 2), scalars, slots, 1, count, halves)
    far_sent = [first if r == last else sent[slots.index(r)] for r in range(count)]
    far_pieces = [slanted(far_sent[r], r) for r in range(count)]

    other_steps = swap(timesteps, "fsdp")
    freqs = jnp.exp(
        -math.log(10000.0) * jnp.arange(FREQ // 2, dtype=jnp.float32) / (FREQ // 2)
    )
    angle = jnp.concatenate([clock[:1], jnp.full((1, LANES), other_steps[0, 0, 0], jnp.float32)])
    angle = angle * freqs
    embedding = jnp.concatenate([jnp.cos(angle), jnp.sin(angle)], axis=-1).astype(jnp.bfloat16)
    modulation = jnp.dot(embedding, time_weight[0], preferred_element_type=jnp.float32)

    near_sent = split_near(x, scalars, count, halves)
    near_pieces = [near_sent[0]] + [along(near_sent[r], r) for r in range(1, count)]

    weight = load_rows(out_weight[0], here, count)
    far_attended = attend_packed(far_pieces, heads, rows)
    far_home = [far_attended[0]]
    far_home += [along(far_attended[r], r) for r in range(1, count)]
    bounds = [0, DIM // 4, DIM]
    partial = []
    for k in range(2):
        term = project_packed(
            far_home,
            range(count),
            count,
            weight,
            rows,
            bounds[k],
            bounds[k + 1] - bounds[k],
            jnp.bfloat16,
        )
        partial.append(swap(term, "fsdp"))

    packed = near_sent[0].shape[0]
    relay = collect([far_pieces[2]], [(0, packed)], span)
    relayed = along(relay, 1)
    line = collect_line(
        [pack, far_pieces[1], far_pieces[2], relayed], [0, packed, packed, 0], span, modulation
    )
    other = swap(line, "fsdp")
    own_slots = [(0 if r == 0 else 1, r * span) for r in range(count)]
    far_slots = [(1 if r == 0 else 0, r * span) for r in range(count)]
    mine = collect([line, other], own_slots + far_slots, span)
    up = swap(mine, "grp")
    near_attended = attend_packed(near_pieces, heads, rows, (modulation, other))
    near_home = [near_attended[0]]
    near_home += [along(near_attended[r], r) for r in range(1, count)]
    done = near_home[0].shape[0] - 2 * MOD_ROWS
    head_rows, lines = arrange(mine, up, modulation, other, near_home, head, scalars, done)
    others = [r for r in range(count) if r != 1]
    most = project_packed(
        [near_home[r] for r in others], others, count, weight, rows, 0, DIM, jnp.float32
    )
    projected = project_packed(
        [near_home[1]], [1], count, weight, rows, 0, DIM, jnp.float32, (most,)
    )
    velocity, stepped = finish(
        projected,
        partial,
        hidden.reshape(rows, DIM),
        lines,
        head_rows,
        latent.reshape(rows // 2, 2 * PATCH),
        clock,
    )
    carried = partner(stepped, "section", 0)
    return (velocity.reshape(latent.shape), carried.reshape(latent.shape))


def packed_fits(mesh, head_shape):
    count, halves = mesh.shape["seq"], mesh.shape["fsdp"]
    rows = head_shape[2]
    return (
        head_shape[1] == 1
        and halves == 2
        and FREQ == 2 * LANES
        and 2 * PATCH == LANES
        and mesh.shape["grp"] == 2
        and count == 4
        and HEADS % (halves * count) == 0
        and 3 * DIM // (halves * count) <= 8 * LANES
        and DIM % (halves * count) == 0
        and HEADS // (halves * count) * HEAD % LANES == LANES // 2
        and rows % 32 == 0
        and rows * count <= 512
    )


def step(mesh, body):
    return jax.shard_map(
        body,
        mesh=mesh,
        in_specs=(
            P("section", ("grp", "fsdp"), "seq", None),
            P("section", ("grp", "fsdp"), "seq", None),
            P("section", "fsdp", None),
            P("section", None, ("seq", "fsdp")),
            P("section", ("seq", "fsdp"), None),
            P("section", ("grp", "fsdp"), "seq", None),
            P("section", ("grp", "fsdp"), None),
        ),
        out_specs=(
            P("section", ("grp", "fsdp"), "seq", None),
            P("section", ("grp", "fsdp"), "seq", None),
        ),
        check_vma=False,
    )


def solution(mesh):
    def choose(head_inputs, *rest):
        local = (
            head_inputs.shape[0] // mesh.shape["section"],
            head_inputs.shape[1] // mesh.shape["grp"] // mesh.shape["fsdp"],
            head_inputs.shape[2] // mesh.shape["seq"],
        )
        if not packed_fits(mesh, local):
            return step(mesh, general_body)(head_inputs, *rest)
        return step(mesh, packed_body)(head_inputs, *rest)

    return choose
```
